32 devices in a mesh: fsdp: 4 (over y, x), ctx: 4 (over z), tp: 2 (over core).
Axes of the slice: x: 2, y: 2, z: 4, core: 2. Of those that a mesh axis runs over, the one named last changes fastest.
Arguments:
- tokens: bfloat16 [8, 256, 768], P('fsdp', 'ctx'), may hold values from -6 to 6
- group_order: int32 [8], replicated, may hold values from 0 to 7, each once
- attn_gain: float32 [768], replicated, may hold values from 0.1 to 1.9
- attn_shift: float32 [768], replicated, may hold values from -3 to 3
- qkv_weight: bfloat16 [768, 2304], P(('fsdp', 'ctx'), 'tp'), as said below
- qkv_bias: float32 [2304], P('tp'), may hold values from -3 to 3
- dense_weight: bfloat16 [768, 768], P('tp', ('fsdp', 'ctx')), may hold values from -3 to 3
- dense_bias: float32 [768], replicated, may hold values from -3 to 3
- mlp_gain: float32 [768], replicated, may hold values from 0.1 to 1.9
- mlp_shift: float32 [768], replicated, may hold values from -3 to 3
- up_weight: bfloat16 [768, 3072], P(('fsdp', 'ctx'), 'tp'), may hold values from -0.21875 to 0.21875
- up_bias: float32 [3072], P('tp'), may hold values from -3 to 3
- down_weight: bfloat16 [3072, 768], P('tp', ('fsdp', 'ctx')), may hold values from -0.109375 to 0.109375
- down_bias: float32 [768], replicated, may hold values from -3 to 3
- out_grad: float32 [8, 256, 768], P('fsdp', 'ctx'), may hold values from -6 to 6
Outputs:
- block_out: bfloat16 [8, 256, 768], P('fsdp', 'ctx')
- tokens_grad: float32 [8, 256, 768], P('fsdp', 'ctx')
- attn_gain_grad: float32 [768], replicated
- attn_shift_grad: float32 [768], replicated
- qkv_weight_grad: float32 [768, 2304], P(('fsdp', 'ctx'), 'tp')
- qkv_bias_grad: float32 [2304], P('tp')
- dense_weight_grad: float32 [768, 768], P('tp', ('fsdp', 'ctx'))
- dense_bias_grad: float32 [768], replicated
- mlp_gain_grad: float32 [768], replicated
- mlp_shift_grad: float32 [768], replicated
- up_weight_grad: float32 [768, 3072], P(('fsdp', 'ctx'), 'tp')
- up_bias_grad: float32 [3072], P('tp')
- down_weight_grad: float32 [3072, 768], P('tp', ('fsdp', 'ctx'))
- down_bias_grad: float32 [768], replicated
The draws below stay inside these ranges and needn't reach their ends.
Inputs may be any that keep to these rules, and one draw needn't show every extreme that they name: Each block number appears once; slot s of every sequence holds positions group_order[s] * 32 to group_order[s] * 32 + 31. `qkv_weight`: columns ordered by head, then query, key and value, then the 64 dimensions of a head.
All inputs are finite; a program needn't handle non-finite values.
Results may differ from the reference program's by a relative error of at most 0.0099.
Values may be sent and summed in bfloat16 or wider, within the bound.
No kernel may reach another device: no remote copies, remote signals or barrier semaphores. Data moves between devices by JAX's collectives and lax.ppermute only.
A program may use at most 128 MiB of HBM per device.

```python
import math
import jax
import jax.numpy as jnp
from jax import lax

D = 768
H = 12
HD = 64
FF = 3072
ROT = 16
BLK = 32
SEQS = 8
SLOTS = 8
L = 256


def draw_qkv_weight(key, part):
    base_key = jax.random.fold_in(jax.random.fold_in(key, 17), 0)
    base = jax.random.normal(base_key, (D, H, 3, HD), jnp.float32) / math.sqrt(D)
    return base.reshape(D, 3 * D).astype(jnp.bfloat16)


def level_of(rng, shape, pieces, low, high):
    level, own = 1.0, jax.random.fold_in(rng, 6)
    for dim, shards_of in pieces:
        draws = jnp.exp(jax.random.uniform(jax.random.fold_in(own, dim), (shards_of,), jnp.float32, low / len(pieces), high / len(pieces)))
        level = level * jnp.repeat(draws, shape[dim] // shards_of).reshape([-1 if axis == dim else 1 for axis in range(len(shape))])
    return level


def bell_draw(key, shape, width, most, pieces=(), kind=jnp.bfloat16):
    level = level_of(key, shape, pieces, -0.22, 0.18) if pieces else 1.0
    values = jax.random.normal(key, shape, jnp.float32) * width * level
    return jnp.minimum(jnp.maximum(values, -most), most).astype(kind)


def setup_inputs(seed: int = 0) -> dict:
    streams_of = jax.random.split(jax.random.key(seed), 16)
    tokens = bell_draw(streams_of[0], (SEQS, L, D), 1.0, 6.0, ((0, 4), (1, 4)))
    group_order = jax.random.permutation(streams_of[1], SLOTS).astype(jnp.int32)
    attn_gain = jnp.clip(1.0 + 0.18 * jax.random.normal(streams_of[2], (D,), jnp.float32), 0.1, 1.9)
    attn_shift = bell_draw(streams_of[3], (D,), 0.5, 3.0, (), jnp.float32)
    qkv_weight = draw_qkv_weight(jax.random.fold_in(streams_of[15], 71), 0)
    qkv_bias = bell_draw(streams_of[5], (3 * D,), 0.5, 3.0, ((0, 2),), jnp.float32)
    dense_weight = bell_draw(streams_of[6], (D, D), 0.5, 3.0, ((0, 2), (1, 16)))
    dense_bias = bell_draw(streams_of[7], (D,), 0.5, 3.0, (), jnp.float32)
    mlp_gain = jnp.clip(1.0 + 0.18 * jax.random.normal(streams_of[8], (D,), jnp.float32), 0.1, 1.9)
    mlp_shift = bell_draw(streams_of[9], (D,), 0.5, 3.0, (), jnp.float32)
    up_weight = bell_draw(streams_of[10], (D, FF), D ** -0.5, 0.21875, ((0, 16), (1, 2)))
    up_bias = bell_draw(streams_of[11], (FF,), 0.5, 3.0, ((0, 2),), jnp.float32)
    down_weight = bell_draw(streams_of[12], (FF, D), FF ** -0.5, 0.109375, ((0, 2), (1, 16)))
    down_bias = bell_draw(streams_of[13], (D,), 0.5, 3.0, (), jnp.float32)
    out_grad = bell_draw(streams_of[14], (SEQS, L, D), 1.0, 6.0, ((0, 4), (1, 4)), jnp.float32)
    return dict(tokens=tokens, group_order=group_order, attn_gain=attn_gain, attn_shift=attn_shift, qkv_weight=qkv_weight, qkv_bias=qkv_bias, dense_weight=dense_weight, dense_bias=dense_bias, mlp_gain=mlp_gain, mlp_shift=mlp_shift, up_weight=up_weight, up_bias=up_bias, down_weight=down_weight, down_bias=down_bias, out_grad=out_grad)


EPSILON = 1e-05
NEGATIVE = -1e+30
HIGHEST = lax.Precision.HIGHEST
ROOT_HALF = 0.7071067811865476
INV_ROOT_TWO_PI = 0.3989422804014327

def layer_norm(values, gain, shift):
    middle = lax.optimization_barrier(jnp.mean(values, axis=-1, keepdims=True))
    centred = values - middle
    inverse = lax.rsqrt(lax.optimization_barrier(jnp.mean(centred * centred, axis=-1, keepdims=True)) + EPSILON)
    normed = centred * inverse
    return (normed * gain + shift, normed, inverse)

def norm_back(grad, normed, inverse, gain):
    scaled = grad * gain
    inner = scaled - lax.optimization_barrier(jnp.mean(scaled, axis=-1, keepdims=True)) - normed * lax.optimization_barrier(jnp.mean(scaled * normed, axis=-1, keepdims=True))
    return (inverse * inner, lax.optimization_barrier(jnp.sum(grad * normed, axis=0)), lax.optimization_barrier(jnp.sum(grad, axis=0)))

def gelu_value(values):
    return 0.5 * values * (1.0 + lax.erf(values * ROOT_HALF))

def gelu_slope(values):
    return 0.5 * (1.0 + lax.erf(values * ROOT_HALF)) + values * jnp.exp(-0.5 * values * values) * INV_ROOT_TWO_PI

def angle_tables(position):
    half = ROT // 2
    frequency = 1.0 / 10000.0 ** (jnp.arange(half, dtype=jnp.float32) * (2.0 / ROT))
    phase = position.astype(jnp.float32)[:, None] * frequency[None, :]
    return (jnp.cos(phase), jnp.sin(phase))

def rotate(values, cosine, sine):
    half = ROT // 2
    first = values[..., :half]
    second = values[..., half:ROT]
    rest = values[..., ROT:]
    return jnp.concatenate([first * cosine - second * sine, second * cosine + first * sine, rest], axis=-1)

def reference(tokens, group_order, attn_gain, attn_shift, qkv_weight, qkv_bias, dense_weight, dense_bias, mlp_gain, mlp_shift, up_weight, up_bias, down_weight, down_bias, out_grad):
    scale = 1.0 / math.sqrt(HD)
    index = jnp.arange(L, dtype=jnp.int32)
    position = group_order[index // BLK].astype(jnp.int32) * BLK + index % BLK
    cosine, sine = angle_tables(position)
    cosine = cosine[:, None, :]
    sine = sine[:, None, :]
    qblock = min(512, L)
    blocks = L // qblock
    pos_blocks = position.reshape(blocks, qblock)

    def one_sequence(carry, item):
        token_rows, grad_rows = item
        inputs = token_rows.astype(jnp.float32)
        attn_full, attn_centred, attn_inverse = layer_norm(inputs, attn_gain, attn_shift)
        mlp_full, mlp_centred, mlp_inverse = layer_norm(inputs, mlp_gain, mlp_shift)
        attn_in = attn_full.astype(jnp.bfloat16)
        mlp_in = mlp_full.astype(jnp.bfloat16)
        projected = (jnp.dot(attn_in, qkv_weight, preferred_element_type=jnp.float32) + qkv_bias).reshape(L, H, 3, HD)
        queries = rotate(projected[:, :, 0], cosine, sine).astype(jnp.bfloat16)
        keys = rotate(projected[:, :, 1], cosine, sine).astype(jnp.bfloat16)
        values = projected[:, :, 2].astype(jnp.bfloat16)
        keys_wide = keys.astype(jnp.float32)
        values_wide = values.astype(jnp.float32)
        pre_act = jnp.dot(mlp_in, up_weight, preferred_element_type=jnp.float32) + up_bias
        hidden = gelu_value(pre_act).astype(jnp.bfloat16)
        query_blocks = queries.reshape(blocks, qblock, H, HD)

        def forward_block(args):
            query_part, query_pos = args
            raw = jnp.einsum('qhd,khd->hqk', query_part.astype(jnp.float32), keys_wide, precision=HIGHEST) * scale
            allowed = position[None, :] <= query_pos[:, None]
            raw = jnp.where(allowed[None], raw, NEGATIVE)
            peak = lax.optimization_barrier(jnp.max(raw, axis=-1))
            weights = jnp.where(allowed[None], jnp.exp(raw - peak[..., None]), 0.0)
            total = lax.optimization_barrier(jnp.sum(weights, axis=-1))
            probs = weights / total[..., None]
            attended = jnp.einsum('hqk,khd->qhd', probs, values_wide, precision=HIGHEST)
            return (attended, peak + jnp.log(total))
        attended, log_total = lax.map(forward_block, (query_blocks, pos_blocks))
        attended_rows = attended.reshape(L, H, HD)
        context = attended_rows.reshape(L, D).astype(jnp.bfloat16)
        branches = jnp.dot(context, dense_weight, preferred_element_type=jnp.float32) + jnp.dot(hidden, down_weight, preferred_element_type=jnp.float32)
        block_out = (inputs + branches + dense_bias + down_bias).astype(jnp.bfloat16)
        grad_low = grad_rows.astype(jnp.bfloat16)
        dense_weight_grad = jnp.dot(context.T, grad_low, preferred_element_type=jnp.float32)
        down_weight_grad = jnp.dot(hidden.T, grad_low, preferred_element_type=jnp.float32)
        bias_grad = lax.optimization_barrier(jnp.sum(grad_rows, axis=0))
        ctx_low = jnp.dot(grad_low, dense_weight.T, preferred_element_type=jnp.float32).astype(jnp.bfloat16)
        pre_grad = jnp.dot(grad_low, down_weight.T, preferred_element_type=jnp.float32) * gelu_slope(pre_act)
        up_bias_grad = lax.optimization_barrier(jnp.sum(pre_grad, axis=0))
        pre_low = pre_grad.astype(jnp.bfloat16)
        up_weight_grad = jnp.dot(mlp_in.T, pre_low, preferred_element_type=jnp.float32)
        ctx_heads = ctx_low.reshape(L, H, HD).astype(jnp.float32)
        delta = lax.optimization_barrier(jnp.sum(ctx_heads * attended_rows, axis=-1))

        def backward_block(acc, args):
            query_part, query_pos, log_part, delta_part, grad_part = args
            raw = jnp.einsum('qhd,khd->hqk', query_part.astype(jnp.float32), keys_wide, precision=HIGHEST) * scale
            allowed = position[None, :] <= query_pos[:, None]
            raw = jnp.where(allowed[None], raw, NEGATIVE)
            probs = jnp.where(allowed[None], jnp.exp(raw - log_part[..., None]), 0.0)
            weight_grad = jnp.einsum('qhd,khd->hqk', grad_part, values_wide, precision=HIGHEST)
            score_grad = probs * (weight_grad - delta_part.T[..., None])
            query_grad = scale * jnp.einsum('hqk,khd->qhd', score_grad, keys_wide, precision=HIGHEST)
            key_grad = acc[0] + scale * jnp.einsum('hqk,qhd->khd', score_grad, query_part.astype(jnp.float32), precision=HIGHEST)
            value_grad = acc[1] + jnp.einsum('hqk,qhd->khd', probs, grad_part, precision=HIGHEST)
            return ((key_grad, value_grad), query_grad)
        zero_heads = jnp.zeros((L, H, HD), jnp.float32)
        (key_grad, value_grad), query_grad = lax.scan(backward_block, (zero_heads, zero_heads), (query_blocks, pos_blocks, log_total, delta.reshape(blocks, qblock, H), ctx_heads.reshape(blocks, qblock, H, HD)))
        query_grad = rotate(query_grad.reshape(L, H, HD), cosine, -sine)
        key_grad = rotate(key_grad, cosine, -sine)
        proj_grad = jnp.stack([query_grad, key_grad, value_grad], axis=2).reshape(L, 3 * D)
        qkv_bias_grad = lax.optimization_barrier(jnp.sum(proj_grad, axis=0))
        proj_low = proj_grad.astype(jnp.bfloat16)
        qkv_weight_grad = jnp.dot(attn_in.T, proj_low, preferred_element_type=jnp.float32)
        attn_norm_grad = jnp.dot(proj_low, qkv_weight.T, preferred_element_type=jnp.float32)
        mlp_norm_grad = jnp.dot(pre_low, up_weight.T, preferred_element_type=jnp.float32)
        attn_back, attn_gain_grad, attn_shift_grad = norm_back(attn_norm_grad, attn_centred, attn_inverse, attn_gain)
        mlp_back, mlp_gain_grad, mlp_shift_grad = norm_back(mlp_norm_grad, mlp_centred, mlp_inverse, mlp_gain)
        tokens_grad = grad_rows + attn_back + mlp_back
        terms = (attn_gain_grad, attn_shift_grad, qkv_weight_grad, qkv_bias_grad, dense_weight_grad, bias_grad, mlp_gain_grad, mlp_shift_grad, up_weight_grad, up_bias_grad, down_weight_grad)
        carry = tuple((old + new for old, new in zip(carry, terms)))
        return (carry, (block_out, tokens_grad))
    start = (jnp.zeros((D,), jnp.float32), jnp.zeros((D,), jnp.float32), jnp.zeros((D, 3 * D), jnp.float32), jnp.zeros((3 * D,), jnp.float32), jnp.zeros((D, D), jnp.float32), jnp.zeros((D,), jnp.float32), jnp.zeros((D,), jnp.float32), jnp.zeros((D,), jnp.float32), jnp.zeros((D, FF), jnp.float32), jnp.zeros((FF,), jnp.float32), jnp.zeros((FF, D), jnp.float32))
    grads, (block_out, tokens_grad) = lax.scan(one_sequence, start, (tokens, out_grad))
    return (block_out, tokens_grad, grads[0], grads[1], grads[2], grads[3], grads[4], grads[5], grads[6], grads[7], grads[8], grads[9], grads[10], grads[5])
```

```python
import math

import jax
import jax.numpy as jnp
from jax import lax
from jax.sharding import PartitionSpec as P

HD = 64
ROT = 16
BLK = 32


EPSILON = 1e-05
NEGATIVE = -1e30
ROOT_HALF = 0.7071067811865476
INV_ROOT_TWO_PI = 0.3989422804014327
CONTRACT_LAST = (((1,), (1,)), ((), ()))
CONTRACT_FIRST = (((0,), (0,)), ((), ()))


def gelu_value(values):
    return 0.5 * values * (1.0 + lax.erf(values * ROOT_HALF))


def gelu_slope(values):
    return (
        0.5 * (1.0 + lax.erf(values * ROOT_HALF))
        + values * jnp.exp(-0.5 * values * values) * INV_ROOT_TWO_PI
    )


def angle_tables(position):
    half = ROT // 2
    frequency = 1.0 / 10000.0 ** (jnp.arange(half, dtype=jnp.float32) * (2.0 / ROT))
    phase = position.astype(jnp.float32)[:, None] * frequency[None, :]
    return (jnp.cos(phase), jnp.sin(phase))


def positions(order, start, count):
    index = start + jnp.arange(count, dtype=jnp.int32)
    slot = index // BLK
    table = jnp.arange(order.shape[0], dtype=jnp.int32)
    first = jnp.sum(jnp.where(slot[:, None] == table[None, :], order[None, :], 0), axis=1)
    return first * BLK + index % BLK


def swapped(parts, index):
    bit = 1
    while bit < len(parts):
        is_set = (index & bit) != 0
        parts = [jnp.where(is_set, parts[j ^ bit], parts[j]) for j in range(len(parts))]
        bit *= 2
    return parts


def exchange(parts, axis):
    count = lax.axis_size(axis)
    return [parts[0]] + [
        lax.ppermute(parts[k], axis, [(i, i ^ k) for i in range(count)]) for k in range(1, count)
    ]


def spread(value, axis):
    return exchange([value] * lax.axis_size(axis), axis)


def butterfly(value, axis):
    count = lax.axis_size(axis)
    bit = 1
    while bit < count:
        value = value + lax.ppermute(value, axis, [(i, i ^ bit) for i in range(count)])
        bit *= 2
    return value


def one_hot_slots(value, index, count):
    slots = jnp.arange(count, dtype=jnp.int32)[:, None] == index
    return jnp.where(slots, value[None, :], 0.0).reshape(-1)


def dot(left, right):
    return jnp.dot(left, right, preferred_element_type=jnp.float32)


def dot_last(left, right):
    return lax.dot_general(left, right, CONTRACT_LAST, preferred_element_type=jnp.float32)


def dot_first(left, right):
    return lax.dot_general(left, right, CONTRACT_FIRST, preferred_element_type=jnp.float32)


def normed_rows(rows):
    middle = jnp.mean(rows, axis=-1, keepdims=True)
    centred = rows - middle
    inverse = lax.rsqrt(jnp.mean(centred * centred, axis=-1, keepdims=True) + EPSILON)
    return centred * inverse, inverse


def rotary_tables(position, heads):
    half = ROT // 2
    cosine, sine = angle_tables(position)
    rest = jnp.ones((position.shape[0], HD - ROT), jnp.float32)
    none = jnp.zeros((position.shape[0], HD - ROT), jnp.float32)
    cos_head = jnp.concatenate([cosine, cosine, rest], axis=1)
    sin_head = jnp.concatenate([-sine, sine, none], axis=1)
    return cos_head[:, None, None, :], sin_head[:, None, None, :]


def turn(values, cos_head, sin_head):
    half = ROT // 2
    partner = jnp.concatenate(
        [values[..., half:ROT], values[..., :half], values[..., ROT:]], axis=-1
    )
    return values * cos_head + partner * sin_head


def on_device(
    tokens,
    group_order,
    attn_gain,
    attn_shift,
    qkv_weight,
    qkv_bias,
    dense_weight,
    dense_bias,
    mlp_gain,
    mlp_shift,
    up_weight,
    up_bias,
    down_weight,
    down_bias,
    out_grad,
):
    bf16 = jnp.bfloat16
    seqs, length, width = tokens.shape
    fsdp_count, ctx_count, tp_count = (lax.axis_size(a) for a in ("fsdp", "ctx", "tp"))
    fsdp_at, ctx_at, tp_at = (lax.axis_index(a) for a in ("fsdp", "ctx", "tp"))
    rows_here = qkv_weight.shape[0]
    heads = qkv_bias.shape[0] // (3 * HD)
    hidden_all = up_bias.shape[0]
    head_groups = math.gcd(heads, ctx_count)
    own_heads = heads // head_groups
    ranks = ctx_count // head_groups
    copies = ranks // seqs
    features = own_heads * HD
    qkv_cols = 3 * features
    ff = hidden_all // ctx_count
    scale = 1.0 / math.sqrt(HD)
    head_at = ctx_at % head_groups
    seq_at = (ctx_at // head_groups) % seqs
    near = seqs // tp_count

    down_t = down_weight.T
    dense_t = dense_weight.T

    def for_rank(rank):
        group = rank % head_groups
        return (
            [
                qkv_weight[:, group * qkv_cols : (group + 1) * qkv_cols],
                dense_t[:, group * features : (group + 1) * features],
            ],
            [
                up_weight[:, rank * ff : (rank + 1) * ff],
                down_t[:, rank * ff : (rank + 1) * ff],
            ],
        )

    by_rank = [for_rank(rank) for rank in range(ctx_count)]
    early = swapped([jnp.concatenate(pair[0], axis=1) for pair in by_rank], ctx_at)
    late = swapped([jnp.concatenate(pair[1], axis=1) for pair in by_rank], ctx_at)

    def gather_weights(parts):
        rows = jnp.concatenate(swapped(exchange(parts, "ctx"), ctx_at), axis=0)
        return jnp.concatenate(swapped(spread(rows, "fsdp"), fsdp_at), axis=0)

    early_weight = gather_weights(early)
    qkv_piece = early_weight[:, :qkv_cols]
    dense_piece = early_weight[:, qkv_cols:]
    late_weight = gather_weights(late)
    up_piece = late_weight[:, :ff]
    down_piece = late_weight[:, ff:]

    def near_part(array):
        parts = [array[j * near : (j + 1) * near] for j in range(tp_count)]
        return swapped(parts, tp_at)[0]

    own_tokens = near_part(tokens)
    own_grads = near_part(out_grad)
    message = jnp.stack([own_tokens, own_grads.astype(bf16)])
    chunks = jnp.stack(spread(message, "ctx"), axis=2)
    both = jnp.stack(spread(chunks, "tp"), axis=1)
    size = ctx_count * length
    all_rows = seqs * size
    by_seq = both.reshape(2, tp_count, near * size, width)
    token_rows = both[0].reshape(all_rows, width)
    grad_rows = both[1].reshape(all_rows, width)
    seq_parts = [
        both[:, j, i].reshape(2, size, width) for j in range(tp_count) for i in range(near)
    ]
    seq_core = (seq_at // near) ^ tp_at
    seq_slot = seq_core * near + seq_at % near
    mine = seq_parts[0]
    for slot in range(1, seqs):
        mine = jnp.where(seq_slot == slot, seq_parts[slot], mine)
    seq_tokens, seq_grads = mine[0], mine[1]

    position = jnp.concatenate(
        [positions(group_order, (ctx_at ^ k) * length, length) for k in range(ctx_count)]
    )
    cos_head, sin_head = rotary_tables(position, own_heads)
    seq_centred, _ = normed_rows(seq_tokens.astype(jnp.float32))
    attn_in = (seq_centred * attn_gain + attn_shift).astype(bf16)
    bias_parts = [qkv_bias[g * qkv_cols : (g + 1) * qkv_cols] for g in range(head_groups)]
    projected = dot(attn_in, qkv_piece) + swapped(bias_parts, head_at)[0]
    projected = projected.reshape(size, own_heads, 3, HD)
    turned = turn(projected[:, :, :2], cos_head, sin_head).astype(bf16)
    queries = turned[:, :, 0]
    keys = turned[:, :, 1]
    values = projected[:, :, 2].astype(bf16)
    allowed = (position[None, :] <= position[:, None])[None]
    scores = jnp.where(
        allowed,
        jnp.einsum("qhd,khd->hqk", queries, keys, preferred_element_type=jnp.float32) * scale,
        NEGATIVE,
    )
    peak = jnp.max(scores, axis=-1, keepdims=True)
    weights = jnp.where(allowed, jnp.exp(scores - peak), 0.0)
    probs = weights / jnp.sum(weights, axis=-1, keepdims=True)
    probs_low = probs.astype(bf16)
    attended = jnp.einsum("hqk,khd->qhd", probs_low, values, preferred_element_type=jnp.float32)
    context = attended.reshape(size, features).astype(bf16)
    ctx_low = dot(seq_grads, dense_piece).astype(bf16).reshape(size, own_heads, HD)
    delta = jnp.sum(ctx_low.astype(jnp.float32) * attended, axis=-1)
    weight_grad = jnp.einsum("qhd,khd->hqk", ctx_low, values, preferred_element_type=jnp.float32)
    score_grad = probs * (weight_grad - jnp.transpose(delta)[..., None])
    if copies > 1:
        first_copy = (ctx_at // (head_groups * seqs)) == 0
        score_grad = jnp.where(first_copy, score_grad, 0.0)
        probs_low = jnp.where(first_copy, probs_low, 0.0)
        context = jnp.where(first_copy, context, 0.0)
    grad_scores = score_grad.astype(bf16)
    value_grad = jnp.einsum("hqk,qhd->khd", probs_low, ctx_low, preferred_element_type=jnp.float32)
    query_grad = scale * jnp.einsum(
        "hqk,khd->qhd", grad_scores, keys, preferred_element_type=jnp.float32
    )
    key_grad = scale * jnp.einsum(
        "hqk,qhd->khd", grad_scores, queries, preferred_element_type=jnp.float32
    )
    back = turn(jnp.stack([query_grad, key_grad], axis=2), cos_head, -sin_head)
    proj_grad = jnp.concatenate([back, value_grad[:, :, None]], axis=2).reshape(size, qkv_cols)
    qkv_bias_part = jnp.sum(proj_grad, axis=0)
    proj_low = proj_grad.astype(bf16)

    all_centred, _ = normed_rows(token_rows.astype(jnp.float32))
    mlp_in = (all_centred * mlp_gain + mlp_shift).astype(bf16)
    up_parts = [up_bias[r * ff : (r + 1) * ff] for r in range(ctx_count)]
    pre_act = dot(mlp_in, up_piece) + swapped(up_parts, ctx_at)[0]
    hidden = gelu_value(pre_act).astype(bf16)
    pre_grad = dot(grad_rows, down_piece) * gelu_slope(pre_act)
    pre_low = pre_grad.astype(bf16)
    up_bias_part = jnp.sum(pre_grad, axis=0)

    def scatter_rows(mlp_part, attn_part):
        total = mlp_part.reshape(tp_count, near, size, width)
        slots = jnp.arange(seqs, dtype=jnp.int32).reshape(tp_count, near, 1, 1)
        total = total + jnp.where(slots == seq_slot, attn_part, 0.0)
        halves = exchange([total[j] for j in range(tp_count)], "tp")
        half = sum(halves).reshape(near, ctx_count, length, width)
        sent = [half[:, k].astype(bf16) if k else half[:, 0] for k in range(ctx_count)]
        return sum(part.astype(jnp.float32) for part in exchange(sent, "ctx"))

    def both_cores(half):
        return jnp.concatenate(swapped(spread(half, "tp"), tp_at), axis=0)

    branches = scatter_rows(dot_last(hidden, down_piece), dot_last(context, dense_piece))
    block_half = own_tokens.astype(jnp.float32) + branches + (dense_bias + down_bias)
    block_out = both_cores(block_half.astype(bf16))

    mlp_norm_grad = dot_last(pre_low, up_piece)
    attn_norm_grad = dot_last(proj_low, qkv_piece)
    inner = scatter_rows(mlp_norm_grad * mlp_gain, attn_norm_grad * attn_gain)
    own_centred, own_inverse = normed_rows(own_tokens.astype(jnp.float32))
    inner = (
        inner
        - jnp.mean(inner, axis=-1, keepdims=True)
        - own_centred * jnp.mean(inner * own_centred, axis=-1, keepdims=True)
    )
    tokens_grad = both_cores(own_grads + own_inverse * inner)

    def scatter_weights(early_part, late_part):
        block = ctx_count * rows_here

        def over_fsdp(part):
            blocks = [part[j * block : (j + 1) * block] for j in range(fsdp_count)]
            sent = [
                piece.astype(bf16) if k else piece
                for k, piece in enumerate(swapped(blocks, fsdp_at))
            ]
            total = sum(piece.astype(jnp.float32) for piece in exchange(sent, "fsdp"))
            pieces = [total[j * rows_here : (j + 1) * rows_here] for j in range(ctx_count)]
            sent = [
                piece.astype(bf16) if k else piece
                for k, piece in enumerate(swapped(pieces, ctx_at))
            ]
            return [piece.astype(jnp.float32) for piece in exchange(sent, "ctx")]

        late_pieces = swapped(over_fsdp(late_part), ctx_at)
        up_grad = jnp.concatenate([piece[:, :ff] for piece in late_pieces], axis=1)
        down_grad = jnp.concatenate([piece[:, ff:] for piece in late_pieces], axis=1).T
        early_pieces = over_fsdp(early_part)
        groups = [sum(early_pieces[g::head_groups]) for g in range(head_groups)]
        groups = swapped(groups, head_at)
        qkv_grad = jnp.concatenate([group[:, :qkv_cols] for group in groups], axis=1)
        dense_grad = jnp.concatenate([group[:, qkv_cols:] for group in groups], axis=1).T
        return qkv_grad, dense_grad, up_grad, down_grad

    early_part = jnp.concatenate(
        [dot_first(attn_in, proj_low), dot_first(seq_grads, context)], axis=1
    )
    late_part = jnp.concatenate([dot_first(mlp_in, pre_low), dot_first(grad_rows, hidden)], axis=1)
    qkv_weight_grad, dense_weight_grad, up_weight_grad, down_weight_grad = scatter_weights(
        early_part, late_part
    )

    norm_parts = jnp.concatenate(
        [
            jnp.sum(attn_norm_grad * seq_centred, axis=0),
            jnp.sum(attn_norm_grad, axis=0),
            jnp.sum(mlp_norm_grad * all_centred, axis=0),
            jnp.sum(mlp_norm_grad, axis=0),
        ]
    )
    bias_parts = jnp.concatenate(
        [
            jnp.sum(out_grad, axis=(0, 1)),
            one_hot_slots(qkv_bias_part, head_at, head_groups),
            one_hot_slots(up_bias_part, ctx_at, ctx_count),
        ]
    )
    small = jnp.concatenate([butterfly(norm_parts, "tp"), bias_parts])
    small = butterfly(butterfly(small, "fsdp"), "ctx")
    ends = [width] * 5 + [3 * HD * heads, hidden_all]
    cuts = []
    start = 0
    for extent in ends:
        cuts.append(small[start : start + extent])
        start += extent
    return (
        block_out,
        tokens_grad,
        cuts[0],
        cuts[1],
        qkv_weight_grad,
        cuts[5],
        dense_weight_grad,
        cuts[4],
        cuts[2],
        cuts[3],
        up_weight_grad,
        cuts[6],
        down_weight_grad,
        cuts[4],
    )


def solution(mesh):
    in_specs = (
        P("fsdp", "ctx", None),
        P(),
        P(),
        P(),
        P(("fsdp", "ctx"), "tp"),
        P("tp"),
        P("tp", ("fsdp", "ctx")),
        P(),
        P(),
        P(),
        P(("fsdp", "ctx"), "tp"),
        P("tp"),
        P("tp", ("fsdp", "ctx")),
        P(),
        P("fsdp", "ctx", None),
    )
    out_specs = (
        P("fsdp", "ctx", None),
        P("fsdp", "ctx", None),
        P(),
        P(),
        P(("fsdp", "ctx"), "tp"),
        P("tp"),
        P("tp", ("fsdp", "ctx")),
        P(),
        P(),
        P(),
        P(("fsdp", "ctx"), "tp"),
        P("tp"),
        P("tp", ("fsdp", "ctx")),
        P(),
    )
    return jax.shard_map(
        on_device, mesh=mesh, in_specs=in_specs, out_specs=out_specs, check_vma=False
    )
```

```python
import functools
import math

import jax
import jax.numpy as jnp
from jax import lax
from jax.experimental import pallas as pl
from jax.experimental.pallas import tpu as pltpu
from jax.sharding import PartitionSpec as P

HD = 64
ROT = 16
BLK = 32


EPSILON = 1e-05
NEGATIVE = -1e30
ROOT_HALF = 0.7071067811865476
INV_ROOT_TWO_PI = 0.3989422804014327
CONTRACT_LAST = (((1,), (1,)), ((), ()))
CONTRACT_FIRST = (((0,), (0,)), ((), ()))


def angle_tables(position):
    half = ROT // 2
    frequency = 1.0 / 10000.0 ** (jnp.arange(half, dtype=jnp.float32) * (2.0 / ROT))
    phase = position.astype(jnp.float32)[:, None] * frequency[None, :]
    return (jnp.cos(phase), jnp.sin(phase))


def positions(order, start, count):
    index = start + jnp.arange(count, dtype=jnp.int32)
    slot = index // BLK
    table = jnp.arange(order.shape[0], dtype=jnp.int32)
    first = jnp.sum(jnp.where(slot[:, None] == table[None, :], order[None, :], 0), axis=1)
    return first * BLK + index % BLK


def swapped(parts, index):
    bit = 1
    while bit < len(parts):
        is_set = (index & bit) != 0
        parts = [jnp.where(is_set, parts[j ^ bit], parts[j]) for j in range(len(parts))]
        bit *= 2
    return parts


def exchange(parts, axis):
    count = lax.axis_size(axis)
    return [parts[0]] + [
        lax.ppermute(parts[k], axis, [(i, i ^ k) for i in range(count)]) for k in range(1, count)
    ]


def spread(value, axis):
    return exchange([value] * lax.axis_size(axis), axis)


def butterfly(value, axis):
    count = lax.axis_size(axis)
    bit = 1
    while bit < count:
        value = value + lax.ppermute(value, axis, [(i, i ^ bit) for i in range(count)])
        bit *= 2
    return value


def one_hot_slots(value, index, count):
    slots = jnp.arange(count, dtype=jnp.int32)[:, None] == index
    return jnp.where(slots, value[None, :], 0.0).reshape(-1)


def dot(left, right):
    return jnp.dot(left, right, preferred_element_type=jnp.float32)


def dot_last(left, right):
    return lax.dot_general(left, right, CONTRACT_LAST, preferred_element_type=jnp.float32)


def dot_first(left, right):
    return lax.dot_general(left, right, CONTRACT_FIRST, preferred_element_type=jnp.float32)


def normed_rows(rows):
    middle = jnp.mean(rows, axis=-1, keepdims=True)
    centred = rows - middle
    inverse = lax.rsqrt(jnp.mean(centred * centred, axis=-1, keepdims=True) + EPSILON)
    return centred * inverse, inverse


VMEM_LIMIT = 60 * 1024 * 1024
LANES = 128


def local_kernel(body, out_shapes, scratch=(), flops=0, moved=0):
    in_vmem = pl.BlockSpec(memory_space=pltpu.VMEM)
    return pl.pallas_call(
        body,
        out_shape=out_shapes,
        out_specs=jax.tree.map(lambda _: in_vmem, out_shapes),
        scratch_shapes=list(scratch),
        compiler_params=pltpu.CompilerParams(vmem_limit_bytes=VMEM_LIMIT),
        cost_estimate=pl.CostEstimate(flops=flops, bytes_accessed=moved, transcendentals=0),
    )


def shaped(shape, kind):
    return jax.ShapeDtypeStruct(tuple(shape), kind)


def rotary_tables(position):
    cosine, sine = angle_tables(position)
    rest = jnp.ones((position.shape[0], HD - ROT), jnp.float32)
    none = jnp.zeros((position.shape[0], HD - ROT), jnp.float32)
    cos_head = jnp.concatenate([cosine, cosine, rest], axis=1)
    sin_head = jnp.concatenate([-sine, sine, none], axis=1)
    return jnp.concatenate([cos_head] * 2, axis=1), jnp.concatenate([sin_head] * 2, axis=1)


def early_message_kernel(groups, qkv_cols, features, qkv_ref, dense_ref, *outs):
    at = lax.rem(lax.axis_index("ctx"), groups)
    dense_t = dense_ref[...].astype(jnp.float32).T.astype(jnp.bfloat16)
    parts = [
        jnp.concatenate(
            [
                qkv_ref[:, g * qkv_cols : (g + 1) * qkv_cols],
                dense_t[:, g * features : (g + 1) * features],
            ],
            axis=1,
        )
        for g in range(groups)
    ]
    for out, part in zip(outs, swapped(parts, at)):
        out[...] = part


def late_message_kernel(count, ff, padded, up_ref, down_ref, *outs):
    at = lax.axis_index("ctx")
    down_t = down_ref[...].astype(jnp.float32).T.astype(jnp.bfloat16)
    rows = up_ref.shape[0]
    gap = [jnp.zeros((rows, padded - ff), jnp.bfloat16)] if padded > ff else []
    parts = [
        jnp.concatenate(
            [up_ref[:, r * ff : (r + 1) * ff]] + gap + [down_t[:, r * ff : (r + 1) * ff]] + gap,
            axis=1,
        )
        for r in range(count)
    ]
    for out, part in zip(outs, swapped(parts, at)):
        out[...] = part


def place_weight(parts, weight):
    at = lax.axis_index("fsdp")
    block = parts[0].shape[0]
    for k, part in enumerate(parts):
        start = pl.multiple_of((at ^ k) * block, 16)
        weight[pl.ds(start, block), :] = part[...]


def send_blocks(total, outs):
    at = lax.axis_index("fsdp")
    block = outs[0].shape[0]
    for k, out in enumerate(outs):
        start = pl.multiple_of((at ^ k) * block, 16)
        out[...] = total[pl.ds(start, block), :].astype(out.dtype)


def attention_kernel(
    fsdp_count,
    core_count,
    near,
    head_groups,
    own_heads,
    copies,
    seqs,
    *refs,
):
    row_refs = refs[:core_count]
    parts = refs[core_count : core_count + fsdp_count]
    (gain, shift, bias, cos_ref, sin_ref, pos_col, pos_row) = refs[
        core_count + fsdp_count : core_count + fsdp_count + 7
    ]
    outs = refs[core_count + fsdp_count + 7 :]
    branch, norm_out, sums = outs[:3]
    grad_outs = outs[3 : 3 + fsdp_count]
    weight, grads, mixed, total = outs[3 + fsdp_count :]
    size = pos_col.shape[0]
    cols = weight.shape[1]
    features = own_heads * HD
    qkv_cols = 3 * features
    scale = 1.0 / math.sqrt(HD)
    ctx_at = lax.axis_index("ctx")
    seq_at = lax.rem(lax.div(ctx_at, head_groups), seqs)
    core = lax.div(seq_at, near) ^ lax.axis_index("tp")
    inner = lax.rem(seq_at, near)
    place_weight(parts, weight)
    seq_tokens, seq_grads = row_refs[0][0, inner], row_refs[0][1, inner]
    for j in range(1, core_count):
        seq_tokens = jnp.where(core == j, row_refs[j][0, inner], seq_tokens)
        seq_grads = jnp.where(core == j, row_refs[j][1, inner], seq_grads)
    centred, _ = normed_rows(seq_tokens.astype(jnp.float32))
    attn_in = (centred * gain[...] + shift[...]).astype(jnp.bfloat16)
    lane = lax.broadcasted_iota(jnp.int32, (1, cols), 1)
    rotated = (lane < qkv_cols) & (lane % (3 * HD) < 2 * HD)
    first = lane % HD < ROT // 2
    repeat = cols // LANES
    cos_all = jnp.where(rotated, jnp.concatenate([cos_ref[...]] * repeat, axis=1), 1.0)
    sin_all = jnp.where(rotated, jnp.concatenate([sin_ref[...]] * repeat, axis=1), 0.0)

    def turn(values, sine):
        ahead = pltpu.roll(values, cols - ROT // 2, 1)
        behind = pltpu.roll(values, ROT // 2, 1)
        return values * cos_all + jnp.where(first, ahead, behind) * sine

    projected = dot(attn_in, weight[...]) + bias[...]
    turned = turn(projected, sin_all).astype(jnp.bfloat16)
    ctx_low = dot(seq_grads, weight[:, qkv_cols:]).astype(jnp.bfloat16)
    allowed = pos_row[...] <= pos_col[...]
    keep = None
    if copies > 1:
        keep = lax.div(ctx_at, head_groups * seqs) == 0
    grads[...] = jnp.zeros(grads.shape, jnp.float32)
    mixed[...] = jnp.zeros(mixed.shape, jnp.bfloat16)
    for head in range(own_heads):
        at = head * 3 * HD
        query = turned[:, at : at + HD]
        key = turned[:, at + HD : at + 2 * HD]
        value = turned[:, at + 2 * HD : at + 3 * HD]
        low = ctx_low[:, head * HD : (head + 1) * HD]
        scores = jnp.where(allowed, dot_last(query, key) * scale, NEGATIVE)
        peak = jnp.max(scores, axis=-1, keepdims=True)
        weights = jnp.where(allowed, jnp.exp(scores - peak), 0.0)
        probs = weights / jnp.sum(weights, axis=-1, keepdims=True)
        probs_low = probs.astype(jnp.bfloat16)
        attended = dot(probs_low, value)
        delta = jnp.sum(low.astype(jnp.float32) * attended, axis=-1, keepdims=True)
        score_grad = probs * (dot_last(low, value) - delta)
        if copies > 1:
            score_grad = jnp.where(keep, score_grad, 0.0)
            probs_low = jnp.where(keep, probs_low, jnp.zeros_like(probs_low))
            attended = jnp.where(keep, attended, 0.0)
        score_low = score_grad.astype(jnp.bfloat16)
        grads[:, at : at + HD] = dot(score_low, key) * scale
        grads[:, at + HD : at + 2 * HD] = dot_first(score_low, query) * scale
        grads[:, at + 2 * HD : at + 3 * HD] = dot_first(probs_low, low)
        mixed[:, qkv_cols + head * HD : qkv_cols + (head + 1) * HD] = attended.astype(jnp.bfloat16)
    proj_grad = turn(grads[...], -sin_all)
    proj_low = proj_grad.astype(jnp.bfloat16)
    total[...] = dot_first(attn_in, proj_low) + dot_first(seq_grads, mixed[...])
    send_blocks(total, grad_outs)
    branch[...] = dot_last(mixed[...], weight[...])
    norm_grad = dot_last(proj_low, weight[...])
    norm_out[...] = norm_grad * gain[...]
    sums[...] = jnp.concatenate(
        [
            jnp.sum(norm_grad * centred, axis=0, keepdims=True),
            jnp.sum(norm_grad, axis=0, keepdims=True),
            jnp.sum(proj_grad, axis=0, keepdims=True),
        ],
        axis=0,
    )


def mlp_kernel(fsdp_count, core_count, near, head_groups, seqs, padded, *refs):
    row_refs = refs[:core_count]
    parts = refs[core_count : core_count + fsdp_count]
    gain, shift, bias, attn_branch, attn_norm = refs[
        core_count + fsdp_count : core_count + fsdp_count + 5
    ]
    outs = refs[core_count + fsdp_count + 5 :]
    branches = outs[:core_count]
    norms = outs[core_count : 2 * core_count]
    sums, bias_out = outs[2 * core_count : 2 * core_count + 2]
    grad_outs = outs[2 * core_count + 2 : 2 * core_count + 2 + fsdp_count]
    weight, total = outs[2 * core_count + 2 + fsdp_count :]
    size = attn_branch.shape[0]
    seq_at = lax.rem(lax.div(lax.axis_index("ctx"), head_groups), seqs)
    core = lax.div(seq_at, near) ^ lax.axis_index("tp")
    inner = lax.rem(seq_at, near)
    place_weight(parts, weight)
    up, down = weight[:, :padded], weight[:, padded:]
    gain_sum = shift_sum = bias_sum = 0.0
    for j in range(core_count):
        width = weight.shape[0]
        rows = row_refs[j][0].reshape(near * size, width)
        grad_rows = row_refs[j][1].reshape(near * size, width)
        centred, _ = normed_rows(rows.astype(jnp.float32))
        mlp_in = (centred * gain[...] + shift[...]).astype(jnp.bfloat16)
        pre_act = dot(mlp_in, up) + bias[...]
        normal = 0.5 * (1.0 + lax.erf(pre_act * ROOT_HALF))
        hidden = (pre_act * normal).astype(jnp.bfloat16)
        slope = normal + pre_act * jnp.exp(-0.5 * pre_act * pre_act) * INV_ROOT_TWO_PI
        pre_grad = dot(grad_rows, down) * slope
        pre_low = pre_grad.astype(jnp.bfloat16)
        up_part, down_part = dot_first(mlp_in, pre_low), dot_first(grad_rows, hidden)
        if j:
            total[:, :padded] += up_part
            total[:, padded:] += down_part
        else:
            total[:, :padded] = up_part
            total[:, padded:] = down_part
        norm_grad = dot_last(pre_low, up)
        gain_sum = gain_sum + jnp.sum(norm_grad * centred, axis=0, keepdims=True)
        shift_sum = shift_sum + jnp.sum(norm_grad, axis=0, keepdims=True)
        bias_sum = bias_sum + jnp.sum(pre_grad, axis=0, keepdims=True)
        norm_grad = norm_grad * gain[...]
        branch = dot_last(hidden, down)
        for i in range(near):
            here = (core == j) & (inner == i)
            span = slice(i * size, (i + 1) * size)
            branches[j][span, :] = branch[span] + jnp.where(here, attn_branch[...], 0.0)
            norms[j][span, :] = norm_grad[span] + jnp.where(here, attn_norm[...], 0.0)
    send_blocks(total, grad_outs)
    sums[...] = jnp.concatenate([gain_sum, shift_sum], axis=0)
    bias_out[...] = bias_sum


def sum_blocks_kernel(fsdp_count, *refs):
    parts, outs = refs[:fsdp_count], refs[fsdp_count:]
    at = lax.axis_index("ctx")
    for k, out in enumerate(outs):
        rank = at ^ k
        block = parts[0][rank]
        for part in parts[1:]:
            block = block + part[rank].astype(jnp.float32)
        out[...] = block.astype(out.dtype)


def early_end_kernel(count, groups, qkv_cols, features, *refs):
    parts, (qkv_out, dense_out) = refs[:count], refs[count:]
    at = lax.rem(lax.axis_index("ctx"), groups)
    sums = []
    for g in range(groups):
        block = parts[g][...].astype(jnp.float32)
        for part in parts[g + groups :: groups]:
            block = block + part[...].astype(jnp.float32)
        sums.append(block)
    for g, block in enumerate(swapped(sums, at)):
        qkv_out[:, g * qkv_cols : (g + 1) * qkv_cols] = block[:, :qkv_cols]
        dense_out[g * features : (g + 1) * features, :] = block[:, qkv_cols:].T


def late_end_kernel(count, ff, padded, *refs):
    parts, (up_out, down_out) = refs[:count], refs[count:]
    blocks = [part[...].astype(jnp.float32) for part in parts]
    for r, block in enumerate(swapped(blocks, lax.axis_index("ctx"))):
        up_out[:, r * ff : (r + 1) * ff] = block[:, :ff]
        down_out[r * ff : (r + 1) * ff, :] = block[:, padded : padded + ff].T


def on_device(
    tokens,
    group_order,
    attn_gain,
    attn_shift,
    qkv_weight,
    qkv_bias,
    dense_weight,
    dense_bias,
    mlp_gain,
    mlp_shift,
    up_weight,
    up_bias,
    down_weight,
    down_bias,
    out_grad,
):
    bf16, f32 = jnp.bfloat16, jnp.float32
    seqs, length, width = tokens.shape
    fsdp_count, ctx_count, tp_count = (lax.axis_size(a) for a in ("fsdp", "ctx", "tp"))
    ctx_at, tp_at = lax.axis_index("ctx"), lax.axis_index("tp")
    rows_here = qkv_weight.shape[0]
    block_rows = ctx_count * rows_here
    heads = qkv_bias.shape[0] // (3 * HD)
    hidden_all = up_bias.shape[0]
    head_groups = math.gcd(heads, ctx_count)
    own_heads = heads // head_groups
    copies = ctx_count // head_groups // seqs
    features = own_heads * HD
    qkv_cols = 3 * features
    cols = qkv_cols + features
    ff = hidden_all // ctx_count
    padded = -(-ff // LANES) * LANES
    head_at = ctx_at % head_groups
    near = seqs // tp_count
    size = ctx_count * length
    near_rows = near * size

    early = local_kernel(
        functools.partial(early_message_kernel, head_groups, qkv_cols, features),
        [shaped((rows_here, cols), bf16)] * head_groups,
    )(qkv_weight, dense_weight)
    late = local_kernel(
        functools.partial(late_message_kernel, ctx_count, ff, padded),
        [shaped((rows_here, 2 * padded), bf16)] * ctx_count,
    )(up_weight, down_weight)
    early_rows = exchange([early[k % head_groups] for k in range(ctx_count)], "ctx")

    def near_part(array):
        parts = [array[j * near : (j + 1) * near] for j in range(tp_count)]
        return swapped(parts, tp_at)[0]

    own_tokens = near_part(tokens)
    own_grads = near_part(out_grad)
    message = jnp.stack([own_tokens, own_grads.astype(bf16)])
    early_rows, message = lax.optimization_barrier((early_rows, message))
    late_rows = exchange(late, "ctx")
    chunks = jnp.stack(spread(message, "ctx"), axis=2).reshape(2, near, size, width)

    def own_rows(parts):
        return jnp.concatenate(swapped(parts, ctx_at), axis=0)

    early_parts = spread(own_rows(early_rows), "fsdp")
    late_parts = spread(own_rows(late_rows), "fsdp")
    by_core = spread(chunks, "tp")

    position = jnp.concatenate(
        [positions(group_order, (ctx_at ^ k) * length, length) for k in range(ctx_count)]
    )
    cos_table, sin_table = rotary_tables(position)
    place = position.astype(f32)

    def row(vector):
        return vector.reshape(1, -1)

    qkv_parts = [qkv_bias[g * qkv_cols : (g + 1) * qkv_cols] for g in range(head_groups)]
    qkv_own = jnp.pad(swapped(qkv_parts, head_at)[0], (0, features))
    up_parts = [up_bias[r * ff : (r + 1) * ff] for r in range(ctx_count)]
    up_own = jnp.pad(swapped(up_parts, ctx_at)[0], (0, padded - ff))

    def grad_blocks(columns):
        return [
            shaped((block_rows, columns), bf16 if k else f32) for k in range(fsdp_count)
        ]

    attn_branch, attn_norm, attn_sums, *early_grads = local_kernel(
        functools.partial(
            attention_kernel, fsdp_count, tp_count, near, head_groups, own_heads, copies, seqs
        ),
        [shaped((size, width), f32), shaped((size, width), f32), shaped((3, cols), f32)]
        + grad_blocks(cols),
        [
            pltpu.VMEM((width, cols), bf16),
            pltpu.VMEM((size, cols), f32),
            pltpu.VMEM((size, cols), bf16),
            pltpu.VMEM((width, cols), f32),
        ],
        flops=16 * size * width * cols,
        moved=16 * size * width,
    )(
        *by_core,
        *early_parts,
        row(attn_gain),
        row(attn_shift),
        row(qkv_own),
        cos_table,
        sin_table,
        place.reshape(-1, 1),
        row(place),
    )
    outs = local_kernel(
        functools.partial(mlp_kernel, fsdp_count, tp_count, near, head_groups, seqs, padded),
        [shaped((near_rows, width), f32)] * (2 * tp_count)
        + [shaped((2, width), f32), shaped((1, padded), f32)]
        + grad_blocks(2 * padded),
        [pltpu.VMEM((width, 2 * padded), bf16), pltpu.VMEM((width, 2 * padded), f32)],
        flops=12 * seqs * size * width * padded,
        moved=32 * size * width,
    )(
        *by_core,
        *late_parts,
        row(mlp_gain),
        row(mlp_shift),
        row(up_own),
        attn_branch,
        attn_norm,
    )
    branch_parts, norm_parts = outs[:tp_count], outs[tp_count : 2 * tp_count]
    mlp_sums, up_bias_part = outs[2 * tp_count : 2 * tp_count + 2]
    late_grads = outs[2 * tp_count + 2 :]

    def scatter_rows(parts):
        half = sum(exchange(parts, "tp")).reshape(near, ctx_count, length, width)
        sent = [half[:, k].astype(bf16) if k else half[:, 0] for k in range(ctx_count)]
        return sum(part.astype(f32) for part in exchange(sent, "ctx"))

    def both_cores(half):
        return jnp.concatenate(swapped(spread(half, "tp"), tp_at), axis=0)

    def scatter_weights(parts):
        columns = parts[0].shape[1]
        received = [
            part.reshape(ctx_count, rows_here, columns) for part in exchange(parts, "fsdp")
        ]
        pieces = local_kernel(
            functools.partial(sum_blocks_kernel, fsdp_count),
            [shaped((rows_here, columns), bf16 if k else f32) for k in range(ctx_count)],
        )(*received)
        return exchange(pieces, "ctx")

    early_pieces = scatter_weights(early_grads)
    late_pieces = scatter_weights(late_grads)
    branches = scatter_rows(branch_parts)
    inner = scatter_rows(norm_parts)
    block_half = own_tokens.astype(f32) + branches + (dense_bias + down_bias)
    block_out = both_cores(block_half.astype(bf16))
    own_centred, own_inverse = normed_rows(own_tokens.astype(f32))
    inner = (
        inner
        - jnp.mean(inner, axis=-1, keepdims=True)
        - own_centred * jnp.mean(inner * own_centred, axis=-1, keepdims=True)
    )
    tokens_grad = both_cores(own_grads + own_inverse * inner)
    qkv_weight_grad, dense_weight_grad = local_kernel(
        functools.partial(early_end_kernel, ctx_count, head_groups, qkv_cols, features),
        [shaped(qkv_weight.shape, f32), shaped(dense_weight.shape, f32)],
    )(*early_pieces)
    up_weight_grad, down_weight_grad = local_kernel(
        functools.partial(late_end_kernel, ctx_count, ff, padded),
        [shaped(up_weight.shape, f32), shaped(down_weight.shape, f32)],
    )(*late_pieces)

    gain_parts = jnp.concatenate([attn_sums[:2].reshape(-1), mlp_sums.reshape(-1)])
    bias_parts = jnp.concatenate(
        [
            jnp.sum(out_grad, axis=(0, 1)),
            one_hot_slots(attn_sums[2, :qkv_cols], head_at, head_groups),
            one_hot_slots(up_bias_part[0, :ff], ctx_at, ctx_count),
        ]
    )
    small = jnp.concatenate([butterfly(gain_parts, "tp"), bias_parts])
    small = butterfly(butterfly(small, "fsdp"), "ctx")
    cuts = []
    start = 0
    for extent in [width] * 5 + [3 * HD * heads, hidden_all]:
        cuts.append(small[start : start + extent])
        start += extent
    return (
        block_out,
        tokens_grad,
        cuts[0],
        cuts[1],
        qkv_weight_grad,
        cuts[5],
        dense_weight_grad,
        cuts[4],
        cuts[2],
        cuts[3],
        up_weight_grad,
        cuts[6],
        down_weight_grad,
        cuts[4],
    )


def solution(mesh):
    in_specs = (
        P("fsdp", "ctx", None),
        P(),
        P(),
        P(),
        P(("fsdp", "ctx"), "tp"),
        P("tp"),
        P("tp", ("fsdp", "ctx")),
        P(),
        P(),
        P(),
        P(("fsdp", "ctx"), "tp"),
        P("tp"),
        P("tp", ("fsdp", "ctx")),
        P(),
        P("fsdp", "ctx", None),
    )
    out_specs = (
        P("fsdp", "ctx", None),
        P("fsdp", "ctx", None),
        P(),
        P(),
        P(("fsdp", "ctx"), "tp"),
        P("tp"),
        P("tp", ("fsdp", "ctx")),
        P(),
        P(),
        P(),
        P(("fsdp", "ctx"), "tp"),
        P("tp"),
        P("tp", ("fsdp", "ctx")),
        P(),
    )
    return jax.shard_map(
        on_device, mesh=mesh, in_specs=in_specs, out_specs=out_specs, check_vma=False
    )
```

```python
import functools
import math

import jax
import jax.numpy as jnp
from jax import lax
from jax.experimental import pallas as pl
from jax.experimental.pallas import tpu as pltpu
from jax.sharding import PartitionSpec as P


HD = 64
ROT = 16
BLK = 32


EPSILON = 1e-05
NEGATIVE = -1e30
ROOT_HALF = 0.7071067811865476
INV_ROOT_TWO_PI = 0.3989422804014327
CONTRACT_LAST = (((1,), (1,)), ((), ()))
CONTRACT_FIRST = (((0,), (0,)), ((), ()))


def angle_tables(position):
    half = ROT // 2
    frequency = 1.0 / 10000.0 ** (jnp.arange(half, dtype=jnp.float32) * (2.0 / ROT))
    phase = position.astype(jnp.float32)[:, None] * frequency[None, :]
    return (jnp.cos(phase), jnp.sin(phase))


def positions(order, start, count):
    index = start + jnp.arange(count, dtype=jnp.int32)
    slot = index // BLK
    table = jnp.arange(order.shape[0], dtype=jnp.int32)
    first = jnp.sum(jnp.where(slot[:, None] == table[None, :], order[None, :], 0), axis=1)
    return first * BLK + index % BLK


def swapped(parts, index):
    bit = 1
    while bit < len(parts):
        is_set = (index & bit) != 0
        parts = [jnp.where(is_set, parts[j ^ bit], parts[j]) for j in range(len(parts))]
        bit *= 2
    return parts


def swap(value, axis, bit):
    return lax.ppermute(value, axis, [(i, i ^ bit) for i in range(lax.axis_size(axis))])


def exchange(parts, axis):
    return [parts[0]] + [swap(parts[k], axis, k) for k in range(1, len(parts))]


def spread(value, axis):
    return exchange([value] * lax.axis_size(axis), axis)


def gather_order(count):
    order, bit = [0], count // 2
    while bit:
        order = order + [k ^ bit for k in order]
        bit //= 2
    return order


def gather_chunks(value, axis, dim):
    bit = lax.axis_size(axis) // 2
    while bit:
        other = swap(value, axis, bit)
        value = jnp.concatenate([value, other], axis=dim)
        bit //= 2
    return value


def scatter_chunks(value, axis, dim):
    count = lax.axis_size(axis)
    bit = 1
    while bit < count:
        kept, sent = jnp.split(value, 2, axis=dim)
        other = swap(sent.astype(jnp.bfloat16), axis, bit)
        value = kept + other.astype(jnp.float32)
        bit *= 2
    return value


def butterfly(value, axis):
    bit = 1
    while bit < lax.axis_size(axis):
        other = swap(value, axis, bit)
        value = value + other
        bit *= 2
    return value


def one_hot_slots(value, index, count):
    slots = jnp.arange(count, dtype=jnp.int32)[:, None] == index
    return jnp.where(slots, value[None, :], 0.0).reshape(-1)


def dot(left, right):
    return jnp.dot(left, right, preferred_element_type=jnp.float32)


def dot_last(left, right):
    return lax.dot_general(left, right, CONTRACT_LAST, preferred_element_type=jnp.float32)


def dot_first(left, right):
    return lax.dot_general(left, right, CONTRACT_FIRST, preferred_element_type=jnp.float32)


def normed_rows(rows):
    middle = jnp.mean(rows, axis=-1, keepdims=True)
    centred = rows - middle
    inverse = lax.rsqrt(jnp.mean(centred * centred, axis=-1, keepdims=True) + EPSILON)
    return centred * inverse, inverse


VMEM_LIMIT = 60 * 1024 * 1024
LANES = 128


def local_kernel(body, out_shapes, scratch=(), flops=0, moved=0):
    in_vmem = pl.BlockSpec(memory_space=pltpu.VMEM)
    return pl.pallas_call(
        body,
        out_shape=out_shapes,
        out_specs=jax.tree.map(lambda _: in_vmem, out_shapes),
        scratch_shapes=list(scratch),
        compiler_params=pltpu.CompilerParams(vmem_limit_bytes=VMEM_LIMIT),
        cost_estimate=pl.CostEstimate(flops=flops, bytes_accessed=moved, transcendentals=0),
    )


def shaped(shape, kind):
    return jax.ShapeDtypeStruct(tuple(shape), kind)


def rotary_tables(position):
    cosine, sine = angle_tables(position)
    rest = jnp.ones((position.shape[0], HD - ROT), jnp.float32)
    none = jnp.zeros((position.shape[0], HD - ROT), jnp.float32)
    cos_head = jnp.concatenate([cosine, cosine, rest], axis=1)
    sin_head = jnp.concatenate([-sine, sine, none], axis=1)
    return jnp.concatenate([cos_head] * 2, axis=1), jnp.concatenate([sin_head] * 2, axis=1)


def early_message_kernel(groups, qkv_cols, features, qkv_ref, dense_ref, *outs):
    at = lax.rem(lax.axis_index("ctx"), groups)
    dense_t = dense_ref[...]
    parts = [
        jnp.concatenate(
            [
                qkv_ref[:, g * qkv_cols : (g + 1) * qkv_cols],
                dense_t[:, g * features : (g + 1) * features],
            ],
            axis=1,
        )
        for g in range(groups)
    ]
    for out, part in zip(outs, swapped(parts, at)):
        out[...] = part


def late_message_kernel(count, ff, padded, up_ref, down_ref, *outs):
    at = lax.axis_index("ctx")
    down_t = down_ref[...]
    rows = up_ref.shape[0]
    gap = [jnp.zeros((rows, padded - ff), jnp.bfloat16)] if padded > ff else []
    parts = [
        jnp.concatenate(
            [up_ref[:, r * ff : (r + 1) * ff]] + gap + [down_t[:, r * ff : (r + 1) * ff]] + gap,
            axis=1,
        )
        for r in range(count)
    ]
    for out, part in zip(outs, swapped(parts, at)):
        out[...] = part


def ordered_kernel(*refs):
    parts, out = refs[:-1], refs[-1]
    for r, part in enumerate(swapped([part[...] for part in parts], lax.axis_index("ctx"))):
        out[r] = part


def place_weight(parts, weight):
    at = lax.axis_index("fsdp")
    block = parts[0].shape[0]
    for k, part in enumerate(parts):
        start = pl.multiple_of((at ^ k) * block, 16)
        weight[pl.ds(start, block), :] = part[...]


def send_blocks(total, outs):
    at = lax.axis_index("fsdp")
    block = outs[0].shape[0]
    for k, out in enumerate(outs):
        start = pl.multiple_of((at ^ k) * block, 16)
        out[...] = total[pl.ds(start, block), :].astype(out.dtype)


def attention_kernel(
    fsdp_count,
    core_count,
    near,
    head_groups,
    own_heads,
    copies,
    seqs,
    *refs,
):
    row_refs = refs[:core_count]
    parts = refs[core_count : core_count + fsdp_count]
    (norms, bias, cos_ref, sin_ref, pos_col, pos_row) = refs[
        core_count + fsdp_count : core_count + fsdp_count + 6
    ]
    gain, shift = norms[0:1, :], norms[1:2, :]
    outs = refs[core_count + fsdp_count + 6 :]
    branch, norm_out, sums = outs[:3]
    grad_outs = outs[3 : 3 + fsdp_count]
    weight, grads, mixed, total = outs[3 + fsdp_count :]
    cols = weight.shape[1]
    features = own_heads * HD
    qkv_cols = 3 * features
    scale = 1.0 / math.sqrt(HD)
    ctx_at = lax.axis_index("ctx")
    seq_at = lax.rem(lax.div(ctx_at, head_groups), seqs)
    core = lax.div(seq_at, near) ^ lax.axis_index("tp")
    inner = lax.rem(seq_at, near)
    place_weight(parts, weight)
    seq_tokens, seq_grads = row_refs[0][0, inner], row_refs[0][1, inner]
    for j in range(1, core_count):
        seq_tokens = jnp.where(core == j, row_refs[j][0, inner], seq_tokens)
        seq_grads = jnp.where(core == j, row_refs[j][1, inner], seq_grads)
    centred, _ = normed_rows(seq_tokens.astype(jnp.float32))
    attn_in = (centred * gain + shift).astype(jnp.bfloat16)
    lane = lax.broadcasted_iota(jnp.int32, (1, cols), 1)
    rotated = (lane < qkv_cols) & (lane % (3 * HD) < 2 * HD)
    first = lane % HD < ROT // 2
    repeat = cols // LANES
    cos_all = jnp.where(rotated, jnp.concatenate([cos_ref[...]] * repeat, axis=1), 1.0)
    sin_all = jnp.where(rotated, jnp.concatenate([sin_ref[...]] * repeat, axis=1), 0.0)

    def turn(values, sine):
        ahead = pltpu.roll(values, cols - ROT // 2, 1)
        behind = pltpu.roll(values, ROT // 2, 1)
        return values * cos_all + jnp.where(first, ahead, behind) * sine

    projected = dot(attn_in, weight[...]) + bias[...]
    turned = turn(projected, sin_all).astype(jnp.bfloat16)
    ctx_low = dot(seq_grads, weight[:, qkv_cols:]).astype(jnp.bfloat16)
    allowed = pos_row[...] <= pos_col[...]
    keep = None
    if copies > 1:
        keep = lax.div(ctx_at, head_groups * seqs) == 0
    grads[...] = jnp.zeros(grads.shape, jnp.float32)
    mixed[...] = jnp.zeros(mixed.shape, jnp.bfloat16)
    for head in range(own_heads):
        at = head * 3 * HD
        query = turned[:, at : at + HD]
        key = turned[:, at + HD : at + 2 * HD]
        value = turned[:, at + 2 * HD : at + 3 * HD]
        low = ctx_low[:, head * HD : (head + 1) * HD]
        scores = jnp.where(allowed, dot_last(query, key) * scale, NEGATIVE)
        peak = jnp.max(scores, axis=-1, keepdims=True)
        weights = jnp.where(allowed, jnp.exp(scores - peak), 0.0)
        probs = weights / jnp.sum(weights, axis=-1, keepdims=True)
        probs_low = probs.astype(jnp.bfloat16)
        attended = dot(probs_low, value)
        delta = jnp.sum(low.astype(jnp.float32) * attended, axis=-1, keepdims=True)
        score_grad = probs * (dot_last(low, value) - delta)
        if copies > 1:
            score_grad = jnp.where(keep, score_grad, 0.0)
            probs_low = jnp.where(keep, probs_low, jnp.zeros_like(probs_low))
            attended = jnp.where(keep, attended, 0.0)
        score_low = score_grad.astype(jnp.bfloat16)
        grads[:, at : at + HD] = dot(score_low, key) * scale
        grads[:, at + HD : at + 2 * HD] = dot_first(score_low, query) * scale
        grads[:, at + 2 * HD : at + 3 * HD] = dot_first(probs_low, low)
        mixed[:, qkv_cols + head * HD : qkv_cols + (head + 1) * HD] = attended.astype(jnp.bfloat16)
    proj_grad = turn(grads[...], -sin_all)
    proj_low = proj_grad.astype(jnp.bfloat16)
    total[...] = dot_first(attn_in, proj_low) + dot_first(seq_grads, mixed[...])
    send_blocks(total, grad_outs)
    branch[...] = dot_last(mixed[...], weight[...])
    norm_grad = dot_last(proj_low, weight[...])
    norm_out[...] = norm_grad * gain
    sums[...] = jnp.concatenate(
        [
            jnp.sum(norm_grad * centred, axis=0, keepdims=True),
            jnp.sum(norm_grad, axis=0, keepdims=True),
            jnp.sum(proj_grad, axis=0, keepdims=True),
        ],
        axis=0,
    )


def mlp_kernel(fsdp_count, core_count, near, head_groups, seqs, padded, *refs):
    row_refs = refs[:core_count]
    parts = refs[core_count : core_count + fsdp_count]
    norm_ref, bias, attn_branch, attn_norm = refs[
        core_count + fsdp_count : core_count + fsdp_count + 4
    ]
    gain, shift = norm_ref[2:3, :], norm_ref[3:4, :]
    outs = refs[core_count + fsdp_count + 4 :]
    branches = outs[:core_count]
    norms = outs[core_count : 2 * core_count]
    sums, bias_out = outs[2 * core_count : 2 * core_count + 2]
    grad_outs = outs[2 * core_count + 2 : 2 * core_count + 2 + fsdp_count]
    weight, total = outs[2 * core_count + 2 + fsdp_count :]
    size = attn_branch.shape[0]
    seq_at = lax.rem(lax.div(lax.axis_index("ctx"), head_groups), seqs)
    core = lax.div(seq_at, near) ^ lax.axis_index("tp")
    inner = lax.rem(seq_at, near)
    place_weight(parts, weight)
    up, down = weight[:, :padded], weight[:, padded:]
    gain_sum = shift_sum = bias_sum = 0.0
    for j in range(core_count):
        width = weight.shape[0]
        rows = row_refs[j][0].reshape(near * size, width)
        grad_rows = row_refs[j][1].reshape(near * size, width)
        centred, _ = normed_rows(rows.astype(jnp.float32))
        mlp_in = (centred * gain + shift).astype(jnp.bfloat16)
        pre_act = dot(mlp_in, up) + bias[...]
        normal = 0.5 * (1.0 + lax.erf(pre_act * ROOT_HALF))
        hidden = (pre_act * normal).astype(jnp.bfloat16)
        slope = normal + pre_act * jnp.exp(-0.5 * pre_act * pre_act) * INV_ROOT_TWO_PI
        pre_grad = dot(grad_rows, down) * slope
        pre_low = pre_grad.astype(jnp.bfloat16)
        up_part, down_part = dot_first(mlp_in, pre_low), dot_first(grad_rows, hidden)
        if j:
            total[:, :padded] += up_part
            total[:, padded:] += down_part
        else:
            total[:, :padded] = up_part
            total[:, padded:] = down_part
        norm_grad = dot_last(pre_low, up)
        gain_sum = gain_sum + jnp.sum(norm_grad * centred, axis=0, keepdims=True)
        shift_sum = shift_sum + jnp.sum(norm_grad, axis=0, keepdims=True)
        bias_sum = bias_sum + jnp.sum(pre_grad, axis=0, keepdims=True)
        norm_grad = norm_grad * gain
        branch = dot_last(hidden, down)
        for i in range(near):
            here = (core == j) & (inner == i)
            span = slice(i * size, (i + 1) * size)
            branches[j][span, :] = branch[span] + jnp.where(here, attn_branch[...], 0.0)
            norms[j][span, :] = norm_grad[span] + jnp.where(here, attn_norm[...], 0.0)
    send_blocks(total, grad_outs)
    sums[...] = jnp.concatenate([gain_sum, shift_sum], axis=0)
    bias_out[...] = bias_sum


def sum_blocks_kernel(fsdp_count, *refs):
    parts, outs = refs[:fsdp_count], refs[fsdp_count:]
    at = lax.axis_index("ctx")
    for k, out in enumerate(outs):
        rank = at ^ k
        block = parts[0][rank]
        for part in parts[1:]:
            block = block + part[rank].astype(jnp.float32)
        out[...] = block.astype(out.dtype)


def early_end_kernel(count, groups, qkv_cols, features, *refs):
    parts, (qkv_out, dense_out) = refs[:count], refs[count:]
    at = lax.rem(lax.axis_index("ctx"), groups)
    sums = []
    for g in range(groups):
        block = parts[g][...].astype(jnp.float32)
        for part in parts[g + groups :: groups]:
            block = block + part[...].astype(jnp.float32)
        sums.append(block)
    for g, block in enumerate(swapped(sums, at)):
        qkv_out[:, g * qkv_cols : (g + 1) * qkv_cols] = block[:, :qkv_cols]
        dense_out[:, g * features : (g + 1) * features] = block[:, qkv_cols:]


def late_end_kernel(count, ff, padded, *refs):
    parts, (up_out, down_out) = refs[:count], refs[count:]
    blocks = [part[...].astype(jnp.float32) for part in parts]
    for r, block in enumerate(swapped(blocks, lax.axis_index("ctx"))):
        up_out[:, r * ff : (r + 1) * ff] = block[:, :ff]
        down_out[:, r * ff : (r + 1) * ff] = block[:, padded : padded + ff]


def on_device(
    tokens,
    group_order,
    attn_gain,
    attn_shift,
    qkv_weight,
    qkv_bias,
    dense_weight,
    dense_bias,
    mlp_gain,
    mlp_shift,
    up_weight,
    up_bias,
    down_weight,
    down_bias,
    out_grad,
):
    bf16, f32 = jnp.bfloat16, jnp.float32
    seqs, length, width = tokens.shape
    fsdp_count, ctx_count, tp_count = (lax.axis_size(a) for a in ("fsdp", "ctx", "tp"))
    ctx_at, tp_at = lax.axis_index("ctx"), lax.axis_index("tp")
    rows_here = qkv_weight.shape[0]
    block_rows = ctx_count * rows_here
    heads = qkv_bias.shape[0] // (3 * HD)
    hidden_all = up_bias.shape[0]
    head_groups = math.gcd(heads, ctx_count)
    own_heads = heads // head_groups
    copies = ctx_count // head_groups // seqs
    features = own_heads * HD
    qkv_cols = 3 * features
    cols = qkv_cols + features
    ff = hidden_all // ctx_count
    padded = -(-ff // LANES) * LANES
    head_at = ctx_at % head_groups
    near = seqs // tp_count
    size = ctx_count * length
    near_rows = near * size

    early = local_kernel(
        functools.partial(early_message_kernel, head_groups, qkv_cols, features),
        [shaped((rows_here, cols), bf16)] * head_groups,
    )(qkv_weight, dense_weight.T)
    late = local_kernel(
        functools.partial(late_message_kernel, ctx_count, ff, padded),
        [shaped((rows_here, 2 * padded), bf16)] * ctx_count,
    )(up_weight, down_weight.T)
    early_rows = exchange([early[k % head_groups] for k in range(ctx_count)], "ctx")

    def near_part(array):
        parts = [array[j * near : (j + 1) * near] for j in range(tp_count)]
        return swapped(parts, tp_at)[0]

    own_tokens = near_part(tokens)
    own_grads = near_part(out_grad)
    message = jnp.stack([own_tokens, own_grads.astype(bf16)])
    late_rows = exchange(late, "ctx")
    chunks = gather_chunks(message[:, :, None], "ctx", 2)
    chunks = chunks.reshape(2, near, size, width)

    def own_rows(parts):
        shape = (ctx_count, rows_here, parts[0].shape[1])
        return local_kernel(ordered_kernel, shaped(shape, bf16))(*parts).reshape(block_rows, -1)

    early_parts = spread(own_rows(early_rows), "fsdp")
    late_parts = spread(own_rows(late_rows), "fsdp")
    by_core = spread(chunks, "tp")

    position = jnp.concatenate(
        [
            positions(group_order, (ctx_at ^ k) * length, length)
            for k in gather_order(ctx_count)
        ]
    )
    cos_table, sin_table = rotary_tables(position)
    place = position.astype(f32)
    norms = jnp.stack([attn_gain, attn_shift, mlp_gain, mlp_shift])

    def row(vector):
        return vector.reshape(1, -1)

    qkv_parts = [qkv_bias[g * qkv_cols : (g + 1) * qkv_cols] for g in range(head_groups)]
    qkv_own = jnp.pad(swapped(qkv_parts, head_at)[0], (0, features))
    up_parts = [up_bias[r * ff : (r + 1) * ff] for r in range(ctx_count)]
    up_own = jnp.pad(swapped(up_parts, ctx_at)[0], (0, padded - ff))

    def grad_blocks(columns):
        return [
            shaped((block_rows, columns), bf16 if k else f32) for k in range(fsdp_count)
        ]

    attn_branch, attn_norm, attn_sums, *early_grads = local_kernel(
        functools.partial(
            attention_kernel, fsdp_count, tp_count, near, head_groups, own_heads, copies, seqs
        ),
        [shaped((size, width), f32), shaped((size, width), f32), shaped((3, cols), f32)]
        + grad_blocks(cols),
        [
            pltpu.VMEM((width, cols), bf16),
            pltpu.VMEM((size, cols), f32),
            pltpu.VMEM((size, cols), bf16),
            pltpu.VMEM((width, cols), f32),
        ],
        flops=16 * size * width * cols,
        moved=16 * size * width,
    )(
        *by_core,
        *early_parts,
        norms,
        row(qkv_own),
        cos_table,
        sin_table,
        place.reshape(-1, 1),
        row(place),
    )
    outs = local_kernel(
        functools.partial(mlp_kernel, fsdp_count, tp_count, near, head_groups, seqs, padded),
        [shaped((near_rows, width), f32)] * (2 * tp_count)
        + [shaped((2, width), f32), shaped((1, padded), f32)]
        + grad_blocks(2 * padded),
        [pltpu.VMEM((width, 2 * padded), bf16), pltpu.VMEM((width, 2 * padded), f32)],
        flops=12 * seqs * size * width * padded,
        moved=32 * size * width,
    )(
        *by_core,
        *late_parts,
        norms,
        row(up_own),
        attn_branch,
        attn_norm,
    )
    branch_parts, norm_parts = outs[:tp_count], outs[tp_count : 2 * tp_count]
    mlp_sums, up_bias_part = outs[2 * tp_count : 2 * tp_count + 2]
    late_grads = outs[2 * tp_count + 2 :]

    def scatter_rows(parts):
        half = sum(exchange(parts, "tp")).reshape(near, ctx_count, length, width)
        return scatter_chunks(half, "ctx", 1).reshape(near, length, width)

    def both_cores(half):
        return jnp.concatenate(swapped(spread(half, "tp"), tp_at), axis=0)

    def scatter_weights(parts):
        columns = parts[0].shape[1]
        received = [part.reshape(ctx_count, rows_here, columns) for part in exchange(parts, "fsdp")]
        pieces = local_kernel(
            functools.partial(sum_blocks_kernel, fsdp_count),
            [shaped((rows_here, columns), bf16 if k else f32) for k in range(ctx_count)],
        )(*received)
        return exchange(pieces, "ctx")

    early_pieces = scatter_weights(early_grads)
    late_pieces = scatter_weights(late_grads)
    branches = scatter_rows(branch_parts)
    inner = scatter_rows(norm_parts)
    block_half = own_tokens.astype(f32) + branches + (dense_bias + down_bias)
    block_out = both_cores(block_half.astype(bf16))
    own_centred, own_inverse = normed_rows(own_tokens.astype(f32))
    inner = (
        inner
        - jnp.mean(inner, axis=-1, keepdims=True)
        - own_centred * jnp.mean(inner * own_centred, axis=-1, keepdims=True)
    )
    tokens_grad = both_cores(own_grads + own_inverse * inner)
    qkv_weight_grad, dense_weight_grad = local_kernel(
        functools.partial(early_end_kernel, ctx_count, head_groups, qkv_cols, features),
        [shaped(qkv_weight.shape, f32), shaped(dense_weight.shape[::-1], f32)],
    )(*early_pieces)
    up_weight_grad, down_weight_grad = local_kernel(
        functools.partial(late_end_kernel, ctx_count, ff, padded),
        [shaped(up_weight.shape, f32), shaped(down_weight.shape[::-1], f32)],
    )(*late_pieces)

    gain_parts = jnp.concatenate([attn_sums[:2].reshape(-1), mlp_sums.reshape(-1)])
    bias_parts = jnp.concatenate(
        [
            jnp.sum(out_grad, axis=(0, 1)),
            one_hot_slots(attn_sums[2, :qkv_cols], head_at, head_groups),
            one_hot_slots(up_bias_part[0, :ff], ctx_at, ctx_count),
        ]
    )
    small = jnp.concatenate([butterfly(gain_parts, "tp"), bias_parts])
    small = butterfly(butterfly(small, "fsdp"), "ctx")
    cuts = []
    start = 0
    for extent in [width] * 5 + [3 * HD * heads, hidden_all]:
        cuts.append(small[start : start + extent])
        start += extent
    return (
        block_out,
        tokens_grad,
        cuts[0],
        cuts[1],
        qkv_weight_grad,
        cuts[5],
        dense_weight_grad.T,
        cuts[4],
        cuts[2],
        cuts[3],
        up_weight_grad,
        cuts[6],
        down_weight_grad.T,
        cuts[4],
    )


def solution(mesh):
    in_specs = (
        P("fsdp", "ctx", None),
        P(),
        P(),
        P(),
        P(("fsdp", "ctx"), "tp"),
        P("tp"),
        P("tp", ("fsdp", "ctx")),
        P(),
        P(),
        P(),
        P(("fsdp", "ctx"), "tp"),
        P("tp"),
        P("tp", ("fsdp", "ctx")),
        P(),
        P("fsdp", "ctx", None),
    )
    out_specs = (
        P("fsdp", "ctx", None),
        P("fsdp", "ctx", None),
        P(),
        P(),
        P(("fsdp", "ctx"), "tp"),
        P("tp"),
        P("tp", ("fsdp", "ctx")),
        P(),
        P(),
        P(),
        P(("fsdp", "ctx"), "tp"),
        P("tp"),
        P("tp", ("fsdp", "ctx")),
        P(),
    )

    return jax.shard_map(
        on_device, mesh=mesh, in_specs=in_specs, out_specs=out_specs, check_vma=False
    )
```

```python
import functools
import math

import jax
import jax.numpy as jnp
from jax import lax
from jax.experimental import pallas as pl
from jax.experimental.pallas import tpu as pltpu
from jax.sharding import PartitionSpec as P


HD = 64
ROT = 16
BLK = 32


EPSILON = 1e-05
NEGATIVE = -1e30
ROOT_HALF = 0.7071067811865476
INV_ROOT_TWO_PI = 0.3989422804014327
CONTRACT_LAST = (((1,), (1,)), ((), ()))
CONTRACT_FIRST = (((0,), (0,)), ((), ()))


def angle_tables(position):
    half = ROT // 2
    frequency = 1.0 / 10000.0 ** (jnp.arange(half, dtype=jnp.float32) * (2.0 / ROT))
    phase = position.astype(jnp.float32)[:, None] * frequency[None, :]
    return (jnp.cos(phase), jnp.sin(phase))


def positions(order, start, count):
    index = start + jnp.arange(count, dtype=jnp.int32)
    slot = index // BLK
    table = jnp.arange(order.shape[0], dtype=jnp.int32)
    first = jnp.sum(jnp.where(slot[:, None] == table[None, :], order[None, :], 0), axis=1)
    return first * BLK + index % BLK


def swapped(parts, index):
    bit = 1
    while bit < len(parts):
        is_set = (index & bit) != 0
        parts = [jnp.where(is_set, parts[j ^ bit], parts[j]) for j in range(len(parts))]
        bit *= 2
    return parts


def swap(value, axis, bit):
    return lax.ppermute(value, axis, [(i, i ^ bit) for i in range(lax.axis_size(axis))])


def exchange(parts, axis):
    return [parts[0]] + [swap(parts[k], axis, k) for k in range(1, len(parts))]


def spread(value, axis):
    return exchange([value] * lax.axis_size(axis), axis)


def gather_order(count):
    order, bit = [0], count // 2
    while bit:
        order = order + [k ^ bit for k in order]
        bit //= 2
    return order


def gather_chunks(value, axis, dim):
    bit = lax.axis_size(axis) // 2
    while bit:
        other = swap(value, axis, bit)
        value = jnp.concatenate([value, other], axis=dim)
        bit //= 2
    return value


def scatter_chunks(value, axis, dim):
    count = lax.axis_size(axis)
    bit = 1
    while bit < count:
        kept, sent = jnp.split(value, 2, axis=dim)
        other = swap(sent.astype(jnp.bfloat16), axis, bit)
        value = kept + other.astype(jnp.float32)
        bit *= 2
    return value


def butterfly(value, axis):
    bit = 1
    while bit < lax.axis_size(axis):
        other = swap(value, axis, bit)
        value = value + other
        bit *= 2
    return value


def one_hot_slots(value, index, count):
    slots = jnp.arange(count, dtype=jnp.int32)[:, None] == index
    return jnp.where(slots, value[None, :], 0.0).reshape(-1)


def dot(left, right):
    return jnp.dot(left, right, preferred_element_type=jnp.float32)


def dot_last(left, right):
    return lax.dot_general(left, right, CONTRACT_LAST, preferred_element_type=jnp.float32)


def dot_first(left, right):
    return lax.dot_general(left, right, CONTRACT_FIRST, preferred_element_type=jnp.float32)


def normed_rows(rows):
    middle = jnp.mean(rows, axis=-1, keepdims=True)
    centred = rows - middle
    inverse = lax.rsqrt(jnp.mean(centred * centred, axis=-1, keepdims=True) + EPSILON)
    return centred * inverse, inverse


VMEM_LIMIT = 60 * 1024 * 1024
LANES = 128
SUBLANES = 16


def local_kernel(body, out_shapes, scratch=(), flops=0, moved=0):
    in_vmem = pl.BlockSpec(memory_space=pltpu.VMEM)
    return pl.pallas_call(
        body,
        out_shape=out_shapes,
        out_specs=jax.tree.map(lambda _: in_vmem, out_shapes),
        scratch_shapes=list(scratch),
        compiler_params=pltpu.CompilerParams(vmem_limit_bytes=VMEM_LIMIT),
        cost_estimate=pl.CostEstimate(flops=flops, bytes_accessed=moved, transcendentals=0),
    )


def shaped(shape, kind):
    return jax.ShapeDtypeStruct(tuple(shape), kind)


def rotary_tables(position):
    cosine, sine = angle_tables(position)
    rest = jnp.ones((position.shape[0], HD - ROT), jnp.float32)
    none = jnp.zeros((position.shape[0], HD - ROT), jnp.float32)
    cos_head = jnp.concatenate([cosine, cosine, rest], axis=1)
    sin_head = jnp.concatenate([-sine, sine, none], axis=1)
    return jnp.concatenate([cos_head] * 2, axis=1), jnp.concatenate([sin_head] * 2, axis=1)


def early_message_kernel(groups, qkv_cols, features, qkv_ref, dense_ref, *outs):
    at = lax.rem(lax.axis_index("ctx"), groups)
    dense_t = dense_ref[...]
    parts = [
        jnp.concatenate(
            [
                qkv_ref[:, g * qkv_cols : (g + 1) * qkv_cols],
                dense_t[:, g * features : (g + 1) * features],
            ],
            axis=1,
        )
        for g in range(groups)
    ]
    for out, part in zip(outs, swapped(parts, at)):
        out[...] = part


def late_message_kernel(count, ff, padded, up_ref, down_ref, *outs):
    at = lax.axis_index("ctx")
    down_t = down_ref[...]
    rows = up_ref.shape[0]
    gap = [jnp.zeros((rows, padded - ff), jnp.bfloat16)] if padded > ff else []
    parts = [
        jnp.concatenate(
            [up_ref[:, r * ff : (r + 1) * ff]] + gap + [down_t[:, r * ff : (r + 1) * ff]] + gap,
            axis=1,
        )
        for r in range(count)
    ]
    for out, part in zip(outs, swapped(parts, at)):
        out[...] = part


def place_weight(parts, weight, count):
    fsdp_at, ctx_at = lax.axis_index("fsdp"), lax.axis_index("ctx")
    rows = parts[0].shape[0] // count
    for k, part in enumerate(parts):
        for j in range(count):
            place = (fsdp_at ^ k) * count + ((ctx_at ^ j) if count > 1 else 0)
            weight[pl.ds(pl.multiple_of(place * rows, SUBLANES), rows), :] = part[
                j * rows : (j + 1) * rows, :
            ]


def send_blocks(total, outs):
    at = lax.axis_index("fsdp")
    block = outs[0].shape[0]
    for k, out in enumerate(outs):
        start = pl.multiple_of((at ^ k) * block, SUBLANES)
        out[...] = total[pl.ds(start, block), :].astype(out.dtype)


def attention_kernel(
    fsdp_count,
    core_count,
    near,
    head_groups,
    own_heads,
    copies,
    seqs,
    row_blocks,
    *refs,
):
    row_refs = refs[:core_count]
    parts = refs[core_count : core_count + fsdp_count]
    (norms, bias, cos_ref, sin_ref, pos_col, pos_row) = refs[
        core_count + fsdp_count : core_count + fsdp_count + 6
    ]
    gain, shift = norms[0:1, :], norms[1:2, :]
    outs = refs[core_count + fsdp_count + 6 :]
    branch, norm_out, sums, bias_out = outs[:4]
    grad_outs = outs[4 : 4 + fsdp_count]
    weight, grads, mixed, total = outs[4 + fsdp_count :]
    cols = weight.shape[1]
    features = own_heads * HD
    qkv_cols = 3 * features
    scale = 1.0 / math.sqrt(HD)
    ctx_at = lax.axis_index("ctx")
    seq_at = lax.rem(lax.div(ctx_at, head_groups), seqs)
    core = lax.div(seq_at, near) ^ lax.axis_index("tp")
    inner = lax.rem(seq_at, near)
    place_weight(parts, weight, row_blocks)
    seq_tokens, seq_grads = row_refs[0][0, inner], row_refs[0][1, inner]
    for j in range(1, core_count):
        seq_tokens = jnp.where(core == j, row_refs[j][0, inner], seq_tokens)
        seq_grads = jnp.where(core == j, row_refs[j][1, inner], seq_grads)
    centred, _ = normed_rows(seq_tokens.astype(jnp.float32))
    attn_in = (centred * gain + shift).astype(jnp.bfloat16)
    lane = lax.broadcasted_iota(jnp.int32, (1, cols), 1)
    rotated = (lane < qkv_cols) & (lane % (3 * HD) < 2 * HD)
    first = lane % HD < ROT // 2
    repeat = cols // LANES
    cos_all = jnp.where(rotated, jnp.concatenate([cos_ref[...]] * repeat, axis=1), 1.0)
    sin_all = jnp.where(rotated, jnp.concatenate([sin_ref[...]] * repeat, axis=1), 0.0)

    def turn(values, sine):
        ahead = pltpu.roll(values, cols - ROT // 2, 1)
        behind = pltpu.roll(values, ROT // 2, 1)
        return values * cos_all + jnp.where(first, ahead, behind) * sine

    projected = dot(attn_in, weight[...]) + bias[...]
    turned = turn(projected, sin_all).astype(jnp.bfloat16)
    ctx_low = dot(seq_grads, weight[:, qkv_cols:]).astype(jnp.bfloat16)
    allowed = pos_row[...] <= pos_col[...]
    keep = None
    if copies > 1:
        keep = lax.div(ctx_at, head_groups * seqs) == 0
    grads[...] = jnp.zeros(grads.shape, jnp.float32)
    mixed[...] = jnp.zeros(mixed.shape, jnp.bfloat16)
    for head in range(own_heads):
        at = head * 3 * HD
        query = turned[:, at : at + HD]
        key = turned[:, at + HD : at + 2 * HD]
        value = turned[:, at + 2 * HD : at + 3 * HD]
        low = ctx_low[:, head * HD : (head + 1) * HD]
        scores = jnp.where(allowed, dot_last(query, key) * scale, NEGATIVE)
        peak = jnp.max(scores, axis=-1, keepdims=True)
        weights = jnp.where(allowed, jnp.exp(scores - peak), 0.0)
        probs = weights / jnp.sum(weights, axis=-1, keepdims=True)
        probs_low = probs.astype(jnp.bfloat16)
        attended = dot(probs_low, value)
        delta = jnp.sum(low.astype(jnp.float32) * attended, axis=-1, keepdims=True)
        score_grad = probs * (dot_last(low, value) - delta)
        if copies > 1:
            score_grad = jnp.where(keep, score_grad, 0.0)
            probs_low = jnp.where(keep, probs_low, jnp.zeros_like(probs_low))
            attended = jnp.where(keep, attended, 0.0)
        score_low = score_grad.astype(jnp.bfloat16)
        grads[:, at : at + HD] = dot(score_low, key) * scale
        grads[:, at + HD : at + 2 * HD] = dot_first(score_low, query) * scale
        grads[:, at + 2 * HD : at + 3 * HD] = dot_first(probs_low, low)
        mixed[:, qkv_cols + head * HD : qkv_cols + (head + 1) * HD] = attended.astype(jnp.bfloat16)
    proj_grad = turn(grads[...], -sin_all)
    proj_low = proj_grad.astype(jnp.bfloat16)
    total[...] = dot_first(attn_in, proj_low) + dot_first(seq_grads, mixed[...])
    send_blocks(total, grad_outs)
    branch[...] = dot_last(mixed[...], weight[...])
    norm_grad = dot_last(proj_low, weight[...])
    norm_out[...] = norm_grad * gain
    sums[...] = jnp.concatenate(
        [
            jnp.sum(norm_grad * centred, axis=0, keepdims=True),
            jnp.sum(norm_grad, axis=0, keepdims=True),
        ],
        axis=0,
    )
    bias_out[...] = jnp.sum(proj_grad, axis=0, keepdims=True)


def mlp_kernel(fsdp_count, core_count, near, head_groups, seqs, padded, row_blocks, *refs):
    row_refs = refs[:core_count]
    parts = refs[core_count : core_count + fsdp_count]
    norm_ref, bias, attn_branch, attn_norm, attn_sums = refs[
        core_count + fsdp_count : core_count + fsdp_count + 5
    ]
    gain, shift = norm_ref[2:3, :], norm_ref[3:4, :]
    outs = refs[core_count + fsdp_count + 5 :]
    both, bias_out = outs[:core_count], outs[core_count]
    grad_outs = outs[core_count + 1 : core_count + 1 + fsdp_count]
    weight, total = outs[core_count + 1 + fsdp_count :]
    size = attn_branch.shape[0]
    seq_at = lax.rem(lax.div(lax.axis_index("ctx"), head_groups), seqs)
    core = lax.div(seq_at, near) ^ lax.axis_index("tp")
    inner = lax.rem(seq_at, near)
    place_weight(parts, weight, row_blocks)
    up, down = weight[:, :padded], weight[:, padded:]
    gain_sum = shift_sum = bias_sum = 0.0
    for j in range(core_count):
        width = weight.shape[0]
        rows = row_refs[j][0].reshape(near * size, width)
        grad_rows = row_refs[j][1].reshape(near * size, width)
        centred, _ = normed_rows(rows.astype(jnp.float32))
        mlp_in = (centred * gain + shift).astype(jnp.bfloat16)
        pre_act = dot(mlp_in, up) + bias[...]
        normal = 0.5 * (1.0 + lax.erf(pre_act * ROOT_HALF))
        hidden = (pre_act * normal).astype(jnp.bfloat16)
        slope = normal + pre_act * jnp.exp(-0.5 * pre_act * pre_act) * INV_ROOT_TWO_PI
        pre_grad = dot(grad_rows, down) * slope
        pre_low = pre_grad.astype(jnp.bfloat16)
        up_part, down_part = dot_first(mlp_in, pre_low), dot_first(grad_rows, hidden)
        if j:
            total[:, :padded] += up_part
            total[:, padded:] += down_part
        else:
            total[:, :padded] = up_part
            total[:, padded:] = down_part
        norm_grad = dot_last(pre_low, up)
        gain_sum = gain_sum + jnp.sum(norm_grad * centred, axis=0, keepdims=True)
        shift_sum = shift_sum + jnp.sum(norm_grad, axis=0, keepdims=True)
        bias_sum = bias_sum + jnp.sum(pre_grad, axis=0, keepdims=True)
        norm_grad = norm_grad * gain
        branch = dot_last(hidden, down)
        for i in range(near):
            here = (core == j) & (inner == i)
            span = slice(i * size, (i + 1) * size)
            both[j][span, :] = branch[span] + jnp.where(here, attn_branch[...], 0.0)
            span_norm = slice((near + i) * size, (near + i + 1) * size)
            both[j][span_norm, :] = norm_grad[span] + jnp.where(here, attn_norm[...], 0.0)
    send_blocks(total, grad_outs)
    for j in range(core_count):
        both[j][2 * near * size : 2 * near * size + 2, :] = attn_sums[...]
        both[j][2 * near * size + 2 : 2 * near * size + 3, :] = gain_sum
        both[j][2 * near * size + 3 : 2 * near * size + 4, :] = shift_sum
        both[j][2 * near * size + 4 :, :] = jnp.zeros((4, width), jnp.float32)
    bias_out[...] = bias_sum


def sum_blocks_kernel(fsdp_count, *refs):
    parts, outs = refs[:fsdp_count], refs[fsdp_count:]
    at = lax.axis_index("ctx")
    for k, out in enumerate(outs):
        rank = at ^ k
        block = parts[0][rank]
        for part in parts[1:]:
            block = block + part[rank].astype(jnp.float32)
        out[...] = block.astype(out.dtype)


def early_end_kernel(count, groups, qkv_cols, features, *refs):
    parts, (qkv_out, dense_out) = refs[:count], refs[count:]
    at = lax.rem(lax.axis_index("ctx"), groups)
    sums = []
    for g in range(groups):
        block = parts[g][...].astype(jnp.float32)
        for part in parts[g + groups :: groups]:
            block = block + part[...].astype(jnp.float32)
        sums.append(block)
    for g, block in enumerate(swapped(sums, at)):
        qkv_out[:, g * qkv_cols : (g + 1) * qkv_cols] = block[:, :qkv_cols]
        dense_out[:, g * features : (g + 1) * features] = block[:, qkv_cols:]


def late_end_kernel(count, ff, padded, *refs):
    parts, (up_out, down_out) = refs[:count], refs[count:]
    blocks = [part[...].astype(jnp.float32) for part in parts]
    for r, block in enumerate(swapped(blocks, lax.axis_index("ctx"))):
        up_out[:, r * ff : (r + 1) * ff] = block[:, :ff]
        down_out[:, r * ff : (r + 1) * ff] = block[:, padded : padded + ff]


def on_device(
    tokens,
    group_order,
    attn_gain,
    attn_shift,
    qkv_weight,
    qkv_bias,
    dense_weight,
    dense_bias,
    mlp_gain,
    mlp_shift,
    up_weight,
    up_bias,
    down_weight,
    down_bias,
    out_grad,
):
    bf16, f32 = jnp.bfloat16, jnp.float32
    seqs, length, width = tokens.shape
    fsdp_count, ctx_count, tp_count = (lax.axis_size(a) for a in ("fsdp", "ctx", "tp"))
    ctx_at, tp_at = lax.axis_index("ctx"), lax.axis_index("tp")
    rows_here = qkv_weight.shape[0]
    block_rows = ctx_count * rows_here
    heads = qkv_bias.shape[0] // (3 * HD)
    hidden_all = up_bias.shape[0]
    head_groups = math.gcd(heads, ctx_count)
    own_heads = heads // head_groups
    copies = ctx_count // head_groups // seqs
    features = own_heads * HD
    qkv_cols = 3 * features
    cols = qkv_cols + features
    ff = hidden_all // ctx_count
    padded = -(-ff // LANES) * LANES
    head_at = ctx_at % head_groups
    near = seqs // tp_count
    size = ctx_count * length
    near_rows = near * size

    early = local_kernel(
        functools.partial(early_message_kernel, head_groups, qkv_cols, features),
        [shaped((rows_here, cols), bf16)] * head_groups,
    )(qkv_weight, dense_weight.T)
    late = local_kernel(
        functools.partial(late_message_kernel, ctx_count, ff, padded),
        [shaped((rows_here, 2 * padded), bf16)] * ctx_count,
    )(up_weight, down_weight.T)
    early_rows = exchange([early[k % head_groups] for k in range(ctx_count)], "ctx")

    def near_part(array):
        parts = [array[j * near : (j + 1) * near] for j in range(tp_count)]
        return swapped(parts, tp_at)[0]

    own_tokens = near_part(tokens)
    own_grads = near_part(out_grad)
    message = jnp.stack([own_tokens, own_grads.astype(bf16)])
    late_rows = exchange(late, "ctx")
    chunks = gather_chunks(message[:, :, None], "ctx", 2)
    chunks = chunks.reshape(2, near, size, width)

    loose = rows_here % SUBLANES == 0

    def own_rows(parts):
        return jnp.concatenate(parts if loose else swapped(parts, ctx_at), axis=0)

    early_parts = spread(own_rows(early_rows), "fsdp")
    late_parts = spread(own_rows(late_rows), "fsdp")
    by_core = spread(chunks, "tp")

    position = jnp.concatenate(
        [
            positions(group_order, (ctx_at ^ k) * length, length)
            for k in gather_order(ctx_count)
        ]
    )
    cos_table, sin_table = rotary_tables(position)
    place = position.astype(f32)
    norms = jnp.stack([attn_gain, attn_shift, mlp_gain, mlp_shift])
    column_sums = jnp.sum(out_grad, axis=(0, 1))

    def row(vector):
        return vector.reshape(1, -1)

    qkv_parts = [qkv_bias[g * qkv_cols : (g + 1) * qkv_cols] for g in range(head_groups)]
    qkv_own = jnp.pad(swapped(qkv_parts, head_at)[0], (0, features))
    up_parts = [up_bias[r * ff : (r + 1) * ff] for r in range(ctx_count)]
    up_own = jnp.pad(swapped(up_parts, ctx_at)[0], (0, padded - ff))

    def grad_blocks(columns):
        return [
            shaped((block_rows, columns), bf16 if k else f32) for k in range(fsdp_count)
        ]

    row_blocks = ctx_count if loose else 1
    attn_branch, attn_norm, attn_sums, qkv_bias_part, *early_grads = local_kernel(
        functools.partial(
            attention_kernel,
            fsdp_count,
            tp_count,
            near,
            head_groups,
            own_heads,
            copies,
            seqs,
            row_blocks,
        ),
        [shaped((size, width), f32)] * 2
        + [shaped((2, width), f32), shaped((1, cols), f32)]
        + grad_blocks(cols),
        [
            pltpu.VMEM((width, cols), bf16),
            pltpu.VMEM((size, cols), f32),
            pltpu.VMEM((size, cols), bf16),
            pltpu.VMEM((width, cols), f32),
        ],
        flops=16 * size * width * cols,
        moved=16 * size * width,
    )(
        *by_core,
        *early_parts,
        norms,
        row(qkv_own),
        cos_table,
        sin_table,
        place.reshape(-1, 1),
        row(place),
    )
    outs = local_kernel(
        functools.partial(
            mlp_kernel, fsdp_count, tp_count, near, head_groups, seqs, padded, row_blocks
        ),
        [shaped((2 * near_rows + 8, width), f32)] * tp_count
        + [shaped((1, padded), f32)]
        + grad_blocks(2 * padded),
        [pltpu.VMEM((width, 2 * padded), bf16), pltpu.VMEM((width, 2 * padded), f32)],
        flops=12 * seqs * size * width * padded,
        moved=32 * size * width,
    )(
        *by_core,
        *late_parts,
        norms,
        row(up_own),
        attn_branch,
        attn_norm,
        attn_sums,
    )
    row_parts, up_bias_part = outs[:tp_count], outs[tp_count]
    late_grads = outs[tp_count + 1 :]
    row_sums = sum(exchange(row_parts, "tp"))
    gain_parts = row_sums[2 * near_rows : 2 * near_rows + 4].reshape(-1)
    row_sums = row_sums[: 2 * near_rows].reshape(2, near, ctx_count, length, width)
    row_sums = scatter_chunks(row_sums, "ctx", 2).reshape(2, near, length, width)
    branches, inner = row_sums[0], row_sums[1]

    def both_cores(half):
        return jnp.concatenate(swapped(spread(half, "tp"), tp_at), axis=0)

    def scatter_weights(parts):
        columns = parts[0].shape[1]
        received = [part.reshape(ctx_count, rows_here, columns) for part in exchange(parts, "fsdp")]
        pieces = local_kernel(
            functools.partial(sum_blocks_kernel, fsdp_count),
            [shaped((rows_here, columns), bf16 if k else f32) for k in range(ctx_count)],
        )(*received)
        return exchange(pieces, "ctx")

    early_pieces = scatter_weights(early_grads)
    late_pieces = scatter_weights(late_grads)
    block_half = own_tokens.astype(f32) + branches + (dense_bias + down_bias)
    block_out = both_cores(block_half.astype(bf16))
    own_centred, own_inverse = normed_rows(own_tokens.astype(f32))
    inner = (
        inner
        - jnp.mean(inner, axis=-1, keepdims=True)
        - own_centred * jnp.mean(inner * own_centred, axis=-1, keepdims=True)
    )
    tokens_grad = both_cores(own_grads + own_inverse * inner)
    qkv_weight_grad, dense_weight_grad = local_kernel(
        functools.partial(early_end_kernel, ctx_count, head_groups, qkv_cols, features),
        [shaped(qkv_weight.shape, f32), shaped(dense_weight.shape[::-1], f32)],
    )(*early_pieces)
    up_weight_grad, down_weight_grad = local_kernel(
        functools.partial(late_end_kernel, ctx_count, ff, padded),
        [shaped(up_weight.shape, f32), shaped(down_weight.shape[::-1], f32)],
    )(*late_pieces)

    bias_parts = jnp.concatenate(
        [
            column_sums,
            one_hot_slots(qkv_bias_part[0, :qkv_cols], head_at, head_groups),
            one_hot_slots(up_bias_part[0, :ff], ctx_at, ctx_count),
        ]
    )
    small = jnp.concatenate([gain_parts, bias_parts])
    small = butterfly(butterfly(small, "fsdp"), "ctx")
    cuts = []
    start = 0
    for extent in [width] * 5 + [3 * HD * heads, hidden_all]:
        cuts.append(small[start : start + extent])
        start += extent
    return (
        block_out,
        tokens_grad,
        cuts[0],
        cuts[1],
        qkv_weight_grad,
        cuts[5],
        dense_weight_grad.T,
        cuts[4],
        cuts[2],
        cuts[3],
        up_weight_grad,
        cuts[6],
        down_weight_grad.T,
        cuts[4],
    )


def solution(mesh):
    in_specs = (
        P("fsdp", "ctx", None),
        P(),
        P(),
        P(),
        P(("fsdp", "ctx"), "tp"),
        P("tp"),
        P("tp", ("fsdp", "ctx")),
        P(),
        P(),
        P(),
        P(("fsdp", "ctx"), "tp"),
        P("tp"),
        P("tp", ("fsdp", "ctx")),
        P(),
        P("fsdp", "ctx", None),
    )
    out_specs = (
        P("fsdp", "ctx", None),
        P("fsdp", "ctx", None),
        P(),
        P(),
        P(("fsdp", "ctx"), "tp"),
        P("tp"),
        P("tp", ("fsdp", "ctx")),
        P(),
        P(),
        P(),
        P(("fsdp", "ctx"), "tp"),
        P("tp"),
        P("tp", ("fsdp", "ctx")),
        P(),
    )

    return jax.shard_map(
        on_device, mesh=mesh, in_specs=in_specs, out_specs=out_specs, check_vma=False
    )
```

```python
import functools
import math

import jax
import jax.numpy as jnp
from jax import lax
from jax.experimental import pallas as pl
from jax.experimental.pallas import tpu as pltpu
from jax.sharding import PartitionSpec as P


HD = 64
ROT = 16
BLK = 32


EPSILON = 1e-05
NEGATIVE = -1e30
ROOT_HALF = 0.7071067811865476
INV_ROOT_TWO_PI = 0.3989422804014327
CONTRACT_LAST = (((1,), (1,)), ((), ()))
CONTRACT_FIRST = (((0,), (0,)), ((), ()))


def positions(order, start, count):
    index = start + jnp.arange(count, dtype=jnp.int32)
    slot = index // BLK
    table = jnp.arange(order.shape[0], dtype=jnp.int32)
    first = jnp.sum(jnp.where(slot[:, None] == table[None, :], order[None, :], 0), axis=1)
    return first * BLK + index % BLK


def swapped(parts, index):
    bit = 1
    while bit < len(parts):
        is_set = (index & bit) != 0
        parts = [jnp.where(is_set, parts[j ^ bit], parts[j]) for j in range(len(parts))]
        bit *= 2
    return parts


def swap(value, axis, bit):
    return lax.ppermute(value, axis, [(i, i ^ bit) for i in range(lax.axis_size(axis))])


def exchange(parts, axis):
    return [parts[0]] + [swap(parts[k], axis, k) for k in range(1, len(parts))]


def spread(value, axis):
    return exchange([value] * lax.axis_size(axis), axis)


def gather_order(count):
    order, bit = [0], count // 2
    while bit:
        order = order + [k ^ bit for k in order]
        bit //= 2
    return order


def gather_chunks(value, axis, dim):
    bit = lax.axis_size(axis) // 2
    while bit:
        other = swap(value, axis, bit)
        value = jnp.concatenate([value, other], axis=dim)
        bit //= 2
    return value


def scatter_chunks(value, axis, dim):
    count = lax.axis_size(axis)
    bit = 1
    while bit < count:
        kept, sent = jnp.split(value, 2, axis=dim)
        other = swap(sent.astype(jnp.bfloat16), axis, bit)
        value = kept + other.astype(jnp.float32)
        bit *= 2
    return value


def dot(left, right):
    return jnp.dot(left, right, preferred_element_type=jnp.float32)


def dot_last(left, right):
    return lax.dot_general(left, right, CONTRACT_LAST, preferred_element_type=jnp.float32)


def dot_first(left, right):
    return lax.dot_general(left, right, CONTRACT_FIRST, preferred_element_type=jnp.float32)


def normed_rows(rows):
    middle = jnp.mean(rows, axis=-1, keepdims=True)
    centred = rows - middle
    inverse = lax.rsqrt(jnp.mean(centred * centred, axis=-1, keepdims=True) + EPSILON)
    return centred * inverse, inverse


VMEM_LIMIT = 60 * 1024 * 1024
LANES = 128
SUBLANES = 16


def local_kernel(body, out_shapes, scratch=(), flops=0, moved=0):
    in_vmem = pl.BlockSpec(memory_space=pltpu.VMEM)
    return pl.pallas_call(
        body,
        out_shape=out_shapes,
        out_specs=jax.tree.map(lambda _: in_vmem, out_shapes),
        scratch_shapes=list(scratch),
        compiler_params=pltpu.CompilerParams(vmem_limit_bytes=VMEM_LIMIT),
        cost_estimate=pl.CostEstimate(flops=flops, bytes_accessed=moved, transcendentals=0),
    )


def shaped(shape, kind):
    return jax.ShapeDtypeStruct(tuple(shape), kind)


def rotary_tables(position):
    lane = jnp.arange(LANES, dtype=jnp.int32) % HD
    half = ROT // 2
    frequency = 1.0 / 10000.0 ** ((lane % half).astype(jnp.float32) * (2.0 / ROT))
    phase = position * jnp.where(lane < ROT, frequency, 0.0)[None, :]
    return jnp.cos(phase), jnp.where(lane < half, -1.0, 1.0)[None, :] * jnp.sin(phase)


def tiled(vector):
    return vector.reshape(-1, LANES)


def row_of(ref):
    return jnp.concatenate([ref[i : i + 1, :] for i in range(ref.shape[0])], axis=1)


def put_row(ref, value):
    for i in range(ref.shape[0]):
        ref[i : i + 1, :] = value[:, i * LANES : (i + 1) * LANES]


def tree_sum(parts):
    while len(parts) > 1:
        parts = [parts[i] + parts[i + 1] for i in range(0, len(parts), 2)]
    return parts[0]


def folded(value, columns):
    return [value[:, i : i + columns] for i in range(0, value.shape[1], columns)]


def early_message_kernel(groups, qkv_cols, features, qkv_ref, dense_ref, *outs):
    at = lax.rem(lax.axis_index("ctx"), groups)
    dense_t = dense_ref[...]
    parts = [
        jnp.concatenate(
            [
                qkv_ref[:, g * qkv_cols : (g + 1) * qkv_cols],
                dense_t[:, g * features : (g + 1) * features],
            ],
            axis=1,
        )
        for g in range(groups)
    ]
    for out, part in zip(outs, swapped(parts, at)):
        out[...] = part


def late_message_kernel(count, ff, padded, up_ref, down_ref, *outs):
    at = lax.axis_index("ctx")
    down_t = down_ref[...]
    rows = up_ref.shape[0]
    gap = [jnp.zeros((rows, padded - ff), jnp.bfloat16)] if padded > ff else []
    parts = [
        jnp.concatenate(
            [up_ref[:, r * ff : (r + 1) * ff]] + gap + [down_t[:, r * ff : (r + 1) * ff]] + gap,
            axis=1,
        )
        for r in range(count)
    ]
    for out, part in zip(outs, swapped(parts, at)):
        out[...] = part


def place_weight(parts, weight, count):
    fsdp_at, ctx_at = lax.axis_index("fsdp"), lax.axis_index("ctx")
    rows = parts[0].shape[0] // count
    for k, part in enumerate(parts):
        for j in range(count):
            place = (fsdp_at ^ k) * count + ((ctx_at ^ j) if count > 1 else 0)
            weight[pl.ds(pl.multiple_of(place * rows, SUBLANES), rows), :] = part[
                j * rows : (j + 1) * rows, :
            ]


def send_blocks(total, outs, block, extra=()):
    at = lax.axis_index("fsdp")
    for k, out in enumerate(outs):
        start = pl.multiple_of((at ^ k) * block, SUBLANES)
        out[:block, :] = total[pl.ds(start, block), :].astype(out.dtype)
        for i, row in enumerate(extra):
            out[block + i : block + i + 1, :] = row.astype(out.dtype)
        rest = out.shape[0] - block - len(extra)
        if rest:
            out[block + len(extra) :, :] = jnp.zeros((rest, out.shape[1]), out.dtype)


def attention_kernel(
    fsdp_count,
    core_count,
    near,
    head_groups,
    own_heads,
    copies,
    seqs,
    row_blocks,
    *refs,
):
    row_refs = refs[:core_count]
    parts = refs[core_count : core_count + fsdp_count]
    (gain_ref, shift_ref, bias_ref, cos_ref, sin_ref, pos_col, pos_row) = refs[
        core_count + fsdp_count : core_count + fsdp_count + 7
    ]
    gain, shift = row_of(gain_ref), row_of(shift_ref)
    outs = refs[core_count + fsdp_count + 7 :]
    branch, norm_out, sums, bias_out = outs[:4]
    grad_outs = outs[4 : 4 + fsdp_count]
    weight, grads, mixed, total = outs[4 + fsdp_count :]
    cols = weight.shape[1]
    features = own_heads * HD
    qkv_cols = 3 * features
    low_cols = qkv_cols // LANES * LANES
    high_cols = -(-qkv_cols // LANES) * LANES
    scale = 1.0 / math.sqrt(HD)
    ctx_at = lax.axis_index("ctx")
    seq_at = lax.rem(lax.div(ctx_at, head_groups), seqs)
    core = lax.div(seq_at, near) ^ lax.axis_index("tp")
    inner = lax.rem(seq_at, near)
    place_weight(parts, weight, row_blocks)
    seq_tokens, seq_grads = row_refs[0][0, inner], row_refs[0][1, inner]
    for j in range(1, core_count):
        seq_tokens = jnp.where(core == j, row_refs[j][0, inner], seq_tokens)
        seq_grads = jnp.where(core == j, row_refs[j][1, inner], seq_grads)
    centred, _ = normed_rows(seq_tokens.astype(jnp.float32))
    attn_in = (centred * gain + shift).astype(jnp.bfloat16)
    bias_all = row_of(bias_ref)
    biases = [bias_all[:, g * qkv_cols : (g + 1) * qkv_cols] for g in range(head_groups)]
    bias = swapped(biases, lax.rem(ctx_at, head_groups))[0]
    if high_cols > qkv_cols:
        bias = jnp.concatenate([bias, jnp.zeros((1, high_cols - qkv_cols), jnp.float32)], axis=1)
    lane = lax.broadcasted_iota(jnp.int32, (1, high_cols), 1)
    rotated = (lane < qkv_cols) & (lane % (3 * HD) < 2 * HD)
    first = lane % HD < ROT // 2
    repeat = high_cols // LANES
    cos_all = jnp.where(rotated, jnp.concatenate([cos_ref[...]] * repeat, axis=1), 1.0)
    sin_all = jnp.where(rotated, jnp.concatenate([sin_ref[...]] * repeat, axis=1), 0.0)

    def turn(values, sine):
        ahead = pltpu.roll(values, high_cols - ROT // 2, 1)
        behind = pltpu.roll(values, ROT // 2, 1)
        return values * cos_all + jnp.where(first, ahead, behind) * sine

    projected = dot(attn_in, weight[:, :high_cols]) + bias
    turned = turn(projected, sin_all).astype(jnp.bfloat16)
    ctx_low = dot(seq_grads, weight[:, low_cols:]).astype(jnp.bfloat16)
    allowed = pos_row[...] <= pos_col[...]
    keep = None
    if copies > 1:
        keep = lax.div(ctx_at, head_groups * seqs) == 0
    grads[...] = jnp.zeros(grads.shape, jnp.float32)
    mixed[...] = jnp.zeros(mixed.shape, jnp.bfloat16)
    for head in range(own_heads):
        at = head * 3 * HD
        query = turned[:, at : at + HD]
        key = turned[:, at + HD : at + 2 * HD]
        value = turned[:, at + 2 * HD : at + 3 * HD]
        spot = qkv_cols - low_cols + head * HD
        low = ctx_low[:, spot : spot + HD]
        scores = jnp.where(allowed, dot_last(query, key) * scale, NEGATIVE)
        peak = jnp.max(scores, axis=-1, keepdims=True)
        weights = jnp.where(allowed, jnp.exp(scores - peak), 0.0)
        probs = weights / jnp.sum(weights, axis=-1, keepdims=True)
        probs_low = probs.astype(jnp.bfloat16)
        attended = dot(probs_low, value)
        delta = jnp.sum(low.astype(jnp.float32) * attended, axis=-1, keepdims=True)
        score_grad = probs * (dot_last(low, value) - delta)
        if copies > 1:
            score_grad = jnp.where(keep, score_grad, 0.0)
            probs_low = jnp.where(keep, probs_low, jnp.zeros_like(probs_low))
            attended = jnp.where(keep, attended, 0.0)
        score_low = score_grad.astype(jnp.bfloat16)
        grads[:, at : at + HD] = dot(score_low, key) * scale
        grads[:, at + HD : at + 2 * HD] = dot_first(score_low, query) * scale
        grads[:, at + 2 * HD : at + 3 * HD] = dot_first(probs_low, low)
        mixed[:, spot : spot + HD] = attended.astype(jnp.bfloat16)
    proj_grad = turn(grads[...], -sin_all)
    proj_low = proj_grad.astype(jnp.bfloat16)
    total[:, :high_cols] = dot_first(attn_in, proj_low)
    if cols > high_cols:
        total[:, high_cols:] = jnp.zeros((weight.shape[0], cols - high_cols), jnp.float32)
    total[:, low_cols:] += dot_first(seq_grads, mixed[...])
    send_blocks(total, grad_outs, grad_outs[0].shape[0])
    branch[...] = dot_last(mixed[...], weight[:, low_cols:])
    norm_grad = dot_last(proj_low, weight[:, :high_cols])
    norm_out[...] = norm_grad * gain
    sums[...] = jnp.concatenate(
        [
            jnp.sum(norm_grad * centred, axis=0, keepdims=True),
            jnp.sum(norm_grad, axis=0, keepdims=True),
        ],
        axis=0,
    )
    bias_out[:, :high_cols] = jnp.sum(proj_grad, axis=0, keepdims=True)
    if cols > high_cols:
        bias_out[:, high_cols:] = jnp.zeros((1, cols - high_cols), jnp.float32)


def mlp_kernel(fsdp_count, core_count, near, head_groups, seqs, ff, row_blocks, *refs):
    row_refs = refs[:core_count]
    parts = refs[core_count : core_count + fsdp_count]
    (
        gain_ref,
        shift_ref,
        bias_ref,
        columns_ref,
        attn_branch,
        attn_norm,
        attn_sums,
        attn_bias,
    ) = refs[core_count + fsdp_count : core_count + fsdp_count + 8]
    outs = refs[core_count + fsdp_count + 8 :]
    both = outs[:core_count]
    grad_outs = outs[core_count : core_count + fsdp_count]
    weight, total = outs[core_count + fsdp_count :]
    gain, shift = row_of(gain_ref), row_of(shift_ref)
    size, width = attn_branch.shape
    both_cols = weight.shape[1]
    padded = both_cols // 2
    ctx_at = lax.axis_index("ctx")
    bias_all = row_of(bias_ref)
    count = bias_all.shape[1] // ff
    bias = swapped([bias_all[:, r * ff : (r + 1) * ff] for r in range(count)], ctx_at)[0]
    if padded > ff:
        bias = jnp.concatenate([bias, jnp.zeros((1, padded - ff), jnp.float32)], axis=1)
    seq_at = lax.rem(lax.div(ctx_at, head_groups), seqs)
    core = lax.div(seq_at, near) ^ lax.axis_index("tp")
    inner = lax.rem(seq_at, near)
    place_weight(parts, weight, row_blocks)
    up, down = weight[:, :padded], weight[:, padded:]
    rows = jnp.concatenate([ref[0].reshape(near * size, width) for ref in row_refs], axis=0)
    grad_rows = jnp.concatenate([ref[1].reshape(near * size, width) for ref in row_refs], axis=0)
    centred, _ = normed_rows(rows.astype(jnp.float32))
    mlp_in = (centred * gain + shift).astype(jnp.bfloat16)
    pre_act = dot(mlp_in, up) + bias
    normal = 0.5 * (1.0 + lax.erf(pre_act * ROOT_HALF))
    hidden = (pre_act * normal).astype(jnp.bfloat16)
    slope = normal + pre_act * jnp.exp(-0.5 * pre_act * pre_act) * INV_ROOT_TWO_PI
    pre_grad = dot(grad_rows, down) * slope
    pre_low = pre_grad.astype(jnp.bfloat16)
    total[:, :padded] = dot_first(mlp_in, pre_low)
    total[:, padded:] = dot_first(grad_rows, hidden)
    norm_grad = dot_last(pre_low, up)
    bias_sum = jnp.concatenate(
        [jnp.sum(pre_grad, axis=0, keepdims=True), jnp.zeros((1, padded), jnp.float32)], axis=1
    )
    vectors = [
        attn_sums[0:1, :],
        attn_sums[1:2, :],
        jnp.sum(norm_grad * centred, axis=0, keepdims=True),
        jnp.sum(norm_grad, axis=0, keepdims=True),
        row_of(columns_ref),
        attn_bias[...],
    ]
    extra = [piece for vector in vectors for piece in folded(vector, both_cols)] + [bias_sum]
    send_blocks(total, grad_outs, width // fsdp_count, extra)
    norm_grad = norm_grad * gain
    branch = dot_last(hidden, down)
    for j in range(core_count):
        for i in range(near):
            here = (core == j) & (inner == i)
            at = (j * near + i) * size
            out = both[j]
            out[0, i] = branch[at : at + size] + jnp.where(here, attn_branch[...], 0.0)
            out[1, i] = norm_grad[at : at + size] + jnp.where(here, attn_norm[...], 0.0)


def sum_blocks_kernel(fsdp_count, ctx_count, rows_here, *refs):
    parts, outs = refs[:fsdp_count], refs[fsdp_count:]
    block = ctx_count * rows_here
    total = parts[0][:block, :]
    for part in parts[1:]:
        total = total + part[:block, :].astype(jnp.float32)
    pieces = [total[r * rows_here : (r + 1) * rows_here] for r in range(ctx_count)]
    for out, piece in zip(outs, swapped(pieces, lax.axis_index("ctx"))):
        out[:rows_here, :] = piece.astype(out.dtype)
    if outs[0].shape[0] > rows_here:
        vectors = tree_sum(
            [part[block:, :].astype(jnp.bfloat16).astype(jnp.float32) for part in parts]
        ).astype(jnp.bfloat16)
        for out in outs:
            out[rows_here:, :] = vectors.astype(out.dtype)


def early_end_kernel(count, groups, qkv_cols, features, *refs):
    parts, (qkv_out, dense_out) = refs[:count], refs[count:]
    at = lax.rem(lax.axis_index("ctx"), groups)
    sums = []
    for g in range(groups):
        sums.append(tree_sum([part[...].astype(jnp.float32) for part in parts[g::groups]]))
    for g, block in enumerate(swapped(sums, at)):
        qkv_out[:, g * qkv_cols : (g + 1) * qkv_cols] = block[:, :qkv_cols]
        dense_out[:, g * features : (g + 1) * features] = block[:, qkv_cols:]


def late_end_kernel(count, groups, ff, padded, qkv_cols, cols, *refs):
    parts, outs = refs[:count], refs[count:]
    up_out, down_out, gains_out, columns_out, qkv_bias_out, up_bias_out = outs
    rows, width = up_out.shape[0], LANES * columns_out.shape[0]
    both_cols = 2 * padded
    ctx_at = lax.axis_index("ctx")
    blocks = [part[:rows, :].astype(jnp.float32) for part in parts]
    for r, block in enumerate(swapped(blocks, ctx_at)):
        up_out[:, r * ff : (r + 1) * ff] = block[:, :ff]
        down_out[:, r * ff : (r + 1) * ff] = block[:, padded : padded + ff]
    vectors = [part[rows:, :].astype(jnp.float32) for part in parts]

    def unfolded(block, start, extent):
        n = extent // both_cols
        return jnp.concatenate([block[start + i : start + i + 1] for i in range(n)], axis=1)

    summed = tree_sum(vectors)
    step = width // both_cols
    gains = jnp.concatenate([unfolded(summed, i * step, width) for i in range(4)], axis=1)
    put_row(gains_out, gains)
    put_row(columns_out, unfolded(summed, 4 * step, width))
    sums = [tree_sum(vectors[g::groups]) for g in range(groups)]
    sums = [unfolded(block, 5 * step, cols)[:, :qkv_cols] for block in sums]
    put_row(
        qkv_bias_out, jnp.concatenate(swapped(sums, lax.rem(ctx_at, groups)), axis=1)
    )
    last = 5 * step + cols // both_cols
    ups = [block[last : last + 1, :ff] for block in vectors]
    put_row(up_bias_out, jnp.concatenate(swapped(ups, ctx_at), axis=1))


def on_device(
    tokens,
    group_order,
    attn_gain,
    attn_shift,
    qkv_weight,
    qkv_bias,
    dense_weight,
    dense_bias,
    mlp_gain,
    mlp_shift,
    up_weight,
    up_bias,
    down_weight,
    down_bias,
    out_grad,
):
    bf16, f32 = jnp.bfloat16, jnp.float32
    seqs, length, width = tokens.shape
    fsdp_count, ctx_count, tp_count = (lax.axis_size(a) for a in ("fsdp", "ctx", "tp"))
    ctx_at, tp_at = lax.axis_index("ctx"), lax.axis_index("tp")
    rows_here = qkv_weight.shape[0]
    block_rows = ctx_count * rows_here
    heads = qkv_bias.shape[0] // (3 * HD)
    hidden_all = up_bias.shape[0]
    head_groups = math.gcd(heads, ctx_count)
    own_heads = heads // head_groups
    copies = ctx_count // head_groups // seqs
    features = own_heads * HD
    qkv_cols = 3 * features
    cols = qkv_cols + features
    low_cols = qkv_cols // LANES * LANES
    high_cols = -(-qkv_cols // LANES) * LANES
    ff = hidden_all // ctx_count
    padded = -(-ff // LANES) * LANES
    near = seqs // tp_count
    size = ctx_count * length

    early = local_kernel(
        functools.partial(early_message_kernel, head_groups, qkv_cols, features),
        [shaped((rows_here, cols), bf16)] * head_groups,
    )(qkv_weight, dense_weight.T)
    late = local_kernel(
        functools.partial(late_message_kernel, ctx_count, ff, padded),
        [shaped((rows_here, 2 * padded), bf16)] * ctx_count,
    )(up_weight, down_weight.T)
    early_rows = exchange([early[k % head_groups] for k in range(ctx_count)], "ctx")

    def near_part(array):
        parts = [array[j * near : (j + 1) * near] for j in range(tp_count)]
        return swapped(parts, tp_at)[0]

    own_tokens = near_part(tokens)
    own_grads = near_part(out_grad)
    message = jnp.stack([own_tokens, own_grads.astype(bf16)])
    late_rows = exchange(late, "ctx")
    chunks = gather_chunks(message[:, :, None], "ctx", 2)
    chunks = chunks.reshape(2, near, size, width)

    loose = rows_here % SUBLANES == 0

    def own_rows(parts):
        return jnp.concatenate(parts if loose else swapped(parts, ctx_at), axis=0)

    early_parts = spread(own_rows(early_rows), "fsdp")
    late_parts = spread(own_rows(late_rows), "fsdp")
    by_core = spread(chunks, "tp")

    position = jnp.concatenate(
        [
            positions(group_order, (ctx_at ^ k) * length, length)
            for k in gather_order(ctx_count)
        ]
    ).astype(f32)
    cos_table, sin_table = rotary_tables(position[:, None])
    column_sums = jnp.sum(out_grad, axis=(0, 1))

    def grad_blocks(columns, extra=0):
        return [
            shaped((block_rows + extra, columns), bf16 if k else f32) for k in range(fsdp_count)
        ]

    vector_rows = (5 * width + cols) // (2 * padded) + 1
    vector_rows = -(-vector_rows // SUBLANES) * SUBLANES

    row_blocks = ctx_count if loose else 1
    attn_branch, attn_norm, attn_sums, qkv_bias_part, *early_grads = local_kernel(
        functools.partial(
            attention_kernel,
            fsdp_count,
            tp_count,
            near,
            head_groups,
            own_heads,
            copies,
            seqs,
            row_blocks,
        ),
        [shaped((size, width), f32)] * 2
        + [shaped((2, width), f32), shaped((1, cols), f32)]
        + grad_blocks(cols),
        [
            pltpu.VMEM((width, cols), bf16),
            pltpu.VMEM((size, high_cols), f32),
            pltpu.VMEM((size, cols - low_cols), bf16),
            pltpu.VMEM((width, cols), f32),
        ],
        flops=16 * size * width * cols,
        moved=16 * size * width,
    )(
        *by_core,
        *early_parts,
        tiled(attn_gain),
        tiled(attn_shift),
        tiled(qkv_bias),
        cos_table,
        sin_table,
        position.reshape(-1, 1),
        position.reshape(1, -1),
    )
    outs = local_kernel(
        functools.partial(
            mlp_kernel, fsdp_count, tp_count, near, head_groups, seqs, ff, row_blocks
        ),
        [shaped((2, near, size, width), f32)] * tp_count + grad_blocks(2 * padded, vector_rows),
        [pltpu.VMEM((width, 2 * padded), bf16), pltpu.VMEM((width, 2 * padded), f32)],
        flops=12 * seqs * size * width * padded,
        moved=32 * size * width,
    )(
        *by_core,
        *late_parts,
        tiled(mlp_gain),
        tiled(mlp_shift),
        tiled(up_bias),
        tiled(column_sums),
        attn_branch,
        attn_norm,
        attn_sums,
        qkv_bias_part,
    )
    row_parts, late_grads = outs[:tp_count], outs[tp_count:]
    row_sums = sum(exchange(row_parts, "tp"))
    row_sums = row_sums.reshape(2, near, ctx_count, length, width)
    row_sums = scatter_chunks(row_sums, "ctx", 2).reshape(2, near, length, width)
    branches, inner = row_sums[0], row_sums[1]

    def both_cores(half):
        halves = spread(half, "tp")
        return jnp.concatenate(swapped(halves, tp_at), axis=0)

    def scatter_weights(parts):
        columns = parts[0].shape[1]
        rows = parts[0].shape[0] - block_rows + rows_here
        pieces = local_kernel(
            functools.partial(sum_blocks_kernel, fsdp_count, ctx_count, rows_here),
            [shaped((rows, columns), bf16 if k else f32) for k in range(ctx_count)],
        )(*exchange(parts, "fsdp"))
        return exchange(pieces, "ctx")

    early_pieces = scatter_weights(early_grads)
    late_pieces = scatter_weights(late_grads)
    block_half = own_tokens.astype(f32) + branches + (dense_bias + down_bias)
    block_out = both_cores(block_half.astype(bf16))
    own_centred, own_inverse = normed_rows(own_tokens.astype(f32))
    inner = (
        inner
        - jnp.mean(inner, axis=-1, keepdims=True)
        - own_centred * jnp.mean(inner * own_centred, axis=-1, keepdims=True)
    )
    tokens_grad = both_cores(own_grads + own_inverse * inner)
    qkv_weight_grad, dense_weight_grad = local_kernel(
        functools.partial(early_end_kernel, ctx_count, head_groups, qkv_cols, features),
        [shaped(qkv_weight.shape, f32), shaped(dense_weight.shape[::-1], f32)],
    )(*early_pieces)
    up_weight_grad, down_weight_grad, gains, column_grad, qkv_bias_grad, up_bias_grad = (
        local_kernel(
            functools.partial(
                late_end_kernel, ctx_count, head_groups, ff, padded, qkv_cols, cols
            ),
            [
                shaped(up_weight.shape, f32),
                shaped(down_weight.shape[::-1], f32),
                shaped((4 * width // LANES, LANES), f32),
                shaped((width // LANES, LANES), f32),
                shaped((3 * HD * heads // LANES, LANES), f32),
                shaped((hidden_all // LANES, LANES), f32),
            ],
        )(*late_pieces)
    )
    gains = sum(spread(gains, "tp")).reshape(4, width)
    column_grad = column_grad.reshape(width)
    return (
        block_out,
        tokens_grad,
        gains[0],
        gains[1],
        qkv_weight_grad,
        qkv_bias_grad.reshape(3 * HD * heads),
        dense_weight_grad.T,
        column_grad,
        gains[2],
        gains[3],
        up_weight_grad,
        up_bias_grad.reshape(hidden_all),
        down_weight_grad.T,
        column_grad,
    )


def solution(mesh):
    in_specs = (
        P("fsdp", "ctx", None),
        P(),
        P(),
        P(),
        P(("fsdp", "ctx"), "tp"),
        P("tp"),
        P("tp", ("fsdp", "ctx")),
        P(),
        P(),
        P(),
        P(("fsdp", "ctx"), "tp"),
        P("tp"),
        P("tp", ("fsdp", "ctx")),
        P(),
        P("fsdp", "ctx", None),
    )
    out_specs = (
        P("fsdp", "ctx", None),
        P("fsdp", "ctx", None),
        P(),
        P(),
        P(("fsdp", "ctx"), "tp"),
        P("tp"),
        P("tp", ("fsdp", "ctx")),
        P(),
        P(),
        P(),
        P(("fsdp", "ctx"), "tp"),
        P("tp"),
        P("tp", ("fsdp", "ctx")),
        P(),
    )

    return jax.shard_map(
        on_device, mesh=mesh, in_specs=in_specs, out_specs=out_specs, check_vma=False
    )
```

```python
import functools
import math

import jax
import jax.numpy as jnp
from jax import lax
from jax.experimental import pallas as pl
from jax.experimental.pallas import tpu as pltpu
from jax.sharding import PartitionSpec as P


HD = 64
ROT = 16
BLK = 32


EPSILON = 1e-05
NEGATIVE = -1e30
ROOT_HALF = 0.7071067811865476
INV_ROOT_TWO_PI = 0.3989422804014327
CONTRACT_LAST = (((1,), (1,)), ((), ()))
CONTRACT_FIRST = (((0,), (0,)), ((), ()))


def positions(order, start, count):
    index = start + jnp.arange(count, dtype=jnp.int32)
    slot = index // BLK
    table = jnp.arange(order.shape[0], dtype=jnp.int32)
    first = jnp.sum(jnp.where(slot[:, None] == table[None, :], order[None, :], 0), axis=1)
    return first * BLK + index % BLK


def swapped(parts, index):
    bit = 1
    while bit < len(parts):
        is_set = (index & bit) != 0
        parts = [jnp.where(is_set, parts[j ^ bit], parts[j]) for j in range(len(parts))]
        bit *= 2
    return parts


def swap(value, axis, bit):
    return lax.ppermute(value, axis, [(i, i ^ bit) for i in range(lax.axis_size(axis))])


def exchange(parts, axis):
    return [parts[0]] + [swap(parts[k], axis, k) for k in range(1, len(parts))]


def spread(value, axis):
    return exchange([value] * lax.axis_size(axis), axis)


def gather_order(count):
    order, bit = [0], count // 2
    while bit:
        order = order + [k ^ bit for k in order]
        bit //= 2
    return order


def gather_chunks(value, axis, dim):
    bit = lax.axis_size(axis) // 2
    while bit:
        other = swap(value, axis, bit)
        value = jnp.concatenate([value, other], axis=dim)
        bit //= 2
    return value


def scatter_chunks(value, axis, dim):
    count = lax.axis_size(axis)
    bit = 1
    while bit < count:
        kept, sent = jnp.split(value, 2, axis=dim)
        other = swap(sent.astype(jnp.bfloat16), axis, bit)
        value = kept + other.astype(jnp.float32)
        bit *= 2
    return value


def dot(left, right):
    return jnp.dot(left, right, preferred_element_type=jnp.float32)


def dot_last(left, right):
    return lax.dot_general(left, right, CONTRACT_LAST, preferred_element_type=jnp.float32)


def dot_first(left, right):
    return lax.dot_general(left, right, CONTRACT_FIRST, preferred_element_type=jnp.float32)


def normed_rows(rows):
    middle = jnp.mean(rows, axis=-1, keepdims=True)
    centred = rows - middle
    inverse = lax.rsqrt(jnp.mean(centred * centred, axis=-1, keepdims=True) + EPSILON)
    return centred * inverse, inverse


VMEM_LIMIT = 60 * 1024 * 1024
LANES = 128
SUBLANES = 16
SCORES_AT_ONCE = 512 * 1024


def local_kernel(body, out_shapes, scratch=(), flops=0, moved=0):
    in_vmem = pl.BlockSpec(memory_space=pltpu.VMEM)
    return pl.pallas_call(
        body,
        out_shape=out_shapes,
        out_specs=jax.tree.map(lambda _: in_vmem, out_shapes),
        scratch_shapes=list(scratch),
        compiler_params=pltpu.CompilerParams(vmem_limit_bytes=VMEM_LIMIT),
        cost_estimate=pl.CostEstimate(flops=flops, bytes_accessed=moved, transcendentals=0),
    )


def shaped(shape, kind):
    return jax.ShapeDtypeStruct(tuple(shape), kind)


def rotary_tables(position):
    lane = jnp.arange(LANES, dtype=jnp.int32) % HD
    half = ROT // 2
    frequency = 1.0 / 10000.0 ** ((lane % half).astype(jnp.float32) * (2.0 / ROT))
    phase = position * jnp.where(lane < ROT, frequency, 0.0)[None, :]
    return jnp.cos(phase), jnp.where(lane < half, -1.0, 1.0)[None, :] * jnp.sin(phase)


def tiled(vector):
    return vector.reshape(-1, LANES)


def row_of(ref):
    return jnp.concatenate([ref[i : i + 1, :] for i in range(ref.shape[0])], axis=1)


def put_row(ref, value):
    for i in range(ref.shape[0]):
        ref[i : i + 1, :] = value[:, i * LANES : (i + 1) * LANES]


def tree_sum(parts):
    while len(parts) > 1:
        parts = [parts[i] + parts[i + 1] for i in range(0, len(parts), 2)]
    return parts[0]


def folded(value, columns):
    return [value[:, i : i + columns] for i in range(0, value.shape[1], columns)]


def early_message_kernel(groups, qkv_cols, features, qkv_ref, dense_ref, *outs):
    at = lax.rem(lax.axis_index("ctx"), groups)
    dense_t = dense_ref[...]
    parts = [
        jnp.concatenate(
            [
                qkv_ref[:, g * qkv_cols : (g + 1) * qkv_cols],
                dense_t[:, g * features : (g + 1) * features],
            ],
            axis=1,
        )
        for g in range(groups)
    ]
    for out, part in zip(outs, swapped(parts, at)):
        out[...] = part


def late_message_kernel(count, ff, padded, up_ref, down_ref, *outs):
    at = lax.axis_index("ctx")
    down_t = down_ref[...]
    rows = up_ref.shape[0]
    gap = [jnp.zeros((rows, padded - ff), jnp.bfloat16)] if padded > ff else []
    parts = [
        jnp.concatenate(
            [up_ref[:, r * ff : (r + 1) * ff]] + gap + [down_t[:, r * ff : (r + 1) * ff]] + gap,
            axis=1,
        )
        for r in range(count)
    ]
    for out, part in zip(outs, swapped(parts, at)):
        out[...] = part


def place_weight(parts, weight, count):
    fsdp_at, ctx_at = lax.axis_index("fsdp"), lax.axis_index("ctx")
    rows = parts[0].shape[0] // count
    for k, part in enumerate(parts):
        for j in range(count):
            place = (fsdp_at ^ k) * count + ((ctx_at ^ j) if count > 1 else 0)
            weight[pl.ds(pl.multiple_of(place * rows, SUBLANES), rows), :] = part[
                j * rows : (j + 1) * rows, :
            ]


def send_blocks(total, outs, block, extra=()):
    at = lax.axis_index("fsdp")
    for k, out in enumerate(outs):
        start = pl.multiple_of((at ^ k) * block, SUBLANES)
        out[:block, :] = total[pl.ds(start, block), :].astype(out.dtype)
        for i, row in enumerate(extra):
            out[block + i : block + i + 1, :] = row.astype(out.dtype)
        rest = out.shape[0] - block - len(extra)
        if rest:
            out[block + len(extra) :, :] = jnp.zeros((rest, out.shape[1]), out.dtype)


def attention_kernel(
    fsdp_count,
    core_count,
    near,
    head_groups,
    own_heads,
    copies,
    seqs,
    row_blocks,
    *refs,
):
    row_refs = refs[:core_count]
    parts = refs[core_count : core_count + fsdp_count]
    (gain_ref, shift_ref, bias_ref, cos_ref, sin_ref, pos_col, pos_row) = refs[
        core_count + fsdp_count : core_count + fsdp_count + 7
    ]
    gain, shift = row_of(gain_ref), row_of(shift_ref)
    outs = refs[core_count + fsdp_count + 7 :]
    branch, norm_out, sums, bias_out = outs[:4]
    grad_outs = outs[4 : 4 + fsdp_count]
    weight, grads, mixed, total = outs[4 + fsdp_count :]
    size = pos_col.shape[0]
    cols = weight.shape[1]
    features = own_heads * HD
    qkv_cols = 3 * features
    low_cols = qkv_cols // LANES * LANES
    high_cols = -(-qkv_cols // LANES) * LANES
    scale = 1.0 / math.sqrt(HD)
    ctx_at = lax.axis_index("ctx")
    seq_at = lax.rem(lax.div(ctx_at, head_groups), seqs)
    core = lax.div(seq_at, near) ^ lax.axis_index("tp")
    inner = lax.rem(seq_at, near)
    place_weight(parts, weight, row_blocks)
    seq_tokens, seq_grads = row_refs[0][0, inner], row_refs[0][1, inner]
    for j in range(1, core_count):
        seq_tokens = jnp.where(core == j, row_refs[j][0, inner], seq_tokens)
        seq_grads = jnp.where(core == j, row_refs[j][1, inner], seq_grads)
    centred, _ = normed_rows(seq_tokens.astype(jnp.float32))
    attn_in = (centred * gain + shift).astype(jnp.bfloat16)
    bias_all = row_of(bias_ref)
    biases = [bias_all[:, g * qkv_cols : (g + 1) * qkv_cols] for g in range(head_groups)]
    bias = swapped(biases, lax.rem(ctx_at, head_groups))[0]
    if high_cols > qkv_cols:
        bias = jnp.concatenate([bias, jnp.zeros((1, high_cols - qkv_cols), jnp.float32)], axis=1)
    lane = lax.broadcasted_iota(jnp.int32, (1, high_cols), 1)
    rotated = (lane < qkv_cols) & (lane % (3 * HD) < 2 * HD)
    first = lane % HD < ROT // 2
    repeat = high_cols // LANES
    cos_all = jnp.where(rotated, jnp.concatenate([cos_ref[...]] * repeat, axis=1), 1.0)
    sin_all = jnp.where(rotated, jnp.concatenate([sin_ref[...]] * repeat, axis=1), 0.0)

    def turn(values, sine):
        ahead = pltpu.roll(values, high_cols - ROT // 2, 1)
        behind = pltpu.roll(values, ROT // 2, 1)
        return values * cos_all + jnp.where(first, ahead, behind) * sine

    projected = dot(attn_in, weight[:, :high_cols]) + bias
    turned = turn(projected, sin_all).astype(jnp.bfloat16)
    ctx_low = dot(seq_grads, weight[:, low_cols:]).astype(jnp.bfloat16)
    allowed = pos_row[...] <= pos_col[...]
    keep = None
    if copies > 1:
        keep = lax.div(ctx_at, head_groups * seqs) == 0
    grads[...] = jnp.zeros(grads.shape, jnp.float32)
    mixed[...] = jnp.zeros(mixed.shape, jnp.bfloat16)
    together = own_heads if own_heads * size * size <= SCORES_AT_ONCE else 1
    for base in range(0, own_heads, together):
        group = range(base, min(base + together, own_heads))
        heads = range(len(group))
        starts = [head * 3 * HD for head in group]
        spots = [qkv_cols - low_cols + head * HD for head in group]
        queries = [turned[:, at : at + HD] for at in starts]
        keys = [turned[:, at + HD : at + 2 * HD] for at in starts]
        values = [turned[:, at + 2 * HD : at + 3 * HD] for at in starts]
        lows = [ctx_low[:, spot : spot + HD] for spot in spots]
        scores = [
            jnp.where(allowed, dot_last(queries[h], keys[h]) * scale, NEGATIVE) for h in heads
        ]
        weight_grads = [dot_last(lows[h], values[h]) for h in heads]
        peaks = [jnp.max(scores[h], axis=-1, keepdims=True) for h in heads]
        weights = [jnp.where(allowed, jnp.exp(scores[h] - peaks[h]), 0.0) for h in heads]
        probs = [weights[h] / jnp.sum(weights[h], axis=-1, keepdims=True) for h in heads]
        probs_low = [probs[h].astype(jnp.bfloat16) for h in heads]
        attended = [dot(probs_low[h], values[h]) for h in heads]
        deltas = [
            jnp.sum(lows[h].astype(jnp.float32) * attended[h], axis=-1, keepdims=True) for h in heads
        ]
        score_grads = [probs[h] * (weight_grads[h] - deltas[h]) for h in heads]
        if copies > 1:
            score_grads = [jnp.where(keep, part, 0.0) for part in score_grads]
            probs_low = [jnp.where(keep, part, jnp.zeros_like(part)) for part in probs_low]
            attended = [jnp.where(keep, part, 0.0) for part in attended]
        score_low = [part.astype(jnp.bfloat16) for part in score_grads]
        for h in heads:
            at, spot = starts[h], spots[h]
            grads[:, at : at + HD] = dot(score_low[h], keys[h]) * scale
            grads[:, at + HD : at + 2 * HD] = dot_first(score_low[h], queries[h]) * scale
            grads[:, at + 2 * HD : at + 3 * HD] = dot_first(probs_low[h], lows[h])
            mixed[:, spot : spot + HD] = attended[h].astype(jnp.bfloat16)
    proj_grad = turn(grads[...], -sin_all)
    proj_low = proj_grad.astype(jnp.bfloat16)
    total[:, :high_cols] = dot_first(attn_in, proj_low)
    if cols > high_cols:
        total[:, high_cols:] = jnp.zeros((weight.shape[0], cols - high_cols), jnp.float32)
    total[:, low_cols:] += dot_first(seq_grads, mixed[...])
    send_blocks(total, grad_outs, grad_outs[0].shape[0])
    branch[...] = dot_last(mixed[...], weight[:, low_cols:])
    norm_grad = dot_last(proj_low, weight[:, :high_cols])
    norm_out[...] = norm_grad * gain
    sums[...] = jnp.concatenate(
        [
            jnp.sum(norm_grad * centred, axis=0, keepdims=True),
            jnp.sum(norm_grad, axis=0, keepdims=True),
        ],
        axis=0,
    )
    bias_out[:, :high_cols] = jnp.sum(proj_grad, axis=0, keepdims=True)
    if cols > high_cols:
        bias_out[:, high_cols:] = jnp.zeros((1, cols - high_cols), jnp.float32)


def mlp_kernel(fsdp_count, core_count, near, head_groups, seqs, ff, row_blocks, *refs):
    row_refs = refs[:core_count]
    parts = refs[core_count : core_count + fsdp_count]
    (
        gain_ref,
        shift_ref,
        bias_ref,
        columns_ref,
        attn_branch,
        attn_norm,
        attn_sums,
        attn_bias,
    ) = refs[core_count + fsdp_count : core_count + fsdp_count + 8]
    outs = refs[core_count + fsdp_count + 8 :]
    both = outs[:core_count]
    grad_outs = outs[core_count : core_count + fsdp_count]
    weight, total = outs[core_count + fsdp_count :]
    gain, shift = row_of(gain_ref), row_of(shift_ref)
    size, width = attn_branch.shape
    both_cols = weight.shape[1]
    padded = both_cols // 2
    ctx_at = lax.axis_index("ctx")
    bias_all = row_of(bias_ref)
    count = bias_all.shape[1] // ff
    bias = swapped([bias_all[:, r * ff : (r + 1) * ff] for r in range(count)], ctx_at)[0]
    if padded > ff:
        bias = jnp.concatenate([bias, jnp.zeros((1, padded - ff), jnp.float32)], axis=1)
    seq_at = lax.rem(lax.div(ctx_at, head_groups), seqs)
    core = lax.div(seq_at, near) ^ lax.axis_index("tp")
    inner = lax.rem(seq_at, near)
    place_weight(parts, weight, row_blocks)
    up, down = weight[:, :padded], weight[:, padded:]
    rows = jnp.concatenate([ref[0].reshape(near * size, width) for ref in row_refs], axis=0)
    grad_rows = jnp.concatenate([ref[1].reshape(near * size, width) for ref in row_refs], axis=0)
    centred, _ = normed_rows(rows.astype(jnp.float32))
    mlp_in = (centred * gain + shift).astype(jnp.bfloat16)
    pre_act = dot(mlp_in, up) + bias
    normal = 0.5 * (1.0 + lax.erf(pre_act * ROOT_HALF))
    hidden = (pre_act * normal).astype(jnp.bfloat16)
    slope = normal + pre_act * jnp.exp(-0.5 * pre_act * pre_act) * INV_ROOT_TWO_PI
    pre_grad = dot(grad_rows, down) * slope
    pre_low = pre_grad.astype(jnp.bfloat16)
    total[:, :padded] = dot_first(mlp_in, pre_low)
    total[:, padded:] = dot_first(grad_rows, hidden)
    norm_grad = dot_last(pre_low, up)
    bias_sum = jnp.concatenate(
        [jnp.sum(pre_grad, axis=0, keepdims=True), jnp.zeros((1, padded), jnp.float32)], axis=1
    )
    vectors = [
        attn_sums[0:1, :],
        attn_sums[1:2, :],
        jnp.sum(norm_grad * centred, axis=0, keepdims=True),
        jnp.sum(norm_grad, axis=0, keepdims=True),
        row_of(columns_ref),
        attn_bias[...],
    ]
    extra = [piece for vector in vectors for piece in folded(vector, both_cols)] + [bias_sum]
    send_blocks(total, grad_outs, width // fsdp_count, extra)
    norm_grad = norm_grad * gain
    branch = dot_last(hidden, down)
    for j in range(core_count):
        for i in range(near):
            here = (core == j) & (inner == i)
            at = (j * near + i) * size
            out = both[j]
            out[0, i] = branch[at : at + size] + jnp.where(here, attn_branch[...], 0.0)
            out[1, i] = norm_grad[at : at + size] + jnp.where(here, attn_norm[...], 0.0)


def sum_blocks_kernel(fsdp_count, ctx_count, rows_here, *refs):
    parts, outs = refs[:fsdp_count], refs[fsdp_count:]
    block = ctx_count * rows_here
    total = parts[0][:block, :]
    for part in parts[1:]:
        total = total + part[:block, :].astype(jnp.float32)
    pieces = [total[r * rows_here : (r + 1) * rows_here] for r in range(ctx_count)]
    for out, piece in zip(outs, swapped(pieces, lax.axis_index("ctx"))):
        out[:rows_here, :] = piece.astype(out.dtype)
    if outs[0].shape[0] > rows_here:
        vectors = tree_sum(
            [part[block:, :].astype(jnp.bfloat16).astype(jnp.float32) for part in parts]
        ).astype(jnp.bfloat16)
        for out in outs:
            out[rows_here:, :] = vectors.astype(out.dtype)


def early_end_kernel(count, groups, qkv_cols, features, *refs):
    parts, (qkv_out, dense_out) = refs[:count], refs[count:]
    at = lax.rem(lax.axis_index("ctx"), groups)
    sums = []
    for g in range(groups):
        sums.append(tree_sum([part[...].astype(jnp.float32) for part in parts[g::groups]]))
    for g, block in enumerate(swapped(sums, at)):
        qkv_out[:, g * qkv_cols : (g + 1) * qkv_cols] = block[:, :qkv_cols]
        dense_out[:, g * features : (g + 1) * features] = block[:, qkv_cols:]


def late_end_kernel(count, groups, ff, padded, qkv_cols, cols, *refs):
    parts, outs = refs[:count], refs[count:]
    up_out, down_out, gains_out, columns_out, columns_again, qkv_bias_out, up_bias_out = outs
    rows, width = up_out.shape[0], LANES * columns_out.shape[0]
    both_cols = 2 * padded
    ctx_at = lax.axis_index("ctx")
    blocks = [part[:rows, :].astype(jnp.float32) for part in parts]
    for r, block in enumerate(swapped(blocks, ctx_at)):
        up_out[:, r * ff : (r + 1) * ff] = block[:, :ff]
        down_out[:, r * ff : (r + 1) * ff] = block[:, padded : padded + ff]
    vectors = [part[rows:, :].astype(jnp.float32) for part in parts]

    def unfolded(block, start, extent):
        n = extent // both_cols
        return jnp.concatenate([block[start + i : start + i + 1] for i in range(n)], axis=1)

    summed = tree_sum(vectors)
    step = width // both_cols
    gains = jnp.concatenate([unfolded(summed, i * step, width) for i in range(4)], axis=1)
    put_row(gains_out, gains)
    columns = unfolded(summed, 4 * step, width)
    put_row(columns_out, columns)
    put_row(columns_again, columns)
    sums = [tree_sum(vectors[g::groups]) for g in range(groups)]
    sums = [unfolded(block, 5 * step, cols)[:, :qkv_cols] for block in sums]
    put_row(
        qkv_bias_out, jnp.concatenate(swapped(sums, lax.rem(ctx_at, groups)), axis=1)
    )
    last = 5 * step + cols // both_cols
    ups = [block[last : last + 1, :ff] for block in vectors]
    put_row(up_bias_out, jnp.concatenate(swapped(ups, ctx_at), axis=1))


def gains_end_kernel(count, *refs):
    parts, outs = refs[:count], refs[count : count + 4]
    total = tree_sum([part[...] for part in parts])
    rows = total.shape[0] // 4
    for i, out in enumerate(outs):
        out[...] = total[i * rows : (i + 1) * rows]


def on_device(
    tokens,
    group_order,
    attn_gain,
    attn_shift,
    qkv_weight,
    qkv_bias,
    dense_weight,
    dense_bias,
    mlp_gain,
    mlp_shift,
    up_weight,
    up_bias,
    down_weight,
    down_bias,
    out_grad,
):
    bf16, f32 = jnp.bfloat16, jnp.float32
    seqs, length, width = tokens.shape
    fsdp_count, ctx_count, tp_count = (lax.axis_size(a) for a in ("fsdp", "ctx", "tp"))
    ctx_at, tp_at = lax.axis_index("ctx"), lax.axis_index("tp")
    rows_here = qkv_weight.shape[0]
    block_rows = ctx_count * rows_here
    heads = qkv_bias.shape[0] // (3 * HD)
    hidden_all = up_bias.shape[0]
    head_groups = math.gcd(heads, ctx_count)
    own_heads = heads // head_groups
    copies = ctx_count // head_groups // seqs
    features = own_heads * HD
    qkv_cols = 3 * features
    cols = qkv_cols + features
    low_cols = qkv_cols // LANES * LANES
    high_cols = -(-qkv_cols // LANES) * LANES
    ff = hidden_all // ctx_count
    padded = -(-ff // LANES) * LANES
    near = seqs // tp_count
    size = ctx_count * length

    early = local_kernel(
        functools.partial(early_message_kernel, head_groups, qkv_cols, features),
        [shaped((rows_here, cols), bf16)] * head_groups,
    )(qkv_weight, dense_weight.T)
    late = local_kernel(
        functools.partial(late_message_kernel, ctx_count, ff, padded),
        [shaped((rows_here, 2 * padded), bf16)] * ctx_count,
    )(up_weight, down_weight.T)
    early_rows = exchange([early[k % head_groups] for k in range(ctx_count)], "ctx")

    def near_part(array):
        parts = [array[j * near : (j + 1) * near] for j in range(tp_count)]
        return swapped(parts, tp_at)[0]

    own_tokens = near_part(tokens)
    own_grads = near_part(out_grad)
    message = jnp.stack([own_tokens, own_grads.astype(bf16)])
    late_rows = exchange(late, "ctx")
    chunks = gather_chunks(message[:, :, None], "ctx", 2)
    chunks = chunks.reshape(2, near, size, width)

    loose = rows_here % SUBLANES == 0

    def own_rows(parts):
        return jnp.concatenate(parts if loose else swapped(parts, ctx_at), axis=0)

    early_parts = spread(own_rows(early_rows), "fsdp")
    late_parts = spread(own_rows(late_rows), "fsdp")
    by_core = spread(chunks, "tp")

    position = jnp.concatenate(
        [
            positions(group_order, (ctx_at ^ k) * length, length)
            for k in gather_order(ctx_count)
        ]
    ).astype(f32)
    cos_table, sin_table = rotary_tables(position[:, None])
    column_sums = jnp.sum(out_grad, axis=(0, 1))

    def grad_blocks(columns, extra=0):
        return [
            shaped((block_rows + extra, columns), bf16 if k else f32) for k in range(fsdp_count)
        ]

    vector_rows = (5 * width + cols) // (2 * padded) + 1
    vector_rows = -(-vector_rows // SUBLANES) * SUBLANES

    row_blocks = ctx_count if loose else 1
    attn_branch, attn_norm, attn_sums, qkv_bias_part, *early_grads = local_kernel(
        functools.partial(
            attention_kernel,
            fsdp_count,
            tp_count,
            near,
            head_groups,
            own_heads,
            copies,
            seqs,
            row_blocks,
        ),
        [shaped((size, width), f32)] * 2
        + [shaped((2, width), f32), shaped((1, cols), f32)]
        + grad_blocks(cols),
        [
            pltpu.VMEM((width, cols), bf16),
            pltpu.VMEM((size, high_cols), f32),
            pltpu.VMEM((size, cols - low_cols), bf16),
            pltpu.VMEM((width, cols), f32),
        ],
        flops=16 * size * width * cols,
        moved=16 * size * width,
    )(
        *by_core,
        *early_parts,
        tiled(attn_gain),
        tiled(attn_shift),
        tiled(qkv_bias),
        cos_table,
        sin_table,
        position.reshape(-1, 1),
        position.reshape(1, -1),
    )
    outs = local_kernel(
        functools.partial(
            mlp_kernel, fsdp_count, tp_count, near, head_groups, seqs, ff, row_blocks
        ),
        [shaped((2, near, size, width), f32)] * tp_count + grad_blocks(2 * padded, vector_rows),
        [pltpu.VMEM((width, 2 * padded), bf16), pltpu.VMEM((width, 2 * padded), f32)],
        flops=12 * seqs * size * width * padded,
        moved=32 * size * width,
    )(
        *by_core,
        *late_parts,
        tiled(mlp_gain),
        tiled(mlp_shift),
        tiled(up_bias),
        tiled(column_sums),
        attn_branch,
        attn_norm,
        attn_sums,
        qkv_bias_part,
    )
    row_parts, late_grads = outs[:tp_count], outs[tp_count:]
    row_sums = sum(exchange(row_parts, "tp"))
    row_sums = row_sums.reshape(2, near, ctx_count, length, width)
    row_sums = scatter_chunks(row_sums, "ctx", 2).reshape(2, near, length, width)
    branches, inner = row_sums[0], row_sums[1]

    def both_cores(half):
        halves = spread(half, "tp")
        return jnp.concatenate(swapped(halves, tp_at), axis=0)

    def scatter_weights(parts):
        columns = parts[0].shape[1]
        rows = parts[0].shape[0] - block_rows + rows_here
        pieces = local_kernel(
            functools.partial(sum_blocks_kernel, fsdp_count, ctx_count, rows_here),
            [shaped((rows, columns), bf16 if k else f32) for k in range(ctx_count)],
        )(*exchange(parts, "fsdp"))
        return exchange(pieces, "ctx")

    early_pieces = scatter_weights(early_grads)
    late_pieces = scatter_weights(late_grads)
    block_half = own_tokens.astype(f32) + branches + (dense_bias + down_bias)
    block_out = both_cores(block_half.astype(bf16))
    own_centred, own_inverse = normed_rows(own_tokens.astype(f32))
    inner = (
        inner
        - jnp.mean(inner, axis=-1, keepdims=True)
        - own_centred * jnp.mean(inner * own_centred, axis=-1, keepdims=True)
    )
    tokens_grad = both_cores(own_grads + own_inverse * inner)
    qkv_weight_grad, dense_weight_grad = local_kernel(
        functools.partial(early_end_kernel, ctx_count, head_groups, qkv_cols, features),
        [shaped(qkv_weight.shape, f32), shaped(dense_weight.shape[::-1], f32)],
    )(*early_pieces)
    up_weight_grad, down_weight_grad, gains, column_grad, column_again, qkv_bias_grad, up_bias_grad = (
        local_kernel(
            functools.partial(
                late_end_kernel, ctx_count, head_groups, ff, padded, qkv_cols, cols
            ),
            [
                shaped(up_weight.shape, f32),
                shaped(down_weight.shape[::-1], f32),
                shaped((4 * width // LANES, LANES), f32),
                shaped((width // LANES, LANES), f32),
                shaped((width // LANES, LANES), f32),
                shaped((3 * HD * heads // LANES, LANES), f32),
                shaped((hidden_all // LANES, LANES), f32),
            ],
        )(*late_pieces)
    )
    gains = [
        part.reshape(width)
        for part in local_kernel(
            functools.partial(gains_end_kernel, tp_count),
            [shaped((width // LANES, LANES), f32)] * 4,
        )(*spread(gains, "tp"))
    ]
    return (
        block_out,
        tokens_grad,
        gains[0],
        gains[1],
        qkv_weight_grad,
        qkv_bias_grad.reshape(3 * HD * heads),
        dense_weight_grad.T,
        column_grad.reshape(width),
        gains[2],
        gains[3],
        up_weight_grad,
        up_bias_grad.reshape(hidden_all),
        down_weight_grad.T,
        column_again.reshape(width),
    )


def solution(mesh):
    in_specs = (
        P("fsdp", "ctx", None),
        P(),
        P(),
        P(),
        P(("fsdp", "ctx"), "tp"),
        P("tp"),
        P("tp", ("fsdp", "ctx")),
        P(),
        P(),
        P(),
        P(("fsdp", "ctx"), "tp"),
        P("tp"),
        P("tp", ("fsdp", "ctx")),
        P(),
        P("fsdp", "ctx", None),
    )
    out_specs = (
        P("fsdp", "ctx", None),
        P("fsdp", "ctx", None),
        P(),
        P(),
        P(("fsdp", "ctx"), "tp"),
        P("tp"),
        P("tp", ("fsdp", "ctx")),
        P(),
        P(),
        P(),
        P(("fsdp", "ctx"), "tp"),
        P("tp"),
        P("tp", ("fsdp", "ctx")),
        P(),
    )

    return jax.shard_map(
        on_device, mesh=mesh, in_specs=in_specs, out_specs=out_specs, check_vma=False
    )
```

```python
import functools
import math

import jax
import jax.numpy as jnp
from jax import lax
from jax.experimental import pallas as pl
from jax.experimental.pallas import tpu as pltpu
from jax.sharding import PartitionSpec as P


HD = 64
ROT = 16
BLK = 32


EPSILON = 1e-05
NEGATIVE = -1e30
ROOT_HALF = 0.7071067811865476
INV_ROOT_TWO_PI = 0.3989422804014327
CONTRACT_LAST = (((1,), (1,)), ((), ()))
CONTRACT_FIRST = (((0,), (0,)), ((), ()))


def positions(order, start, count):
    index = start + jnp.arange(count, dtype=jnp.int32)
    slot = index // BLK
    table = jnp.arange(order.shape[0], dtype=jnp.int32)
    first = jnp.sum(jnp.where(slot[:, None] == table[None, :], order[None, :], 0), axis=1)
    return first * BLK + index % BLK


def swapped(parts, index):
    bit = 1
    while bit < len(parts):
        is_set = (index & bit) != 0
        parts = [jnp.where(is_set, parts[j ^ bit], parts[j]) for j in range(len(parts))]
        bit *= 2
    return parts


def swap(value, axis, bit):
    return lax.ppermute(value, axis, [(i, i ^ bit) for i in range(lax.axis_size(axis))])


def exchange(parts, axis):
    return [parts[0]] + [swap(parts[k], axis, k) for k in range(1, len(parts))]


def spread(value, axis):
    return exchange([value] * lax.axis_size(axis), axis)


def gather_order(count):
    order, bit = [0], count // 2
    while bit:
        order = order + [k ^ bit for k in order]
        bit //= 2
    return order


def gather_chunks(value, axis, dim):
    bit = lax.axis_size(axis) // 2
    while bit:
        other = swap(value, axis, bit)
        value = jnp.concatenate([value, other], axis=dim)
        bit //= 2
    return value


def scatter_chunks(value, axis, dim):
    count = lax.axis_size(axis)
    bit = 1
    while bit < count:
        kept, sent = jnp.split(value, 2, axis=dim)
        other = swap(sent.astype(jnp.bfloat16), axis, bit)
        value = kept + other.astype(jnp.float32)
        bit *= 2
    return value


def dot(left, right):
    return jnp.dot(left, right, preferred_element_type=jnp.float32)


def dot_last(left, right):
    return lax.dot_general(left, right, CONTRACT_LAST, preferred_element_type=jnp.float32)


def dot_first(left, right):
    return lax.dot_general(left, right, CONTRACT_FIRST, preferred_element_type=jnp.float32)


def normed_rows(rows):
    middle = jnp.mean(rows, axis=-1, keepdims=True)
    centred = rows - middle
    inverse = lax.rsqrt(jnp.mean(centred * centred, axis=-1, keepdims=True) + EPSILON)
    return centred * inverse, inverse


VMEM_LIMIT = 60 * 1024 * 1024
LANES = 128
SUBLANES = 16
SCORES_AT_ONCE = 512 * 1024


def local_kernel(body, out_shapes, scratch=(), flops=0, moved=0):
    in_vmem = pl.BlockSpec(memory_space=pltpu.VMEM)
    return pl.pallas_call(
        body,
        out_shape=out_shapes,
        out_specs=jax.tree.map(lambda _: in_vmem, out_shapes),
        scratch_shapes=list(scratch),
        compiler_params=pltpu.CompilerParams(vmem_limit_bytes=VMEM_LIMIT),
        cost_estimate=pl.CostEstimate(flops=flops, bytes_accessed=moved, transcendentals=0),
    )


def shaped(shape, kind):
    return jax.ShapeDtypeStruct(tuple(shape), kind)


def rotary_tables(position):
    lane = jnp.arange(LANES, dtype=jnp.int32) % HD
    half = ROT // 2
    frequency = 1.0 / 10000.0 ** ((lane % half).astype(jnp.float32) * (2.0 / ROT))
    phase = position * jnp.where(lane < ROT, frequency, 0.0)[None, :]
    return jnp.cos(phase), jnp.where(lane < half, -1.0, 1.0)[None, :] * jnp.sin(phase)


def tiled(vector):
    return vector.reshape(-1, LANES)


def row_of(ref):
    return jnp.concatenate([ref[i : i + 1, :] for i in range(ref.shape[0])], axis=1)


def put_row(ref, value):
    for i in range(ref.shape[0]):
        ref[i : i + 1, :] = value[:, i * LANES : (i + 1) * LANES]


def tree_sum(parts):
    while len(parts) > 1:
        parts = [parts[i] + parts[i + 1] for i in range(0, len(parts), 2)]
    return parts[0]


def folded(value, columns):
    return [value[:, i : i + columns] for i in range(0, value.shape[1], columns)]


def early_message_kernel(groups, qkv_cols, features, qkv_ref, dense_ref, *outs):
    at = lax.rem(lax.axis_index("ctx"), groups)
    dense_t = dense_ref[...]
    parts = [
        jnp.concatenate(
            [
                qkv_ref[:, g * qkv_cols : (g + 1) * qkv_cols],
                dense_t[:, g * features : (g + 1) * features],
            ],
            axis=1,
        )
        for g in range(groups)
    ]
    for out, part in zip(outs, swapped(parts, at)):
        out[...] = part


def late_message_kernel(count, ff, padded, up_ref, down_ref, *outs):
    at = lax.axis_index("ctx")
    down_t = down_ref[...]
    rows = up_ref.shape[0]
    gap = [jnp.zeros((rows, padded - ff), jnp.bfloat16)] if padded > ff else []
    parts = [
        jnp.concatenate(
            [up_ref[:, r * ff : (r + 1) * ff]] + gap + [down_t[:, r * ff : (r + 1) * ff]] + gap,
            axis=1,
        )
        for r in range(count)
    ]
    for out, part in zip(outs, swapped(parts, at)):
        out[...] = part


def place_weight(parts, weight, count):
    fsdp_at, ctx_at = lax.axis_index("fsdp"), lax.axis_index("ctx")
    rows = parts[0].shape[0] // count
    for k, part in enumerate(parts):
        for j in range(count):
            place = (fsdp_at ^ k) * count + ((ctx_at ^ j) if count > 1 else 0)
            weight[pl.ds(pl.multiple_of(place * rows, SUBLANES), rows), :] = part[
                j * rows : (j + 1) * rows, :
            ]


def send_blocks(total, outs, block, extra=()):
    at = lax.axis_index("fsdp")
    for k, out in enumerate(outs):
        start = pl.multiple_of((at ^ k) * block, SUBLANES)
        out[:block, :] = total[pl.ds(start, block), :].astype(out.dtype)
        for i, row in enumerate(extra):
            out[block + i : block + i + 1, :] = row.astype(out.dtype)
        rest = out.shape[0] - block - len(extra)
        if rest:
            out[block + len(extra) :, :] = jnp.zeros((rest, out.shape[1]), out.dtype)


def attention_kernel(
    fsdp_count,
    core_count,
    near,
    head_groups,
    own_heads,
    copies,
    seqs,
    row_blocks,
    *refs,
):
    row_refs = refs[:core_count]
    parts = refs[core_count : core_count + fsdp_count]
    (gain_ref, shift_ref, bias_ref, cos_ref, sin_ref, pos_col, pos_row) = refs[
        core_count + fsdp_count : core_count + fsdp_count + 7
    ]
    gain, shift = row_of(gain_ref), row_of(shift_ref)
    outs = refs[core_count + fsdp_count + 7 :]
    mixed, proj_out, weight, bias_out = outs[:4]
    grad_outs = outs[4 : 4 + fsdp_count]
    grads, total = outs[4 + fsdp_count :]
    size = pos_col.shape[0]
    cols = weight.shape[1]
    features = own_heads * HD
    qkv_cols = 3 * features
    low_cols = qkv_cols // LANES * LANES
    high_cols = -(-qkv_cols // LANES) * LANES
    scale = 1.0 / math.sqrt(HD)
    ctx_at = lax.axis_index("ctx")
    seq_at = lax.rem(lax.div(ctx_at, head_groups), seqs)
    core = lax.div(seq_at, near) ^ lax.axis_index("tp")
    inner = lax.rem(seq_at, near)
    place_weight(parts, weight, row_blocks)
    seq_tokens, seq_grads = row_refs[0][0, inner], row_refs[0][1, inner]
    for j in range(1, core_count):
        seq_tokens = jnp.where(core == j, row_refs[j][0, inner], seq_tokens)
        seq_grads = jnp.where(core == j, row_refs[j][1, inner], seq_grads)
    centred, _ = normed_rows(seq_tokens.astype(jnp.float32))
    attn_in = (centred * gain + shift).astype(jnp.bfloat16)
    bias_all = row_of(bias_ref)
    biases = [bias_all[:, g * qkv_cols : (g + 1) * qkv_cols] for g in range(head_groups)]
    bias = swapped(biases, lax.rem(ctx_at, head_groups))[0]
    if high_cols > qkv_cols:
        bias = jnp.concatenate([bias, jnp.zeros((1, high_cols - qkv_cols), jnp.float32)], axis=1)
    lane = lax.broadcasted_iota(jnp.int32, (1, high_cols), 1)
    rotated = (lane < qkv_cols) & (lane % (3 * HD) < 2 * HD)
    first = lane % HD < ROT // 2
    repeat = high_cols // LANES
    cos_all = jnp.where(rotated, jnp.concatenate([cos_ref[...]] * repeat, axis=1), 1.0)
    sin_all = jnp.where(rotated, jnp.concatenate([sin_ref[...]] * repeat, axis=1), 0.0)

    def turn(values, sine):
        ahead = pltpu.roll(values, high_cols - ROT // 2, 1)
        behind = pltpu.roll(values, ROT // 2, 1)
        return values * cos_all + jnp.where(first, ahead, behind) * sine

    projected = dot(attn_in, weight[:, :high_cols]) + bias
    turned = turn(projected, sin_all).astype(jnp.bfloat16)
    ctx_low = dot(seq_grads, weight[:, low_cols:]).astype(jnp.bfloat16)
    allowed = pos_row[...] <= pos_col[...]
    keep = None
    if copies > 1:
        keep = lax.div(ctx_at, head_groups * seqs) == 0
    grads[...] = jnp.zeros(grads.shape, jnp.float32)
    mixed[...] = jnp.zeros(mixed.shape, jnp.bfloat16)
    together = own_heads if own_heads * size * size <= SCORES_AT_ONCE else 1
    for base in range(0, own_heads, together):
        group = range(base, min(base + together, own_heads))
        heads = range(len(group))
        starts = [head * 3 * HD for head in group]
        spots = [qkv_cols - low_cols + head * HD for head in group]
        queries = [turned[:, at : at + HD] for at in starts]
        keys = [turned[:, at + HD : at + 2 * HD] for at in starts]
        values = [turned[:, at + 2 * HD : at + 3 * HD] for at in starts]
        lows = [ctx_low[:, spot : spot + HD] for spot in spots]
        scores = [
            jnp.where(allowed, dot_last(queries[h], keys[h]) * scale, NEGATIVE) for h in heads
        ]
        weight_grads = [dot_last(lows[h], values[h]) for h in heads]
        peaks = [jnp.max(scores[h], axis=-1, keepdims=True) for h in heads]
        weights = [jnp.where(allowed, jnp.exp(scores[h] - peaks[h]), 0.0) for h in heads]
        probs = [weights[h] / jnp.sum(weights[h], axis=-1, keepdims=True) for h in heads]
        probs_low = [probs[h].astype(jnp.bfloat16) for h in heads]
        attended = [dot(probs_low[h], values[h]) for h in heads]
        deltas = [
            jnp.sum(lows[h].astype(jnp.float32) * attended[h], axis=-1, keepdims=True) for h in heads
        ]
        score_grads = [probs[h] * (weight_grads[h] - deltas[h]) for h in heads]
        if copies > 1:
            score_grads = [jnp.where(keep, part, 0.0) for part in score_grads]
            probs_low = [jnp.where(keep, part, jnp.zeros_like(part)) for part in probs_low]
            attended = [jnp.where(keep, part, 0.0) for part in attended]
        score_low = [part.astype(jnp.bfloat16) for part in score_grads]
        for h in heads:
            at, spot = starts[h], spots[h]
            grads[:, at : at + HD] = dot(score_low[h], keys[h]) * scale
            grads[:, at + HD : at + 2 * HD] = dot_first(score_low[h], queries[h]) * scale
            grads[:, at + 2 * HD : at + 3 * HD] = dot_first(probs_low[h], lows[h])
            mixed[:, spot : spot + HD] = attended[h].astype(jnp.bfloat16)
    proj_grad = turn(grads[...], -sin_all)
    proj_low = proj_grad.astype(jnp.bfloat16)
    total[:, :high_cols] = dot_first(attn_in, proj_low)
    if cols > high_cols:
        total[:, high_cols:] = jnp.zeros((weight.shape[0], cols - high_cols), jnp.float32)
    total[:, low_cols:] += dot_first(seq_grads, mixed[...])
    send_blocks(total, grad_outs, grad_outs[0].shape[0])
    proj_out[...] = proj_low
    bias_out[:, :high_cols] = jnp.sum(proj_grad, axis=0, keepdims=True)
    if cols > high_cols:
        bias_out[:, high_cols:] = jnp.zeros((1, cols - high_cols), jnp.float32)


def mlp_kernel(fsdp_count, core_count, near, head_groups, seqs, ff, row_blocks, *refs):
    row_refs = refs[:core_count]
    parts = refs[core_count : core_count + fsdp_count]
    (
        gain_ref,
        shift_ref,
        bias_ref,
        columns_ref,
        attn_gain_ref,
        mixed,
        proj_low,
        attn_weight,
        attn_bias,
    ) = refs[core_count + fsdp_count : core_count + fsdp_count + 9]
    outs = refs[core_count + fsdp_count + 9 :]
    both = outs[:core_count]
    grad_outs = outs[core_count : core_count + fsdp_count]
    weight, total = outs[core_count + fsdp_count :]
    gain, shift = row_of(gain_ref), row_of(shift_ref)
    size, width = mixed.shape[0], weight.shape[0]
    both_cols = weight.shape[1]
    padded = both_cols // 2
    ctx_at = lax.axis_index("ctx")
    bias_all = row_of(bias_ref)
    count = bias_all.shape[1] // ff
    bias = swapped([bias_all[:, r * ff : (r + 1) * ff] for r in range(count)], ctx_at)[0]
    if padded > ff:
        bias = jnp.concatenate([bias, jnp.zeros((1, padded - ff), jnp.float32)], axis=1)
    seq_at = lax.rem(lax.div(ctx_at, head_groups), seqs)
    core = lax.div(seq_at, near) ^ lax.axis_index("tp")
    inner = lax.rem(seq_at, near)
    place_weight(parts, weight, row_blocks)
    up, down = weight[:, :padded], weight[:, padded:]
    rows = jnp.concatenate([ref[0].reshape(near * size, width) for ref in row_refs], axis=0)
    grad_rows = jnp.concatenate([ref[1].reshape(near * size, width) for ref in row_refs], axis=0)
    centred, _ = normed_rows(rows.astype(jnp.float32))
    mlp_in = (centred * gain + shift).astype(jnp.bfloat16)
    pre_act = dot(mlp_in, up) + bias
    normal = 0.5 * (1.0 + lax.erf(pre_act * ROOT_HALF))
    hidden = (pre_act * normal).astype(jnp.bfloat16)
    slope = normal + pre_act * jnp.exp(-0.5 * pre_act * pre_act) * INV_ROOT_TWO_PI
    pre_grad = dot(grad_rows, down) * slope
    pre_low = pre_grad.astype(jnp.bfloat16)
    total[:, :padded] = dot_first(mlp_in, pre_low)
    total[:, padded:] = dot_first(grad_rows, hidden)
    norm_grad = dot_last(pre_low, up)
    low_cols = attn_weight.shape[1] - mixed.shape[1]
    attn_branch = dot_last(mixed[...], attn_weight[:, low_cols:])
    attn_norm = dot_last(proj_low[...], attn_weight[:, : proj_low.shape[1]])
    slot = core * near + inner
    seq_centred = centred[:size]
    for i in range(1, core_count * near):
        seq_centred = jnp.where(slot == i, centred[i * size : (i + 1) * size], seq_centred)
    bias_sum = jnp.concatenate(
        [jnp.sum(pre_grad, axis=0, keepdims=True), jnp.zeros((1, padded), jnp.float32)], axis=1
    )
    vectors = [
        jnp.sum(attn_norm * seq_centred, axis=0, keepdims=True),
        jnp.sum(attn_norm, axis=0, keepdims=True),
        jnp.sum(norm_grad * centred, axis=0, keepdims=True),
        jnp.sum(norm_grad, axis=0, keepdims=True),
        row_of(columns_ref),
        attn_bias[...],
    ]
    extra = [piece for vector in vectors for piece in folded(vector, both_cols)] + [bias_sum]
    send_blocks(total, grad_outs, width // fsdp_count, extra)
    norm_grad = norm_grad * gain
    attn_norm = attn_norm * row_of(attn_gain_ref)
    branch = dot_last(hidden, down)
    for j in range(core_count):
        for i in range(near):
            here = (core == j) & (inner == i)
            at = (j * near + i) * size
            out = both[j]
            out[0, i] = branch[at : at + size] + jnp.where(here, attn_branch, 0.0)
            out[1, i] = norm_grad[at : at + size] + jnp.where(here, attn_norm, 0.0)


def sum_blocks_kernel(fsdp_count, ctx_count, rows_here, *refs):
    parts, outs = refs[:fsdp_count], refs[fsdp_count:]
    block = ctx_count * rows_here
    total = parts[0][:block, :]
    for part in parts[1:]:
        total = total + part[:block, :].astype(jnp.float32)
    pieces = [total[r * rows_here : (r + 1) * rows_here] for r in range(ctx_count)]
    for out, piece in zip(outs, swapped(pieces, lax.axis_index("ctx"))):
        out[:rows_here, :] = piece.astype(out.dtype)
    if outs[0].shape[0] > rows_here:
        vectors = tree_sum(
            [part[block:, :].astype(jnp.bfloat16).astype(jnp.float32) for part in parts]
        ).astype(jnp.bfloat16)
        for out in outs:
            out[rows_here:, :] = vectors.astype(out.dtype)


def early_end_kernel(count, groups, qkv_cols, features, *refs):
    parts, (qkv_out, dense_out) = refs[:count], refs[count:]
    at = lax.rem(lax.axis_index("ctx"), groups)
    sums = []
    for g in range(groups):
        sums.append(tree_sum([part[...].astype(jnp.float32) for part in parts[g::groups]]))
    for g, block in enumerate(swapped(sums, at)):
        qkv_out[:, g * qkv_cols : (g + 1) * qkv_cols] = block[:, :qkv_cols]
        dense_out[:, g * features : (g + 1) * features] = block[:, qkv_cols:]


def late_end_kernel(count, groups, ff, padded, qkv_cols, cols, *refs):
    parts, outs = refs[:count], refs[count:]
    up_out, down_out, gains_out, columns_out, columns_again, qkv_bias_out, up_bias_out = outs
    rows, width = up_out.shape[0], LANES * columns_out.shape[0]
    both_cols = 2 * padded
    ctx_at = lax.axis_index("ctx")
    blocks = [part[:rows, :].astype(jnp.float32) for part in parts]
    for r, block in enumerate(swapped(blocks, ctx_at)):
        up_out[:, r * ff : (r + 1) * ff] = block[:, :ff]
        down_out[:, r * ff : (r + 1) * ff] = block[:, padded : padded + ff]
    vectors = [part[rows:, :].astype(jnp.float32) for part in parts]

    def unfolded(block, start, extent):
        n = extent // both_cols
        return jnp.concatenate([block[start + i : start + i + 1] for i in range(n)], axis=1)

    summed = tree_sum(vectors)
    step = width // both_cols
    gains = jnp.concatenate([unfolded(summed, i * step, width) for i in range(4)], axis=1)
    put_row(gains_out, gains)
    columns = unfolded(summed, 4 * step, width)
    put_row(columns_out, columns)
    put_row(columns_again, columns)
    sums = [tree_sum(vectors[g::groups]) for g in range(groups)]
    sums = [unfolded(block, 5 * step, cols)[:, :qkv_cols] for block in sums]
    put_row(
        qkv_bias_out, jnp.concatenate(swapped(sums, lax.rem(ctx_at, groups)), axis=1)
    )
    last = 5 * step + cols // both_cols
    ups = [block[last : last + 1, :ff] for block in vectors]
    put_row(up_bias_out, jnp.concatenate(swapped(ups, ctx_at), axis=1))


def gains_end_kernel(count, *refs):
    parts, outs = refs[:count], refs[count : count + 4]
    total = tree_sum([part[...] for part in parts])
    rows = total.shape[0] // 4
    for i, out in enumerate(outs):
        out[...] = total[i * rows : (i + 1) * rows]


def on_device(
    tokens,
    group_order,
    attn_gain,
    attn_shift,
    qkv_weight,
    qkv_bias,
    dense_weight,
    dense_bias,
    mlp_gain,
    mlp_shift,
    up_weight,
    up_bias,
    down_weight,
    down_bias,
    out_grad,
):
    bf16, f32 = jnp.bfloat16, jnp.float32
    seqs, length, width = tokens.shape
    fsdp_count, ctx_count, tp_count = (lax.axis_size(a) for a in ("fsdp", "ctx", "tp"))
    ctx_at, tp_at = lax.axis_index("ctx"), lax.axis_index("tp")
    rows_here = qkv_weight.shape[0]
    block_rows = ctx_count * rows_here
    heads = qkv_bias.shape[0] // (3 * HD)
    hidden_all = up_bias.shape[0]
    head_groups = math.gcd(heads, ctx_count)
    own_heads = heads // head_groups
    copies = ctx_count // head_groups // seqs
    features = own_heads * HD
    qkv_cols = 3 * features
    cols = qkv_cols + features
    low_cols = qkv_cols // LANES * LANES
    high_cols = -(-qkv_cols // LANES) * LANES
    ff = hidden_all // ctx_count
    padded = -(-ff // LANES) * LANES
    near = seqs // tp_count
    size = ctx_count * length

    early = local_kernel(
        functools.partial(early_message_kernel, head_groups, qkv_cols, features),
        [shaped((rows_here, cols), bf16)] * head_groups,
    )(qkv_weight, dense_weight.T)
    late = local_kernel(
        functools.partial(late_message_kernel, ctx_count, ff, padded),
        [shaped((rows_here, 2 * padded), bf16)] * ctx_count,
    )(up_weight, down_weight.T)
    early_rows = exchange([early[k % head_groups] for k in range(ctx_count)], "ctx")

    def near_part(array):
        parts = [array[j * near : (j + 1) * near] for j in range(tp_count)]
        return swapped(parts, tp_at)[0]

    own_tokens = near_part(tokens)
    own_grads = near_part(out_grad)
    message = jnp.stack([own_tokens, own_grads.astype(bf16)])
    late_rows = exchange(late, "ctx")
    chunks = gather_chunks(message[:, :, None], "ctx", 2)
    chunks = chunks.reshape(2, near, size, width)

    loose = rows_here % SUBLANES == 0

    def own_rows(parts):
        return jnp.concatenate(parts if loose else swapped(parts, ctx_at), axis=0)

    early_parts = spread(own_rows(early_rows), "fsdp")
    late_parts = spread(own_rows(late_rows), "fsdp")
    by_core = spread(chunks, "tp")

    position = jnp.concatenate(
        [
            positions(group_order, (ctx_at ^ k) * length, length)
            for k in gather_order(ctx_count)
        ]
    ).astype(f32)
    cos_table, sin_table = rotary_tables(position[:, None])
    column_sums = jnp.sum(out_grad, axis=(0, 1))

    def grad_blocks(columns, extra=0):
        return [
            shaped((block_rows + extra, columns), bf16 if k else f32) for k in range(fsdp_count)
        ]

    vector_rows = (5 * width + cols) // (2 * padded) + 1
    vector_rows = -(-vector_rows // SUBLANES) * SUBLANES

    row_blocks = ctx_count if loose else 1
    mixed, proj_low, attn_weight, qkv_bias_part, *early_grads = local_kernel(
        functools.partial(
            attention_kernel,
            fsdp_count,
            tp_count,
            near,
            head_groups,
            own_heads,
            copies,
            seqs,
            row_blocks,
        ),
        [
            shaped((size, cols - low_cols), bf16),
            shaped((size, high_cols), bf16),
            shaped((width, cols), bf16),
            shaped((1, cols), f32),
        ]
        + grad_blocks(cols),
        [pltpu.VMEM((size, high_cols), f32), pltpu.VMEM((width, cols), f32)],
        flops=16 * size * width * cols,
        moved=16 * size * width,
    )(
        *by_core,
        *early_parts,
        tiled(attn_gain),
        tiled(attn_shift),
        tiled(qkv_bias),
        cos_table,
        sin_table,
        position.reshape(-1, 1),
        position.reshape(1, -1),
    )
    outs = local_kernel(
        functools.partial(
            mlp_kernel, fsdp_count, tp_count, near, head_groups, seqs, ff, row_blocks
        ),
        [shaped((2, near, size, width), f32)] * tp_count + grad_blocks(2 * padded, vector_rows),
        [pltpu.VMEM((width, 2 * padded), bf16), pltpu.VMEM((width, 2 * padded), f32)],
        flops=12 * seqs * size * width * padded,
        moved=32 * size * width,
    )(
        *by_core,
        *late_parts,
        tiled(mlp_gain),
        tiled(mlp_shift),
        tiled(up_bias),
        tiled(column_sums),
        tiled(attn_gain),
        mixed,
        proj_low,
        attn_weight,
        qkv_bias_part,
    )
    row_parts, late_grads = outs[:tp_count], outs[tp_count:]
    row_sums = sum(exchange(row_parts, "tp"))
    row_sums = row_sums.reshape(2, near, ctx_count, length, width)
    row_sums = scatter_chunks(row_sums, "ctx", 2).reshape(2, near, length, width)
    branches, inner = row_sums[0], row_sums[1]

    def both_cores(half):
        halves = spread(half, "tp")
        return jnp.concatenate(swapped(halves, tp_at), axis=0)

    def scatter_weights(parts):
        columns = parts[0].shape[1]
        rows = parts[0].shape[0] - block_rows + rows_here
        pieces = local_kernel(
            functools.partial(sum_blocks_kernel, fsdp_count, ctx_count, rows_here),
            [shaped((rows, columns), bf16 if k else f32) for k in range(ctx_count)],
        )(*exchange(parts, "fsdp"))
        return exchange(pieces, "ctx")

    early_pieces = scatter_weights(early_grads)
    late_pieces = scatter_weights(late_grads)
    block_half = own_tokens.astype(f32) + branches + (dense_bias + down_bias)
    block_out = both_cores(block_half.astype(bf16))
    own_centred, own_inverse = normed_rows(own_tokens.astype(f32))
    inner = (
        inner
        - jnp.mean(inner, axis=-1, keepdims=True)
        - own_centred * jnp.mean(inner * own_centred, axis=-1, keepdims=True)
    )
    tokens_grad = both_cores(own_grads + own_inverse * inner)
    qkv_weight_grad, dense_weight_grad = local_kernel(
        functools.partial(early_end_kernel, ctx_count, head_groups, qkv_cols, features),
        [shaped(qkv_weight.shape, f32), shaped(dense_weight.shape[::-1], f32)],
    )(*early_pieces)
    up_weight_grad, down_weight_grad, gains, column_grad, column_again, qkv_bias_grad, up_bias_grad = (
        local_kernel(
            functools.partial(
                late_end_kernel, ctx_count, head_groups, ff, padded, qkv_cols, cols
            ),
            [
                shaped(up_weight.shape, f32),
                shaped(down_weight.shape[::-1], f32),
                shaped((4 * width // LANES, LANES), f32),
                shaped((width // LANES, LANES), f32),
                shaped((width // LANES, LANES), f32),
                shaped((3 * HD * heads // LANES, LANES), f32),
                shaped((hidden_all // LANES, LANES), f32),
            ],
        )(*late_pieces)
    )
    gains = [
        part.reshape(width)
        for part in local_kernel(
            functools.partial(gains_end_kernel, tp_count),
            [shaped((width // LANES, LANES), f32)] * 4,
        )(*spread(gains, "tp"))
    ]
    return (
        block_out,
        tokens_grad,
        gains[0],
        gains[1],
        qkv_weight_grad,
        qkv_bias_grad.reshape(3 * HD * heads),
        dense_weight_grad.T,
        column_grad.reshape(width),
        gains[2],
        gains[3],
        up_weight_grad,
        up_bias_grad.reshape(hidden_all),
        down_weight_grad.T,
        column_again.reshape(width),
    )


def solution(mesh):
    in_specs = (
        P("fsdp", "ctx", None),
        P(),
        P(),
        P(),
        P(("fsdp", "ctx"), "tp"),
        P("tp"),
        P("tp", ("fsdp", "ctx")),
        P(),
        P(),
        P(),
        P(("fsdp", "ctx"), "tp"),
        P("tp"),
        P("tp", ("fsdp", "ctx")),
        P(),
        P("fsdp", "ctx", None),
    )
    out_specs = (
        P("fsdp", "ctx", None),
        P("fsdp", "ctx", None),
        P(),
        P(),
        P(("fsdp", "ctx"), "tp"),
        P("tp"),
        P("tp", ("fsdp", "ctx")),
        P(),
        P(),
        P(),
        P(("fsdp", "ctx"), "tp"),
        P("tp"),
        P("tp", ("fsdp", "ctx")),
        P(),
    )

    return jax.shard_map(
        on_device, mesh=mesh, in_specs=in_specs, out_specs=out_specs, check_vma=False
    )
```

```python
import functools
import math

import jax
import jax.numpy as jnp
from jax import lax
from jax.experimental import pallas as pl
from jax.experimental.pallas import tpu as pltpu
from jax.sharding import PartitionSpec as P


HD = 64
ROT = 16
BLK = 32


EPSILON = 1e-05
NEGATIVE = -1e30
ROOT_HALF = 0.7071067811865476
INV_ROOT_TWO_PI = 0.3989422804014327
CONTRACT_LAST = (((1,), (1,)), ((), ()))
CONTRACT_FIRST = (((0,), (0,)), ((), ()))


def positions(order, start, count):
    index = start + jnp.arange(count, dtype=jnp.int32)
    slot = index // BLK
    table = jnp.arange(order.shape[0], dtype=jnp.int32)
    first = jnp.sum(jnp.where(slot[:, None] == table[None, :], order[None, :], 0), axis=1)
    return first * BLK + index % BLK


def swapped(parts, index):
    bit = 1
    while bit < len(parts):
        is_set = (index & bit) != 0
        parts = [jnp.where(is_set, parts[j ^ bit], parts[j]) for j in range(len(parts))]
        bit *= 2
    return parts


def swap(value, axis, bit):
    return lax.ppermute(value, axis, [(i, i ^ bit) for i in range(lax.axis_size(axis))])


def exchange(parts, axis):
    return [parts[0]] + [swap(parts[k], axis, k) for k in range(1, len(parts))]


def spread(value, axis):
    return exchange([value] * lax.axis_size(axis), axis)


def gather_order(count):
    order, bit = [0], count // 2
    while bit:
        order = order + [k ^ bit for k in order]
        bit //= 2
    return order


def gather_chunks(value, axis, dim):
    bit = lax.axis_size(axis) // 2
    while bit:
        other = swap(value, axis, bit)
        value = jnp.concatenate([value, other], axis=dim)
        bit //= 2
    return value


def scatter_chunks(value, axis, dim):
    count = lax.axis_size(axis)
    bit = 1
    while bit < count:
        kept, sent = jnp.split(value, 2, axis=dim)
        other = swap(sent.astype(jnp.bfloat16), axis, bit)
        value = kept + other.astype(jnp.float32)
        bit *= 2
    return value


def dot(left, right):
    return jnp.dot(left, right, preferred_element_type=jnp.float32)


def dot_last(left, right):
    return lax.dot_general(left, right, CONTRACT_LAST, preferred_element_type=jnp.float32)


def dot_first(left, right):
    return lax.dot_general(left, right, CONTRACT_FIRST, preferred_element_type=jnp.float32)


def normed_rows(rows):
    middle = jnp.mean(rows, axis=-1, keepdims=True)
    centred = rows - middle
    inverse = lax.rsqrt(jnp.mean(centred * centred, axis=-1, keepdims=True) + EPSILON)
    return centred * inverse, inverse


VMEM_LIMIT = 60 * 1024 * 1024
LANES = 128
SUBLANES = 16
SCORES_AT_ONCE = 512 * 1024


def local_kernel(body, out_shapes, scratch=(), flops=0, moved=0):
    in_vmem = pl.BlockSpec(memory_space=pltpu.VMEM)
    return pl.pallas_call(
        body,
        out_shape=out_shapes,
        out_specs=jax.tree.map(lambda _: in_vmem, out_shapes),
        scratch_shapes=list(scratch),
        compiler_params=pltpu.CompilerParams(vmem_limit_bytes=VMEM_LIMIT),
        cost_estimate=pl.CostEstimate(flops=flops, bytes_accessed=moved, transcendentals=0),
    )


def shaped(shape, kind):
    return jax.ShapeDtypeStruct(tuple(shape), kind)


def rotary_tables(position):
    lane = jnp.arange(LANES, dtype=jnp.int32) % HD
    half = ROT // 2
    frequency = 1.0 / 10000.0 ** ((lane % half).astype(jnp.float32) * (2.0 / ROT))
    phase = position * jnp.where(lane < ROT, frequency, 0.0)[None, :]
    return jnp.cos(phase), jnp.where(lane < half, -1.0, 1.0)[None, :] * jnp.sin(phase)


def tiled(vector):
    return vector.reshape(-1, LANES)


def row_of(ref):
    return jnp.concatenate([ref[i : i + 1, :] for i in range(ref.shape[0])], axis=1)


def put_row(ref, value):
    for i in range(ref.shape[0]):
        ref[i : i + 1, :] = value[:, i * LANES : (i + 1) * LANES]


def tree_sum(parts):
    while len(parts) > 1:
        parts = [parts[i] + parts[i + 1] for i in range(0, len(parts), 2)]
    return parts[0]


def folded(value, columns):
    return [value[:, i : i + columns] for i in range(0, value.shape[1], columns)]


def early_message_kernel(groups, qkv_cols, features, qkv_ref, dense_ref, *outs):
    at = lax.rem(lax.axis_index("ctx"), groups)
    dense_t = dense_ref[...]
    parts = [
        jnp.concatenate(
            [
                qkv_ref[:, g * qkv_cols : (g + 1) * qkv_cols],
                dense_t[:, g * features : (g + 1) * features],
            ],
            axis=1,
        )
        for g in range(groups)
    ]
    for out, part in zip(outs, swapped(parts, at)):
        out[...] = part


def late_message_kernel(count, ff, padded, up_ref, down_ref, *outs):
    at = lax.axis_index("ctx")
    down_t = down_ref[...]
    rows = up_ref.shape[0]
    gap = [jnp.zeros((rows, padded - ff), jnp.bfloat16)] if padded > ff else []
    parts = [
        jnp.concatenate(
            [up_ref[:, r * ff : (r + 1) * ff]] + gap + [down_t[:, r * ff : (r + 1) * ff]] + gap,
            axis=1,
        )
        for r in range(count)
    ]
    for out, part in zip(outs, swapped(parts, at)):
        out[...] = part


def place_weight(parts, weight, count):
    fsdp_at, ctx_at = lax.axis_index("fsdp"), lax.axis_index("ctx")
    rows = parts[0].shape[0] // count
    for k, part in enumerate(parts):
        for j in range(count):
            place = (fsdp_at ^ k) * count + ((ctx_at ^ j) if count > 1 else 0)
            weight[pl.ds(pl.multiple_of(place * rows, SUBLANES), rows), :] = part[
                j * rows : (j + 1) * rows, :
            ]


def send_blocks(total, outs, block, extra=()):
    at = lax.axis_index("fsdp")
    for k, out in enumerate(outs):
        start = pl.multiple_of((at ^ k) * block, SUBLANES)
        out[:block, :] = total[pl.ds(start, block), :].astype(out.dtype)
        for i, row in enumerate(extra):
            out[block + i : block + i + 1, :] = row.astype(out.dtype)
        rest = out.shape[0] - block - len(extra)
        if rest:
            out[block + len(extra) :, :] = jnp.zeros((rest, out.shape[1]), out.dtype)


def attention_kernel(
    fsdp_count,
    core_count,
    near,
    head_groups,
    own_heads,
    copies,
    seqs,
    row_blocks,
    *refs,
):
    row_refs = refs[:core_count]
    parts = refs[core_count : core_count + fsdp_count]
    (gain_ref, shift_ref, bias_ref, cos_ref, sin_ref, pos_col, pos_row) = refs[
        core_count + fsdp_count : core_count + fsdp_count + 7
    ]
    gain, shift = row_of(gain_ref), row_of(shift_ref)
    outs = refs[core_count + fsdp_count + 7 :]
    mixed, proj_out, weight, bias_out = outs[:4]
    grad_outs = outs[4 : 4 + fsdp_count]
    grads, total = outs[4 + fsdp_count :]
    size = pos_col.shape[0]
    cols = weight.shape[1]
    features = own_heads * HD
    qkv_cols = 3 * features
    low_cols = qkv_cols // LANES * LANES
    high_cols = -(-qkv_cols // LANES) * LANES
    scale = 1.0 / math.sqrt(HD)
    ctx_at = lax.axis_index("ctx")
    seq_at = lax.rem(lax.div(ctx_at, head_groups), seqs)
    core = lax.div(seq_at, near) ^ lax.axis_index("tp")
    inner = lax.rem(seq_at, near)
    place_weight(parts, weight, row_blocks)
    seq_tokens, seq_grads = row_refs[0][0, inner], row_refs[0][1, inner]
    for j in range(1, core_count):
        seq_tokens = jnp.where(core == j, row_refs[j][0, inner], seq_tokens)
        seq_grads = jnp.where(core == j, row_refs[j][1, inner], seq_grads)
    centred, _ = normed_rows(seq_tokens.astype(jnp.float32))
    attn_in = (centred * gain + shift).astype(jnp.bfloat16)
    bias_all = row_of(bias_ref)
    biases = [bias_all[:, g * qkv_cols : (g + 1) * qkv_cols] for g in range(head_groups)]
    bias = swapped(biases, lax.rem(ctx_at, head_groups))[0]
    if high_cols > qkv_cols:
        bias = jnp.concatenate([bias, jnp.zeros((1, high_cols - qkv_cols), jnp.float32)], axis=1)
    lane = lax.broadcasted_iota(jnp.int32, (1, high_cols), 1)
    rotated = (lane < qkv_cols) & (lane % (3 * HD) < 2 * HD)
    first = lane % HD < ROT // 2
    repeat = high_cols // LANES
    cos_all = jnp.where(rotated, jnp.concatenate([cos_ref[...]] * repeat, axis=1), 1.0)
    sin_all = jnp.where(rotated, jnp.concatenate([sin_ref[...]] * repeat, axis=1), 0.0)

    def turn(values, sine):
        ahead = pltpu.roll(values, high_cols - ROT // 2, 1)
        behind = pltpu.roll(values, ROT // 2, 1)
        return values * cos_all + jnp.where(first, ahead, behind) * sine

    projected = dot(attn_in, weight[:, :high_cols]) + bias
    turned = turn(projected, sin_all).astype(jnp.bfloat16)
    ctx_low = dot(seq_grads, weight[:, low_cols:]).astype(jnp.bfloat16)
    allowed = pos_row[...] <= pos_col[...]
    keep = None
    if copies > 1:
        keep = lax.div(ctx_at, head_groups * seqs) == 0
    grads[...] = jnp.zeros(grads.shape, jnp.float32)
    mixed[...] = jnp.zeros(mixed.shape, jnp.bfloat16)
    together = own_heads if own_heads * size * size <= SCORES_AT_ONCE else 1
    for base in range(0, own_heads, together):
        group = range(base, min(base + together, own_heads))
        heads = range(len(group))
        starts = [head * 3 * HD for head in group]
        spots = [qkv_cols - low_cols + head * HD for head in group]
        queries = [turned[:, at : at + HD] for at in starts]
        keys = [turned[:, at + HD : at + 2 * HD] for at in starts]
        values = [turned[:, at + 2 * HD : at + 3 * HD] for at in starts]
        lows = [ctx_low[:, spot : spot + HD] for spot in spots]
        scores = [
            jnp.where(allowed, dot_last(queries[h], keys[h]) * scale, NEGATIVE) for h in heads
        ]
        weight_grads = [dot_last(lows[h], values[h]) for h in heads]
        peaks = [jnp.max(scores[h], axis=-1, keepdims=True) for h in heads]
        weights = [jnp.where(allowed, jnp.exp(scores[h] - peaks[h]), 0.0) for h in heads]
        probs = [weights[h] / jnp.sum(weights[h], axis=-1, keepdims=True) for h in heads]
        probs_low = [probs[h].astype(jnp.bfloat16) for h in heads]
        attended = [dot(probs_low[h], values[h]) for h in heads]
        deltas = [
            jnp.sum(lows[h].astype(jnp.float32) * attended[h], axis=-1, keepdims=True) for h in heads
        ]
        score_grads = [probs[h] * (weight_grads[h] - deltas[h]) for h in heads]
        if copies > 1:
            score_grads = [jnp.where(keep, part, 0.0) for part in score_grads]
            probs_low = [jnp.where(keep, part, jnp.zeros_like(part)) for part in probs_low]
            attended = [jnp.where(keep, part, 0.0) for part in attended]
        score_low = [part.astype(jnp.bfloat16) for part in score_grads]
        for h in heads:
            at, spot = starts[h], spots[h]
            grads[:, at : at + HD] = dot(score_low[h], keys[h]) * scale
            grads[:, at + HD : at + 2 * HD] = dot_first(score_low[h], queries[h]) * scale
            grads[:, at + 2 * HD : at + 3 * HD] = dot_first(probs_low[h], lows[h])
            mixed[:, spot : spot + HD] = attended[h].astype(jnp.bfloat16)
    proj_grad = turn(grads[...], -sin_all)
    proj_low = proj_grad.astype(jnp.bfloat16)
    total[:, :high_cols] = dot_first(attn_in, proj_low)
    if cols > high_cols:
        total[:, high_cols:] = jnp.zeros((weight.shape[0], cols - high_cols), jnp.float32)
    total[:, low_cols:] += dot_first(seq_grads, mixed[...])
    send_blocks(total, grad_outs, grad_outs[0].shape[0])
    proj_out[...] = proj_low
    bias_out[:, :high_cols] = jnp.sum(proj_grad, axis=0, keepdims=True)
    if cols > high_cols:
        bias_out[:, high_cols:] = jnp.zeros((1, cols - high_cols), jnp.float32)


def mlp_kernel(fsdp_count, core_count, near, head_groups, seqs, ff, row_blocks, *refs):
    row_refs = refs[:core_count]
    parts = refs[core_count : core_count + fsdp_count]
    (
        gain_ref,
        shift_ref,
        bias_ref,
        columns_ref,
        attn_gain_ref,
        mixed,
        proj_low,
        attn_weight,
        attn_bias,
    ) = refs[core_count + fsdp_count : core_count + fsdp_count + 9]
    outs = refs[core_count + fsdp_count + 9 :]
    both = outs[:core_count]
    grad_outs = outs[core_count : core_count + fsdp_count]
    weight, total = outs[core_count + fsdp_count :]
    gain, shift = row_of(gain_ref), row_of(shift_ref)
    size, width = mixed.shape[0], weight.shape[0]
    both_cols = weight.shape[1]
    padded = both_cols // 2
    ctx_at = lax.axis_index("ctx")
    bias_all = row_of(bias_ref)
    count = bias_all.shape[1] // ff
    bias = swapped([bias_all[:, r * ff : (r + 1) * ff] for r in range(count)], ctx_at)[0]
    if padded > ff:
        bias = jnp.concatenate([bias, jnp.zeros((1, padded - ff), jnp.float32)], axis=1)
    seq_at = lax.rem(lax.div(ctx_at, head_groups), seqs)
    core = lax.div(seq_at, near) ^ lax.axis_index("tp")
    inner = lax.rem(seq_at, near)
    place_weight(parts, weight, row_blocks)
    up, down = weight[:, :padded], weight[:, padded:]
    rows = jnp.concatenate([ref[0].reshape(near * size, width) for ref in row_refs], axis=0)
    grad_rows = jnp.concatenate([ref[1].reshape(near * size, width) for ref in row_refs], axis=0)
    centred, _ = normed_rows(rows.astype(jnp.float32))
    mlp_in = (centred * gain + shift).astype(jnp.bfloat16)
    pre_act = dot(mlp_in, up) + bias
    normal = 0.5 * (1.0 + lax.erf(pre_act * ROOT_HALF))
    hidden = (pre_act * normal).astype(jnp.bfloat16)
    slope = normal + pre_act * jnp.exp(-0.5 * pre_act * pre_act) * INV_ROOT_TWO_PI
    pre_grad = dot(grad_rows, down) * slope
    pre_low = pre_grad.astype(jnp.bfloat16)
    total[:, :padded] = dot_first(mlp_in, pre_low)
    total[:, padded:] = dot_first(grad_rows, hidden)
    norm_grad = dot_last(pre_low, up)
    low_cols = attn_weight.shape[1] - mixed.shape[1]
    attn_branch = dot_last(mixed[...], attn_weight[:, low_cols:])
    attn_norm = dot_last(proj_low[...], attn_weight[:, : proj_low.shape[1]])
    slot = core * near + inner
    seq_centred = centred[:size]
    for i in range(1, core_count * near):
        seq_centred = jnp.where(slot == i, centred[i * size : (i + 1) * size], seq_centred)
    bias_sum = jnp.concatenate(
        [jnp.sum(pre_grad, axis=0, keepdims=True), jnp.zeros((1, padded), jnp.float32)], axis=1
    )
    vectors = [
        jnp.sum(attn_norm * seq_centred, axis=0, keepdims=True),
        jnp.sum(attn_norm, axis=0, keepdims=True),
        jnp.sum(norm_grad * centred, axis=0, keepdims=True),
        jnp.sum(norm_grad, axis=0, keepdims=True),
        row_of(columns_ref),
        attn_bias[...],
    ]
    extra = [piece for vector in vectors for piece in folded(vector, both_cols)] + [bias_sum]
    send_blocks(total, grad_outs, width // fsdp_count, extra)
    norm_grad = norm_grad * gain
    attn_norm = attn_norm * row_of(attn_gain_ref)
    branch = dot_last(hidden, down)
    for j in range(core_count):
        for i in range(near):
            here = (core == j) & (inner == i)
            at = (j * near + i) * size
            out = both[j]
            out[0, i] = branch[at : at + size] + jnp.where(here, attn_branch, 0.0)
            out[1, i] = norm_grad[at : at + size] + jnp.where(here, attn_norm, 0.0)


def sum_blocks_kernel(fsdp_count, ctx_count, rows_here, *refs):
    parts, outs = refs[:fsdp_count], refs[fsdp_count:]
    block = ctx_count * rows_here
    total = parts[0][:block, :]
    for part in parts[1:]:
        total = total + part[:block, :].astype(jnp.float32)
    pieces = [total[r * rows_here : (r + 1) * rows_here] for r in range(ctx_count)]
    for out, piece in zip(outs, swapped(pieces, lax.axis_index("ctx"))):
        out[:rows_here, :] = piece.astype(out.dtype)
    if outs[0].shape[0] > rows_here:
        vectors = tree_sum(
            [part[block:, :].astype(jnp.bfloat16).astype(jnp.float32) for part in parts]
        ).astype(jnp.bfloat16)
        for out in outs:
            out[rows_here:, :] = vectors.astype(out.dtype)


def early_end_kernel(count, groups, qkv_cols, features, *refs):
    parts, (qkv_out, dense_out) = refs[:count], refs[count:]
    at = lax.rem(lax.axis_index("ctx"), groups)
    sums = []
    for g in range(groups):
        sums.append(tree_sum([part[...].astype(jnp.float32) for part in parts[g::groups]]))
    for g, block in enumerate(swapped(sums, at)):
        qkv_out[:, g * qkv_cols : (g + 1) * qkv_cols] = block[:, :qkv_cols]
        dense_out[:, g * features : (g + 1) * features] = block[:, qkv_cols:]


def late_end_kernel(count, groups, ff, padded, qkv_cols, cols, *refs):
    parts, outs = refs[:count], refs[count:]
    up_out, down_out, gains_out, columns_out, columns_again, qkv_bias_out, up_bias_out = outs
    rows, width = up_out.shape[0], LANES * columns_out.shape[0]
    both_cols = 2 * padded
    ctx_at = lax.axis_index("ctx")
    blocks = [part[:rows, :].astype(jnp.float32) for part in parts]
    for r, block in enumerate(swapped(blocks, ctx_at)):
        up_out[:, r * ff : (r + 1) * ff] = block[:, :ff]
        down_out[:, r * ff : (r + 1) * ff] = block[:, padded : padded + ff]
    vectors = [part[rows:, :].astype(jnp.float32) for part in parts]

    def unfolded(block, start, extent):
        n = extent // both_cols
        return jnp.concatenate([block[start + i : start + i + 1] for i in range(n)], axis=1)

    summed = tree_sum(vectors)
    step = width // both_cols
    gains = jnp.concatenate([unfolded(summed, i * step, width) for i in range(4)], axis=1)
    put_row(gains_out, gains)
    columns = unfolded(summed, 4 * step, width)
    put_row(columns_out, columns)
    put_row(columns_again, columns)
    sums = [tree_sum(vectors[g::groups]) for g in range(groups)]
    sums = [unfolded(block, 5 * step, cols)[:, :qkv_cols] for block in sums]
    put_row(
        qkv_bias_out, jnp.concatenate(swapped(sums, lax.rem(ctx_at, groups)), axis=1)
    )
    last = 5 * step + cols // both_cols
    ups = [block[last : last + 1, :ff] for block in vectors]
    put_row(up_bias_out, jnp.concatenate(swapped(ups, ctx_at), axis=1))


def on_device(
    tokens,
    group_order,
    attn_gain,
    attn_shift,
    qkv_weight,
    qkv_bias,
    dense_weight,
    dense_bias,
    mlp_gain,
    mlp_shift,
    up_weight,
    up_bias,
    down_weight,
    down_bias,
    out_grad,
):
    bf16, f32 = jnp.bfloat16, jnp.float32
    seqs, length, width = tokens.shape
    fsdp_count, ctx_count, tp_count = (lax.axis_size(a) for a in ("fsdp", "ctx", "tp"))
    ctx_at, tp_at = lax.axis_index("ctx"), lax.axis_index("tp")
    rows_here = qkv_weight.shape[0]
    block_rows = ctx_count * rows_here
    heads = qkv_bias.shape[0] // (3 * HD)
    hidden_all = up_bias.shape[0]
    head_groups = math.gcd(heads, ctx_count)
    own_heads = heads // head_groups
    copies = ctx_count // head_groups // seqs
    features = own_heads * HD
    qkv_cols = 3 * features
    cols = qkv_cols + features
    low_cols = qkv_cols // LANES * LANES
    high_cols = -(-qkv_cols // LANES) * LANES
    ff = hidden_all // ctx_count
    padded = -(-ff // LANES) * LANES
    near = seqs // tp_count
    size = ctx_count * length

    early = local_kernel(
        functools.partial(early_message_kernel, head_groups, qkv_cols, features),
        [shaped((rows_here, cols), bf16)] * head_groups,
    )(qkv_weight, dense_weight.T)
    late = local_kernel(
        functools.partial(late_message_kernel, ctx_count, ff, padded),
        [shaped((rows_here, 2 * padded), bf16)] * ctx_count,
    )(up_weight, down_weight.T)
    early_rows = exchange([early[k % head_groups] for k in range(ctx_count)], "ctx")

    def near_part(array):
        parts = [array[j * near : (j + 1) * near] for j in range(tp_count)]
        return swapped(parts, tp_at)[0]

    own_tokens = near_part(tokens)
    own_grads = near_part(out_grad)
    message = jnp.stack([own_tokens, own_grads.astype(bf16)])
    late_rows = exchange(late, "ctx")
    chunks = gather_chunks(message[:, :, None], "ctx", 2)
    chunks = chunks.reshape(2, near, size, width)

    loose = rows_here % SUBLANES == 0

    def own_rows(parts):
        return jnp.concatenate(parts if loose else swapped(parts, ctx_at), axis=0)

    early_parts = spread(own_rows(early_rows), "fsdp")
    late_parts = spread(own_rows(late_rows), "fsdp")
    by_core = spread(chunks, "tp")

    position = jnp.concatenate(
        [
            positions(group_order, (ctx_at ^ k) * length, length)
            for k in gather_order(ctx_count)
        ]
    ).astype(f32)
    cos_table, sin_table = rotary_tables(position[:, None])
    column_sums = jnp.sum(out_grad, axis=(0, 1))

    def grad_blocks(columns, extra=0):
        return [
            shaped((block_rows + extra, columns), bf16 if k else f32) for k in range(fsdp_count)
        ]

    vector_rows = (5 * width + cols) // (2 * padded) + 1
    vector_rows = -(-vector_rows // SUBLANES) * SUBLANES

    row_blocks = ctx_count if loose else 1
    mixed, proj_low, attn_weight, qkv_bias_part, *early_grads = local_kernel(
        functools.partial(
            attention_kernel,
            fsdp_count,
            tp_count,
            near,
            head_groups,
            own_heads,
            copies,
            seqs,
            row_blocks,
        ),
        [
            shaped((size, cols - low_cols), bf16),
            shaped((size, high_cols), bf16),
            shaped((width, cols), bf16),
            shaped((1, cols), f32),
        ]
        + grad_blocks(cols),
        [pltpu.VMEM((size, high_cols), f32), pltpu.VMEM((width, cols), f32)],
        flops=16 * size * width * cols,
        moved=16 * size * width,
    )(
        *by_core,
        *early_parts,
        tiled(attn_gain),
        tiled(attn_shift),
        tiled(qkv_bias),
        cos_table,
        sin_table,
        position.reshape(-1, 1),
        position.reshape(1, -1),
    )
    outs = local_kernel(
        functools.partial(
            mlp_kernel, fsdp_count, tp_count, near, head_groups, seqs, ff, row_blocks
        ),
        [shaped((2, near, size, width), f32)] * tp_count + grad_blocks(2 * padded, vector_rows),
        [pltpu.VMEM((width, 2 * padded), bf16), pltpu.VMEM((width, 2 * padded), f32)],
        flops=12 * seqs * size * width * padded,
        moved=32 * size * width,
    )(
        *by_core,
        *late_parts,
        tiled(mlp_gain),
        tiled(mlp_shift),
        tiled(up_bias),
        tiled(column_sums),
        tiled(attn_gain),
        mixed,
        proj_low,
        attn_weight,
        qkv_bias_part,
    )
    row_parts, late_grads = outs[:tp_count], outs[tp_count:]
    row_sums = sum(exchange(row_parts, "tp"))
    row_sums = row_sums.reshape(2, near, ctx_count, length, width)
    row_sums = scatter_chunks(row_sums, "ctx", 2).reshape(2, near, length, width)
    branches, inner = row_sums[0], row_sums[1]

    def both_cores(half):
        halves = spread(half, "tp")
        return jnp.concatenate(swapped(halves, tp_at), axis=0)

    def scatter_weights(parts):
        columns = parts[0].shape[1]
        rows = parts[0].shape[0] - block_rows + rows_here
        pieces = local_kernel(
            functools.partial(sum_blocks_kernel, fsdp_count, ctx_count, rows_here),
            [shaped((rows, columns), bf16 if k else f32) for k in range(ctx_count)],
        )(*exchange(parts, "fsdp"))
        return exchange(pieces, "ctx")

    early_pieces = scatter_weights(early_grads)
    late_pieces = scatter_weights(late_grads)
    block_half = own_tokens.astype(f32) + branches + (dense_bias + down_bias)
    block_out = both_cores(block_half.astype(bf16))
    later_tokens, _ = lax.optimization_barrier((own_tokens, chunks))
    own_centred, own_inverse = normed_rows(later_tokens.astype(f32))
    inner = (
        inner
        - jnp.mean(inner, axis=-1, keepdims=True)
        - own_centred * jnp.mean(inner * own_centred, axis=-1, keepdims=True)
    )
    tokens_grad = both_cores(own_grads + own_inverse * inner)
    qkv_weight_grad, dense_weight_grad = local_kernel(
        functools.partial(early_end_kernel, ctx_count, head_groups, qkv_cols, features),
        [shaped(qkv_weight.shape, f32), shaped(dense_weight.shape[::-1], f32)],
    )(*early_pieces)
    up_weight_grad, down_weight_grad, gains, column_grad, column_again, qkv_bias_grad, up_bias_grad = (
        local_kernel(
            functools.partial(
                late_end_kernel, ctx_count, head_groups, ff, padded, qkv_cols, cols
            ),
            [
                shaped(up_weight.shape, f32),
                shaped(down_weight.shape[::-1], f32),
                shaped((4 * width // LANES, LANES), f32),
                shaped((width // LANES, LANES), f32),
                shaped((width // LANES, LANES), f32),
                shaped((3 * HD * heads // LANES, LANES), f32),
                shaped((hidden_all // LANES, LANES), f32),
            ],
        )(*late_pieces)
    )
    gains = sum(spread(gains, "tp")).reshape(4, width)
    return (
        block_out,
        tokens_grad,
        gains[0],
        gains[1],
        qkv_weight_grad,
        qkv_bias_grad.reshape(3 * HD * heads),
        dense_weight_grad.T,
        column_grad.reshape(width),
        gains[2],
        gains[3],
        up_weight_grad,
        up_bias_grad.reshape(hidden_all),
        down_weight_grad.T,
        column_again.reshape(width),
    )


def solution(mesh):
    in_specs = (
        P("fsdp", "ctx", None),
        P(),
        P(),
        P(),
        P(("fsdp", "ctx"), "tp"),
        P("tp"),
        P("tp", ("fsdp", "ctx")),
        P(),
        P(),
        P(),
        P(("fsdp", "ctx"), "tp"),
        P("tp"),
        P("tp", ("fsdp", "ctx")),
        P(),
        P("fsdp", "ctx", None),
    )
    out_specs = (
        P("fsdp", "ctx", None),
        P("fsdp", "ctx", None),
        P(),
        P(),
        P(("fsdp", "ctx"), "tp"),
        P("tp"),
        P("tp", ("fsdp", "ctx")),
        P(),
        P(),
        P(),
        P(("fsdp", "ctx"), "tp"),
        P("tp"),
        P("tp", ("fsdp", "ctx")),
        P(),
    )

    return jax.shard_map(
        on_device, mesh=mesh, in_specs=in_specs, out_specs=out_specs, check_vma=False
    )
```
